32 devices in a mesh: dp: 4 (over z), tensor: 8 (over y, x, core).
Axes of the slice: x: 2, y: 2, z: 4, core: 2. Of those that a mesh axis runs over, the one named last changes fastest.
Arguments:
- hidden_in: bfloat16 [4, 1024, 2304], P('dp', 'tensor'), may hold values from -6 to 6
- prompt_len: int32 [4], P('dp'), may hold values from 1 to 1024, 2560 in all
- start_pos: int32 [4], P('dp'), may hold values from 0 to 511
- routes: int32 [4, 1024, 2], P('dp'), may hold values from 0 to 7, as said below
- trainer_qkv: float32 [2304, 3, 2048], P(('tensor', 'dp')), may hold values from -1 to 1
- trainer_out: float32 [2048, 2304], P(('tensor', 'dp')), may hold values from -0.125 to 0.125
- trainer_gate: float32 [2304, 5760], P('tensor'), may hold values from -0.125 to 0.125
- trainer_up: float32 [2304, 5760], P('tensor'), may hold values from -0.125 to 0.125
- trainer_down: float32 [2304, 5760], P('tensor'), may hold values from -0.078125 to 0.078125
- attn_gain: float32 [2304], replicated, may hold values from 0.25 to 1.75
- moe_gain: float32 [2304], replicated, may hold values from 0.25 to 1.75
- router: bfloat16 [2304, 8], replicated, may hold values from -0.125 to 0.125
Outputs:
- server_qkv: bfloat16 [2304, 3, 2048], P(None, None, 'tensor')
- server_out: bfloat16 [2048, 2304], P('tensor')
- server_gate: bfloat16 [2304, 5760], P(None, 'tensor')
- server_up: bfloat16 [2304, 5760], P(None, 'tensor')
- server_down: bfloat16 [2304, 5760], P(None, 'tensor')
- hidden_out: bfloat16 [4, 1024, 2304], P('dp', 'tensor')
- kv_cache: bfloat16 [4, 2, 1024, 2048], P('dp', None, None, 'tensor')
The draws below stay inside these ranges and needn't reach their ends.
Inputs may be any that keep to these rules, and one draw needn't show every extreme that they name: `routes`: each row names two different experts; expert 0 is named by at most 512 rows of each prompt and by exactly 512 rows of some prompt.
All inputs are finite; a program needn't handle non-finite values. No bound on the sum of `prompt_len` on one device may be relied on, other than what follows from the above.
Results may differ from the reference program's by a relative error of at most 0.011.
The reference program's roundings to bfloat16 on the way count: a program that leaves them out, or rounds other values in their place, can miss the bound.
Values may be sent and summed in bfloat16 or wider, within the bound.
No kernel may reach another device: no remote copies, remote signals or barrier semaphores. Data moves between devices by JAX's collectives and lax.ppermute only.
A program may use at most 256 MiB of HBM per device.

```python
import math
import jax
import jax.numpy as jnp
import numpy as np
from jax import lax

D = 2304
HEADS = 32
HEAD_DIM = 64
FF = 5760
EXPERTS = 8
SEQ = 1024
PROMPTS = 4
CAP = 512
N_TENSOR = 8


def draw_routes(key, part):
    keys_all = jax.random.split(key, 6)
    counts = jax.random.randint(keys_all[0], (PROMPTS,), CAP // 4, CAP + 1)
    full_prompt = jax.random.randint(keys_all[1], (), 0, PROMPTS)
    counts = jnp.where(jnp.arange(PROMPTS) == full_prompt, CAP, counts)
    order = jax.vmap(lambda prompt_key: jax.random.permutation(prompt_key, SEQ))(jax.random.split(keys_all[2], PROMPTS))
    chosen = order < counts[:, None]
    first_pick = jax.random.randint(keys_all[3], (PROMPTS, SEQ), 1, EXPERTS)
    step_pick = jax.random.randint(keys_all[4], (PROMPTS, SEQ), 1, EXPERTS - 1)
    second_pick = 1 + (first_pick - 1 + step_pick) % (EXPERTS - 1)
    lead_col = jnp.where(chosen, 0, first_pick)
    trail_col = jnp.where(chosen, first_pick, second_pick)
    swapped = jax.random.randint(keys_all[5], (PROMPTS, SEQ), 0, 2) == 1
    return jnp.stack([jnp.where(swapped, trail_col, lead_col), jnp.where(swapped, lead_col, trail_col)], axis=-1).astype(jnp.int32)


def draw_trainer_qkv(key, part):
    noise_key = jax.random.fold_in(key, 0)
    base = jax.random.truncated_normal(noise_key, -6.0, 6.0, (D, 3, HEADS * HEAD_DIM), jnp.float32) * D ** (-0.5)
    return jnp.clip(base, -1.0, 1.0)


def touch_ends(drawn, stream_key, least, largest):
    place = [jax.random.randint(jax.random.fold_in(stream_key, axis), (), 0, length) for axis, length in enumerate(drawn.shape)]
    widest = drawn.shape.index(max(drawn.shape))
    neighbour = place[:widest] + [(place[widest] + 1) % drawn.shape[widest]] + place[widest + 1:]
    return drawn.at[tuple(place)].set(least).at[tuple(neighbour)].set(largest)


def block_levels(stream_key, extent, cuts, low, high):
    loudness = 1.0
    for dim, shards_of in cuts:
        steps = jax.random.uniform(jax.random.fold_in(jax.random.fold_in(stream_key, 6), dim), (shards_of,), jnp.float32, low / len(cuts), high / len(cuts))
        loudness = loudness * jnp.repeat(jnp.exp(steps), extent[dim] // shards_of).reshape((-1,) + (1,) * (len(extent) - 1 - dim))
    return loudness


def length_profile(count, total, limit, lean):
    loads = [(1 << 20) // math.isqrt(standing ** lean) + 1 for standing in range(2, count + 1)]
    spare, given = total - limit - (count - 1), [1] * (count - 1)
    while spare > 0:
        movable = [i for i in range(count - 1) if given[i] < limit]
        whole, left = sum([loads[i] for i in movable]), spare
        for i in movable:
            more = min(limit - given[i], max(1, left * loads[i] // whole), spare)
            given[i] = given[i] + more
            spare = spare - more
    return np.array([limit] + given)


def ragged_sizes(key, count, total, bound, skew):
    if count == 2:
        one = jax.random.randint(key, (), max(1, total - bound), min(bound, total - 1) + 1)
        return jnp.stack([one, total - one])
    sizes = jnp.asarray(length_profile(count, total, bound, skew), jnp.int32)
    pairs = (count - 1) // 2
    giver, taker = sizes[1:1 + 2 * pairs:2], sizes[2:2 + 2 * pairs:2]
    margin = jnp.minimum(giver - 1, bound - taker)
    shifted = jax.random.randint(jax.random.fold_in(key, 1), (pairs,), 0, 1 << 20) % (margin + 1)
    sizes = sizes.at[1:1 + 2 * pairs:2].set(giver - shifted).at[2:2 + 2 * pairs:2].set(taker + shifted)
    return sizes[jax.random.permutation(jax.random.fold_in(key, 2), count)]


def noise(rng, extent, deviation, limit, cuts=(), kind=jnp.bfloat16):
    drawn = jax.random.normal(rng, extent, jnp.float32) * deviation
    if len(cuts) > 0:
        drawn = block_levels(rng, extent, cuts, -0.22, 0.18) * drawn
    return jnp.clip(drawn, min=-limit, max=limit).astype(kind)


def setup_inputs(seed: int = 0) -> dict:
    keys = jax.random.split(jax.random.key(seed), 13)
    hidden_in = noise(keys[0], (PROMPTS, SEQ, D), 1.0, 6.0, ((0, 4), (1, 8)))
    prompt_len = ragged_sizes(keys[1], PROMPTS, PROMPTS * SEQ * 5 // 8, SEQ, 2).astype(jnp.int32)
    start_pos = touch_ends(jax.random.randint(keys[2], (PROMPTS,), 0, 512), jax.random.fold_in(keys[2], 1), 0, 511).astype(jnp.int32)
    routes = draw_routes(jax.random.fold_in(keys[12], 71), 0)
    trainer_qkv = draw_trainer_qkv(jax.random.fold_in(keys[12], 71), 0)
    trainer_out = noise(keys[5], (HEADS * HEAD_DIM, D), (HEADS * HEAD_DIM) ** -0.5, 0.125, ((0, 32),), jnp.float32)
    trainer_gate = noise(keys[6], (D, FF), D ** -0.5, 0.125, ((0, 8),), jnp.float32)
    trainer_up = noise(keys[7], (D, FF), D ** -0.5, 0.125, ((0, 8),), jnp.float32)
    trainer_down = noise(keys[8], (D, FF), FF ** -0.5, 0.078125, ((0, 8),), jnp.float32)
    attn_gain = jnp.clip(1.0 + 0.15 * jax.random.normal(keys[9], (D,), jnp.float32), 0.25, 1.75)
    moe_gain = jnp.clip(1.0 + 0.15 * jax.random.normal(keys[10], (D,), jnp.float32), 0.25, 1.75)
    router = noise(keys[11], (D, EXPERTS), D ** -0.5, 0.125)
    return dict(hidden_in=hidden_in, prompt_len=prompt_len, start_pos=start_pos, routes=routes, trainer_qkv=trainer_qkv, trainer_out=trainer_out, trainer_gate=trainer_gate, trainer_up=trainer_up, trainer_down=trainer_down, attn_gain=attn_gain, moe_gain=moe_gain, router=router)


def rms_scale(values, gain_row):
    mean_sq = lax.optimization_barrier(jnp.mean(values * values, axis=-1, keepdims=True))
    return values * lax.rsqrt(mean_sq + 1e-05) * gain_row

def rotate(head_block, positions):
    half_dim = head_block.shape[-1] // 2
    inv_freq = jnp.power(10000.0, jnp.arange(half_dim, dtype=jnp.float32) * (-2.0 / head_block.shape[-1]))
    angles = positions.astype(jnp.float32)[:, None] * inv_freq[None, :]
    cosine = jnp.cos(angles)[:, None, :]
    sine_part = jnp.sin(angles)[:, None, :]
    first_half = head_block[..., :half_dim]
    second_half = head_block[..., half_dim:]
    return jnp.concatenate([first_half * cosine - second_half * sine_part, second_half * cosine + first_half * sine_part], axis=-1)

def reference(hidden_in, prompt_len, start_pos, routes, trainer_qkv, trainer_out, trainer_gate, trainer_up, trainer_down, attn_gain, moe_gain, router):
    server_qkv = trainer_qkv.astype(jnp.bfloat16)
    server_out = trainer_out.astype(jnp.bfloat16)
    server_gate = trainer_gate.astype(jnp.bfloat16)
    server_up = trainer_up.astype(jnp.bfloat16)
    server_down = trainer_down.astype(jnp.bfloat16)
    qkv_flat = server_qkv.reshape(D, 3 * HEADS * HEAD_DIM)
    group_width = HEADS * HEAD_DIM // N_TENSOR
    unit_width = FF // N_TENSOR
    score_scale = HEAD_DIM ** (-0.5)

    def one_head(head_items):
        query_head, key_head, value_head = head_items
        scores = jnp.dot(query_head, key_head.T, preferred_element_type=jnp.float32) * score_scale
        row_ids = jnp.arange(SEQ, dtype=jnp.int32)
        scores = jnp.where(row_ids[:, None] >= row_ids[None, :], scores, -1e+30)
        row_max = lax.optimization_barrier(jnp.max(scores, axis=-1, keepdims=True))
        exp_scores = jnp.exp(scores - row_max)
        attn_probs = (exp_scores / lax.optimization_barrier(jnp.sum(exp_scores, axis=-1, keepdims=True))).astype(jnp.bfloat16)
        return jnp.dot(attn_probs, value_head, preferred_element_type=jnp.float32).astype(jnp.bfloat16)

    def one_prompt(items):
        tokens_in, length, offset, route_rows = items
        seq_ids = jnp.arange(SEQ, dtype=jnp.int32)
        valid_rows = seq_ids < length
        tokens = tokens_in.astype(jnp.float32)
        normed = rms_scale(tokens, attn_gain).astype(jnp.bfloat16)
        mixed = jnp.dot(normed, qkv_flat, preferred_element_type=jnp.float32).reshape(SEQ, 3, HEADS, HEAD_DIM)
        places = offset + seq_ids
        query_all = rotate(mixed[:, 0], places).astype(jnp.bfloat16)
        keys_all = rotate(mixed[:, 1], places).astype(jnp.bfloat16)
        values_all = mixed[:, 2].astype(jnp.bfloat16)
        head_outs = lax.map(one_head, (jnp.moveaxis(query_all, 1, 0), jnp.moveaxis(keys_all, 1, 0), jnp.moveaxis(values_all, 1, 0)))
        attended = jnp.moveaxis(head_outs, 0, 1).reshape(SEQ, HEADS * HEAD_DIM)

        def add_group(group_id, running):
            part_sum = jnp.dot(lax.dynamic_slice_in_dim(attended, group_id * group_width, group_width, 1), lax.dynamic_slice_in_dim(server_out, group_id * group_width, group_width, 0), preferred_element_type=jnp.float32)
            rounded = lax.optimization_barrier(part_sum.astype(jnp.bfloat16))
            return running + rounded.astype(jnp.float32)
        attn = lax.fori_loop(0, N_TENSOR, add_group, jnp.zeros((SEQ, D), jnp.float32))
        middle = (tokens + attn).astype(jnp.bfloat16)
        normed_moe = rms_scale(middle.astype(jnp.float32), moe_gain).astype(jnp.bfloat16)
        logits = jnp.dot(normed_moe, router, preferred_element_type=jnp.float32)
        expert_ids = jnp.arange(EXPERTS, dtype=jnp.int32)
        logit_first = lax.optimization_barrier(jnp.sum(jnp.where(route_rows[:, 0:1] == expert_ids[None, :], logits, 0.0), axis=1))
        logit_second = lax.optimization_barrier(jnp.sum(jnp.where(route_rows[:, 1:2] == expert_ids[None, :], logits, 0.0), axis=1))
        other_logit = jnp.where(route_rows[:, 0] == 0, logit_second, logit_first)
        routed = jnp.any(route_rows == 0, axis=1)
        route_w = jnp.where(routed, jax.nn.sigmoid(logits[:, 0] - other_logit), 0.0)
        slot = (jnp.cumsum(routed.astype(jnp.int32)) - 1).astype(jnp.int32)
        slot_rows = jnp.full((CAP,), SEQ, jnp.int32).at[jnp.where(routed, slot, CAP)].set(seq_ids, mode='drop')
        picked = normed_moe[jnp.minimum(slot_rows, SEQ - 1)]
        gate_val = jnp.dot(picked, server_gate, preferred_element_type=jnp.float32)
        up_val = jnp.dot(picked, server_up, preferred_element_type=jnp.float32)
        act = (jax.nn.silu(gate_val) * up_val).astype(jnp.bfloat16)

        def add_units(group_id, running):
            act_part = lax.dynamic_slice_in_dim(act, group_id * unit_width, unit_width, 1)
            down_part = lax.dynamic_slice_in_dim(server_down, group_id * unit_width, unit_width, 1)
            part_sum = lax.dot_general(act_part, down_part, (((1,), (1,)), ((), ())), preferred_element_type=jnp.float32)
            rounded = lax.optimization_barrier(part_sum.astype(jnp.bfloat16))
            return running + rounded.astype(jnp.float32)
        slot_sums = lax.fori_loop(0, N_TENSOR, add_units, jnp.zeros((CAP, D), jnp.float32))
        expert_sum = jnp.zeros((SEQ, D), jnp.float32).at[slot_rows].add(slot_sums, mode='drop')
        result = middle.astype(jnp.float32) + route_w[:, None] * expert_sum
        hidden_rows = jnp.where(valid_rows[:, None], result, 0.0).astype(jnp.bfloat16)
        cache_pair = jnp.stack([keys_all.reshape(SEQ, HEADS * HEAD_DIM), values_all.reshape(SEQ, HEADS * HEAD_DIM)], axis=0)
        cache_pair = jnp.where(valid_rows[None, :, None], cache_pair, jnp.zeros((), jnp.bfloat16))
        return (hidden_rows, cache_pair)
    hidden_out, kv_cache = lax.map(one_prompt, (hidden_in, prompt_len, start_pos, routes))
    return (server_qkv, server_out, server_gate, server_up, server_down, hidden_out, kv_cache)
```

```python
import jax
import jax.numpy as jnp
from jax import lax
from jax.experimental import pallas as pl
from jax.experimental.pallas import tpu as pltpu
from jax.sharding import PartitionSpec as P

HEAD_DIM = 64


def swap_pairs(size, step):
    return [(i, i ^ step) for i in range(size)]


def send(block, size, step):
    return lax.ppermute(block, "tensor", swap_pairs(size, step))


def split_columns(matrix, parts):
    rows, width = matrix.shape
    part = width // parts
    chunk = rows
    for cand in (48, 32, 16):
        if rows % cand == 0:
            chunk = cand
            break

    def kernel(x_ref, o_ref):
        for t in range(parts):
            o_ref[t] = x_ref[:, t * part : (t + 1) * part].astype(jnp.bfloat16)

    return pl.pallas_call(
        kernel,
        out_shape=jax.ShapeDtypeStruct((parts, rows, part), jnp.bfloat16),
        grid=(rows // chunk,),
        in_specs=[pl.BlockSpec((chunk, width), lambda i: (i, 0))],
        out_specs=pl.BlockSpec((parts, chunk, part), lambda i: (0, i, 0)),
        name="split_columns",
    )(matrix)


def split_heads(qkv, parts):
    _, rows, width = qkv.shape
    part = width // parts

    def kernel(x_ref, o_ref):
        for t in range(parts):
            for j in range(3):
                o_ref[t, j] = x_ref[j, :, t * part : (t + 1) * part].astype(jnp.bfloat16)

    return pl.pallas_call(
        kernel,
        out_shape=jax.ShapeDtypeStruct((parts, 3, rows, part), jnp.bfloat16),
        name="split_heads",
    )(qkv)


def reorder_blocks(stacked, me):
    count, rows, width = stacked.shape

    def kernel(me_ref, x_ref, o_ref):
        o_ref[...] = x_ref[0]

    return pl.pallas_call(
        kernel,
        out_shape=jax.ShapeDtypeStruct((count * rows, width), stacked.dtype),
        grid_spec=pltpu.PrefetchScalarGridSpec(
            num_scalar_prefetch=1,
            grid=(count,),
            in_specs=[pl.BlockSpec((1, rows, width), lambda i, m: (m[0] ^ i, 0, 0))],
            out_specs=pl.BlockSpec((rows, width), lambda i, m: (i, 0)),
        ),
        name="reorder_blocks",
    )(me.reshape(1), stacked)


def rms_scale(values, gain_row):
    mean_sq = jnp.mean(values * values, axis=-1, keepdims=True)
    return values * lax.rsqrt(mean_sq + 1e-05) * gain_row


def rotate(head_block, positions):
    half_dim = head_block.shape[-1] // 2
    inv_freq = jnp.power(
        10000.0, jnp.arange(half_dim, dtype=jnp.float32) * (-2.0 / head_block.shape[-1])
    )
    angles = positions.astype(jnp.float32)[:, None] * inv_freq[None, :]
    cosine = jnp.cos(angles)[:, None, :]
    sine_part = jnp.sin(angles)[:, None, :]
    first_half = head_block[..., :half_dim]
    second_half = head_block[..., half_dim:]
    return jnp.concatenate(
        [
            first_half * cosine - second_half * sine_part,
            second_half * cosine + first_half * sine_part,
        ],
        axis=-1,
    )


def attend_block(query_blk, key_blk, value_blk, row_start):
    scores = jnp.einsum(
        "qhd,khd->hqk", query_blk, key_blk, preferred_element_type=jnp.float32
    ) * query_blk.shape[-1] ** (-0.5)
    row_ids = row_start + jnp.arange(query_blk.shape[0], dtype=jnp.int32)
    col_ids = jnp.arange(key_blk.shape[0], dtype=jnp.int32)
    scores = jnp.where(row_ids[None, :, None] >= col_ids[None, None, :], scores, -1e30)
    row_max = jnp.max(scores, axis=-1, keepdims=True)
    exp_scores = jnp.exp(scores - row_max)
    attn_probs = (exp_scores / jnp.sum(exp_scores, axis=-1, keepdims=True)).astype(jnp.bfloat16)
    return jnp.einsum(
        "hqk,khd->qhd", attn_probs, value_blk, preferred_element_type=jnp.float32
    ).astype(jnp.bfloat16)


def shards(
    hidden_in,
    prompt_len,
    start_pos,
    routes,
    trainer_qkv,
    trainer_out,
    trainer_gate,
    trainer_up,
    trainer_down,
    attn_gain,
    moe_gain,
    router,
):
    size = lax.axis_size("tensor")
    replicas = lax.axis_size("dp")
    chips = size // 2
    me = lax.axis_index("tensor").astype(jnp.int32)
    plane = lax.axis_index("dp").astype(jnp.int32)
    chip, core = me // 2, me % 2
    rows_dev, model = hidden_in.shape[1], hidden_in.shape[2]
    seq_len = rows_dev * size
    length = prompt_len[0]
    offset = start_pos[0]
    my_first = me * rows_dev

    qkv_parts = split_heads(trainer_qkv.transpose(1, 0, 2), size)
    qkv_cols = lax.all_to_all(qkv_parts, "tensor", 0, 0, tiled=True)
    out_cast = trainer_out.astype(jnp.bfloat16)

    tokens = hidden_in[0].astype(jnp.float32)
    normed = rms_scale(tokens, attn_gain).astype(jnp.bfloat16)
    same_core = jnp.stack([normed] + [send(normed, size, 2 * j) for j in range(1, chips)])
    other_core = send(same_core, size, 1)
    stacked = jnp.stack([same_core, other_core], axis=1).reshape(size, rows_dev, model)
    piece = reorder_blocks(stacked, me)

    gate_parts = split_columns(trainer_gate, size)
    up_parts = split_columns(trainer_up, size)
    down_rows = trainer_down.shape[0] // replicas
    down_quarter = lax.dynamic_slice_in_dim(trainer_down, plane * down_rows, down_rows, 0)
    down_parts = split_columns(down_quarter, size)

    server_out = lax.all_gather(out_cast, "dp", axis=0, tiled=True)
    qkv_all = lax.all_gather(qkv_cols, "dp", axis=0)
    server_gate = lax.all_to_all(gate_parts, "tensor", 0, 0, tiled=True).reshape(model, -1)
    server_up = lax.all_to_all(up_parts, "tensor", 0, 0, tiled=True).reshape(model, -1)
    down_cols = lax.all_to_all(down_parts, "tensor", 0, 0, tiled=True)
    down_all = lax.all_gather(down_cols, "dp", axis=0)
    units = server_gate.shape[1]
    down_t = down_all.transpose(3, 1, 0, 2).reshape(units, model)
    server_down = down_t.T
    local_width = trainer_qkv.shape[2] // size
    qkv_server = qkv_all.transpose(2, 1, 0, 3, 4).reshape(3, model, local_width)
    server_qkv = qkv_server.transpose(1, 0, 2)

    out_pair = jnp.concatenate([server_out, send(server_out, size, 1)], axis=0)
    gate_other = send(server_gate, size, 1)
    up_other = send(server_up, size, 1)
    down_other = send(down_t, size, 1)

    heads_here = local_width // HEAD_DIM
    mixed = jnp.einsum("sd,tdc->tsc", piece, qkv_server, preferred_element_type=jnp.float32)
    places = offset + jnp.arange(seq_len, dtype=jnp.int32)
    query_all = rotate(mixed[0].reshape(-1, heads_here, HEAD_DIM), places).astype(jnp.bfloat16)
    keys_all = rotate(mixed[1].reshape(-1, heads_here, HEAD_DIM), places).astype(jnp.bfloat16)
    values_all = mixed[2].reshape(-1, heads_here, HEAD_DIM).astype(jnp.bfloat16)
    block_len = min(512, seq_len)
    block_outs = []
    for block_id in range(seq_len // block_len):
        row_lo = block_id * block_len
        row_hi = row_lo + block_len
        block_outs.append(
            attend_block(query_all[row_lo:row_hi], keys_all[:row_hi], values_all[:row_hi], row_lo)
        )
    attended = jnp.concatenate(block_outs, axis=0).reshape(chips, 2, rows_dev, local_width)
    seq_valid = jnp.arange(seq_len, dtype=jnp.int32) < length
    cache_pair = jnp.where(
        seq_valid[None, :, None],
        jnp.stack([keys_all.reshape(seq_len, -1), values_all.reshape(seq_len, -1)]),
        jnp.zeros((), jnp.bfloat16),
    )

    att_mine = lax.dynamic_index_in_dim(attended, core, 1, keepdims=False)
    att_other = send(lax.dynamic_index_in_dim(attended, 1 - core, 1, keepdims=False), size, 1)
    att_pair = jnp.concatenate([att_mine, att_other], axis=-1)

    def attn_part(j):
        rows = lax.dynamic_index_in_dim(att_pair, chip ^ j, 0, keepdims=False)
        return jnp.dot(rows, out_pair, preferred_element_type=jnp.float32)

    got = [send(attn_part(j).astype(jnp.bfloat16), size, 2 * j) for j in range(1, chips)]
    attn_sum = attn_part(0)
    for part in got:
        attn_sum = attn_sum + part.astype(jnp.float32)
    middle = (tokens + attn_sum).astype(jnp.bfloat16)
    normed_moe = rms_scale(middle.astype(jnp.float32), moe_gain).astype(jnp.bfloat16)

    moe_rows = jnp.concatenate(
        [normed_moe] + [send(normed_moe, size, 2 * j) for j in range(1, chips)], axis=0
    )

    local_routes = lax.dynamic_slice_in_dim(routes[0], my_first, rows_dev, 0)
    local_valid = my_first + jnp.arange(rows_dev, dtype=jnp.int32) < length
    logits = jnp.dot(normed_moe, router, preferred_element_type=jnp.float32)
    expert_ids = jnp.arange(router.shape[1], dtype=jnp.int32)
    logit_first = jnp.sum(
        jnp.where(local_routes[:, 0:1] == expert_ids[None, :], logits, 0.0), axis=1
    )
    logit_second = jnp.sum(
        jnp.where(local_routes[:, 1:2] == expert_ids[None, :], logits, 0.0), axis=1
    )
    other_logit = jnp.where(local_routes[:, 0] == 0, logit_second, logit_first)
    local_routed = jnp.any(local_routes == 0, axis=1)
    route_w = jnp.where(local_routed, jax.nn.sigmoid(logits[:, 0] - other_logit), 0.0)

    def activate(gate_w, up_w):
        gate_val = jnp.dot(moe_rows, gate_w, preferred_element_type=jnp.float32)
        up_val = jnp.dot(moe_rows, up_w, preferred_element_type=jnp.float32)
        return (jax.nn.silu(gate_val) * up_val).astype(jnp.bfloat16)

    sums = jnp.dot(
        activate(server_gate, server_up), down_t, preferred_element_type=jnp.float32
    ) + jnp.dot(activate(gate_other, up_other), down_other, preferred_element_type=jnp.float32)
    sums = sums.reshape(chips, rows_dev, model)
    expert_sum = sums[0]
    for j in range(1, chips):
        expert_sum = expert_sum + send(sums[j].astype(jnp.bfloat16), size, 2 * j).astype(
            jnp.float32
        )
    expert_sum = jnp.where(local_routed[:, None], expert_sum, 0.0)
    result = middle.astype(jnp.float32) + route_w[:, None] * expert_sum
    hidden_out = jnp.where(local_valid[:, None], result, 0.0).astype(jnp.bfloat16)[None]
    return (
        server_qkv,
        server_out,
        server_gate,
        server_up,
        server_down,
        hidden_out,
        cache_pair[None],
    )


def solution(mesh):
    placed = (
        P("dp", "tensor", None),
        P("dp"),
        P("dp"),
        P("dp", None, None),
        P(("tensor", "dp"), None, None),
        P(("tensor", "dp"), None),
        P("tensor", None),
        P("tensor", None),
        P("tensor", None),
        P(),
        P(),
        P(),
    )
    return jax.shard_map(
        shards,
        mesh=mesh,
        in_specs=placed,
        out_specs=(
            P(None, None, "tensor"),
            P("tensor", None),
            P(None, "tensor"),
            P(None, "tensor"),
            P(None, "tensor"),
            P("dp", "tensor", None),
            P("dp", None, None, "tensor"),
        ),
        check_vma=False,
    )
```

```python
import jax
import jax.numpy as jnp
from jax import lax
from jax.experimental import pallas as pl
from jax.experimental.pallas import tpu as pltpu
from jax.sharding import PartitionSpec as P

HEAD_DIM = 64


def swap_pairs(size, step):
    return [(i, i ^ step) for i in range(size)]


def send(block, size, step):
    return lax.ppermute(block, "tensor", swap_pairs(size, step))


def gather_line(block, count, plane):
    rows = block.shape[0]
    below, above = [], []
    up = down = block
    for step in range(1, count):
        up = lax.ppermute(up, "dp", [(i, i + 1) for i in range(step - 1, count - 1)])
        down = lax.ppermute(down, "dp", [(i, i - 1) for i in range(1, count - step + 1)])
        below.insert(0, up)
        above.append(down)
    line = jnp.concatenate(below + [block] + above, axis=0)
    return lax.dynamic_slice_in_dim(line, (count - 1 - plane) * rows, count * rows, 0)


def split_stacked(matrix, parts):
    rows, width = matrix.shape
    part = width // parts
    chunk = rows
    for cand in (48, 32, 16):
        if rows % cand == 0:
            chunk = cand
            break

    def kernel(x_ref, o_ref):
        for t in range(parts):
            o_ref[t] = x_ref[:, t * part : (t + 1) * part].astype(jnp.bfloat16)

    return pl.pallas_call(
        kernel,
        out_shape=jax.ShapeDtypeStruct((parts, rows, part), jnp.bfloat16),
        grid=(rows // chunk,),
        in_specs=[pl.BlockSpec((chunk, width), lambda i: (i, 0))],
        out_specs=pl.BlockSpec((parts, chunk, part), lambda i: (0, i, 0)),
        name="split_stacked",
    )(matrix)


def split_heads(qkv, parts):
    _, rows, width = qkv.shape
    part = width // parts

    def kernel(x_ref, o_ref):
        for t in range(parts):
            for j in range(3):
                o_ref[t, j] = x_ref[j, :, t * part : (t + 1) * part].astype(jnp.bfloat16)

    return pl.pallas_call(
        kernel,
        out_shape=jax.ShapeDtypeStruct((parts, 3, rows, part), jnp.bfloat16),
        name="split_heads",
    )(qkv)


def join_rows(blocks, me):
    count = len(blocks)
    many, rows, width = blocks[0].shape

    def kernel(me_ref, *refs):
        ins, o_ref, sem = refs[:count], refs[count], refs[count + 1]
        copies = []
        for k in range(count):
            place = pl.multiple_of((me_ref[0] ^ k) * rows, 16)
            copies.append(
                pltpu.make_async_copy(
                    ins[k].at[pl.program_id(0)], o_ref.at[0, pl.ds(place, rows), :], sem.at[k]
                )
            )
        for copy in copies:
            copy.start()
        for copy in copies:
            copy.wait()

    return pl.pallas_call(
        kernel,
        out_shape=jax.ShapeDtypeStruct((many, count * rows, width), blocks[0].dtype),
        grid_spec=pltpu.PrefetchScalarGridSpec(
            num_scalar_prefetch=1,
            grid=(many,),
            in_specs=[pl.BlockSpec(memory_space=pl.ANY)] * count,
            out_specs=pl.BlockSpec((1, count * rows, width), lambda i, m: (i, 0, 0)),
            scratch_shapes=[pltpu.SemaphoreType.DMA((count,))],
        ),
        compiler_params=pltpu.CompilerParams(vmem_limit_bytes=32 * 1024 * 1024),
        name="join_rows",
    )(me.reshape(1), *blocks)


def split_columns(first, second, parts, me):
    rows, width = first.shape
    part = width // parts
    window = min(width, (part + 127) // 128 * 128 + 128)
    chunk = rows
    for cand in (48, 32, 16):
        if rows % cand == 0:
            chunk = cand
            break

    def kernel(me_ref, first_ref, second_ref, *o_refs):
        for k in range(parts):
            left = (me_ref[0] ^ k) * part
            base = jnp.minimum(lax.div(left, 128) * 128, width - window)
            for i, x_ref in enumerate((first_ref, second_ref)):
                cols = x_ref[:, pl.ds(pl.multiple_of(base, 128), window)]
                cols = pltpu.roll(cols, window - (left - base), 1)
                o_refs[k][i] = cols[:, :part].astype(jnp.bfloat16)

    return pl.pallas_call(
        kernel,
        out_shape=[jax.ShapeDtypeStruct((2, rows, part), jnp.bfloat16)] * parts,
        grid_spec=pltpu.PrefetchScalarGridSpec(
            num_scalar_prefetch=1,
            grid=(rows // chunk,),
            in_specs=[pl.BlockSpec((chunk, width), lambda i, m: (i, 0))] * 2,
            out_specs=[pl.BlockSpec((2, chunk, part), lambda i, m: (0, i, 0))] * parts,
        ),
        name="split_columns",
    )(me.reshape(1), first, second)


def dot_nt(a, b):
    return lax.dot_general(a, b, (((1,), (1,)), ((), ())), preferred_element_type=jnp.float32)


def attention(tokens, weights, cosine, sine, scalars, rows_dev):
    seq, model = tokens.shape
    width = weights.shape[2]
    heads = width // HEAD_DIM
    block = min(256, seq)
    steps = seq // block
    half = HEAD_DIM // 2

    def kernel(s_ref, x_ref, w_ref, cos_ref, sin_ref, kv_ref, att_ref, k_all, v_all):
        step = pl.program_id(0)
        lane = lax.broadcasted_iota(jnp.int32, (block, width), 1)
        low = lax.rem(lane, HEAD_DIM) < half
        head_of = lax.div(lane, HEAD_DIM)
        x = x_ref[...]

        def rotated(j):
            m = jnp.dot(x, w_ref[j], preferred_element_type=jnp.float32)
            turned = jnp.where(
                low, -pltpu.roll(m, width - half, 1), pltpu.roll(m, half, 1)
            )
            return m * cos_ref[...] + turned * sin_ref[...]

        row = step * block + lax.broadcasted_iota(jnp.int32, (block, width), 0)
        valid = row < s_ref[0]
        start = pl.multiple_of(step * block, block)
        key = rotated(1)
        k_all[pl.ds(start, block), :] = key.astype(jnp.bfloat16)
        kv_ref[0] = jnp.where(valid, key, 0.0).astype(jnp.bfloat16)
        value = jnp.dot(x, w_ref[2], preferred_element_type=jnp.float32)
        v_all[pl.ds(start, block), :] = value.astype(jnp.bfloat16)
        kv_ref[1] = jnp.where(valid, value, 0.0).astype(jnp.bfloat16)
        query = rotated(0).astype(jnp.bfloat16).astype(jnp.float32) * HEAD_DIM ** (-0.5)

        for here in range(steps):

            @pl.when(step == here)
            def _():
                lo = here * block
                causal = lax.broadcasted_iota(
                    jnp.int32, (block, block), 0
                ) >= lax.broadcasted_iota(jnp.int32, (block, block), 1)
                out = jnp.zeros((block, width), jnp.float32)
                for h in range(heads):
                    q = jnp.where(head_of == h, query, 0.0).astype(jnp.bfloat16)
                    diag = jnp.where(causal, dot_nt(q, k_all[lo : lo + block, :]), -1e30)
                    top = jnp.max(diag, axis=-1, keepdims=True)
                    if lo:
                        past = dot_nt(q, k_all[:lo, :])
                        top = jnp.maximum(top, jnp.max(past, axis=-1, keepdims=True))
                        past = jnp.exp(past - top)
                    diag = jnp.exp(diag - top)
                    total = jnp.sum(diag, axis=-1, keepdims=True)
                    if lo:
                        total = total + jnp.sum(past, axis=-1, keepdims=True)
                    inv = 1.0 / total
                    res = jnp.dot(
                        (diag * inv).astype(jnp.bfloat16),
                        v_all[lo : lo + block, :],
                        preferred_element_type=jnp.float32,
                    )
                    if lo:
                        res = res + jnp.dot(
                            (past * inv).astype(jnp.bfloat16),
                            v_all[:lo, :],
                            preferred_element_type=jnp.float32,
                        )
                    out = jnp.where(head_of == h, res, out)
                out = out.astype(jnp.bfloat16)
                for piece in range(block // rows_dev):
                    dev = here * (block // rows_dev) + piece
                    slot = jnp.where(s_ref[1] == dev % 2, 0, 1)
                    att_ref[slot, (dev // 2) * rows_dev : (dev // 2 + 1) * rows_dev, :] = out[
                        piece * rows_dev : (piece + 1) * rows_dev
                    ]

    return pl.pallas_call(
        kernel,
        out_shape=(
            jax.ShapeDtypeStruct((2, seq, width), jnp.bfloat16),
            jax.ShapeDtypeStruct((2, seq // 2, width), jnp.bfloat16),
        ),
        grid_spec=pltpu.PrefetchScalarGridSpec(
            num_scalar_prefetch=1,
            grid=(steps,),
            in_specs=[
                pl.BlockSpec((block, model), lambda i, s: (i, 0)),
                pl.BlockSpec((3, model, width), lambda i, s: (0, 0, 0)),
                pl.BlockSpec((block, width), lambda i, s: (i, 0)),
                pl.BlockSpec((block, width), lambda i, s: (i, 0)),
            ],
            out_specs=(
                pl.BlockSpec((2, block, width), lambda i, s: (0, i, 0)),
                pl.BlockSpec((2, seq // 2, width), lambda i, s: (0, 0, 0)),
            ),
            scratch_shapes=[
                pltpu.VMEM((seq, width), jnp.bfloat16),
                pltpu.VMEM((seq, width), jnp.bfloat16),
            ],
        ),
        compiler_params=pltpu.CompilerParams(vmem_limit_bytes=48 * 1024 * 1024),
        name="attention",
    )(scalars, tokens, weights, cosine, sine)


def expert(blocks, own, other):
    count = len(blocks)
    rows, model = blocks[0].shape
    units = own[0].shape[0]

    def kernel(*refs):
        x_in, w_in = refs[:count], refs[count : count + 6]
        outs = refs[count + 6 : 2 * count + 6]
        x_all, w_all, total, x_sem, w_sem = refs[2 * count + 6 :]
        x_copies = [
            pltpu.make_async_copy(x_in[j], x_all.at[pl.ds(j * rows, rows), :], x_sem.at[j])
            for j in range(count)
        ]
        w_copies = [
            pltpu.make_async_copy(w_in[j], w_all.at[j], w_sem.at[j]) for j in range(6)
        ]
        for copy in x_copies + w_copies:
            copy.start()
        for copy in x_copies:
            copy.wait()
        x = x_all[...]
        for half in range(2):
            w_copies[3 * half].wait()
            gate = dot_nt(x, w_all[3 * half])
            w_copies[3 * half + 1].wait()
            up = dot_nt(x, w_all[3 * half + 1])
            act = (gate / (1.0 + jnp.exp(-gate)) * up).astype(jnp.bfloat16)
            w_copies[3 * half + 2].wait()
            part = jnp.dot(act, w_all[3 * half + 2], preferred_element_type=jnp.float32)
            if half == 0:
                total[...] = part
            else:
                part = (total[...] + part).astype(jnp.bfloat16)
                for j in range(count):
                    outs[j][...] = part[j * rows : (j + 1) * rows]

    return pl.pallas_call(
        kernel,
        out_shape=[jax.ShapeDtypeStruct((rows, model), jnp.bfloat16)] * count,
        in_specs=[pl.BlockSpec(memory_space=pl.ANY)] * (count + 6),
        out_specs=[pl.BlockSpec(memory_space=pltpu.VMEM)] * count,
        scratch_shapes=[
            pltpu.VMEM((count * rows, model), jnp.bfloat16),
            pltpu.VMEM((6, units, model), jnp.bfloat16),
            pltpu.VMEM((count * rows, model), jnp.float32),
            pltpu.SemaphoreType.DMA((count,)),
            pltpu.SemaphoreType.DMA((6,)),
        ],
        compiler_params=pltpu.CompilerParams(vmem_limit_bytes=56 * 1024 * 1024),
        name="expert",
    )(*blocks, *own, *other)


def rms_scale(values, gain_row):
    mean_sq = jnp.mean(values * values, axis=-1, keepdims=True)
    return values * lax.rsqrt(mean_sq + 1e-05) * gain_row


def shards(
    hidden_in,
    prompt_len,
    start_pos,
    routes,
    trainer_qkv,
    trainer_out,
    trainer_gate,
    trainer_up,
    trainer_down,
    attn_gain,
    moe_gain,
    router,
):
    size = lax.axis_size("tensor")
    replicas = lax.axis_size("dp")
    chips = size // 2
    me = lax.axis_index("tensor").astype(jnp.int32)
    plane = lax.axis_index("dp").astype(jnp.int32)
    chip, core = me // 2, me % 2
    rows_dev, model = hidden_in.shape[1], hidden_in.shape[2]
    seq_len = rows_dev * size
    length = prompt_len[0]
    offset = start_pos[0]
    my_first = me * rows_dev

    local_width = trainer_qkv.shape[2] // size
    qkv_parts = split_heads(trainer_qkv.transpose(1, 0, 2), size)
    qkv_cols = lax.all_to_all(qkv_parts, "tensor", 0, 0, tiled=True)
    qkv_all = lax.all_gather(qkv_cols, "dp", axis=0)
    qkv_server = qkv_all.transpose(2, 1, 0, 3, 4).reshape(3, model, local_width)
    server_qkv = qkv_server.transpose(1, 0, 2)
    server_out = gather_line(trainer_out.astype(jnp.bfloat16), replicas, plane)

    tokens = hidden_in[0].astype(jnp.float32)
    normed = rms_scale(tokens, attn_gain).astype(jnp.bfloat16)
    blocks = []
    for j in range(chips):
        block = send(normed, size, 2 * j) if j else normed
        blocks += [block[None], send(block, size, 1)[None]]
    piece = join_rows(blocks, me)[0]

    down_rows = trainer_down.shape[0] // replicas
    down_quarter = lax.dynamic_slice_in_dim(trainer_down, plane * down_rows, down_rows, 0)
    down_cols = lax.all_to_all(split_stacked(down_quarter, size), "tensor", 0, 0, tiled=True)
    down_all = lax.all_gather(down_cols, "dp", axis=0)

    parts = split_columns(trainer_gate, trainer_up, size, me)
    early = [send(parts[k], size, k) for k in [1] + list(range(2, size, 2))]
    late = list(lax.optimization_barrier((*parts[3::2], *early)))[: chips - 1]
    late = [send(block, size, 2 * j + 3) for j, block in enumerate(late)]
    joined = [parts[0], early[0]]
    for j in range(1, chips):
        joined += [early[j], late[j - 1]]


    out_pair = jnp.concatenate([server_out, send(server_out, size, 1)], axis=0)

    half_dim = HEAD_DIM // 2
    inv_freq = jnp.power(
        10000.0, jnp.arange(half_dim, dtype=jnp.float32) * (-2.0 / HEAD_DIM)
    )
    places = offset + jnp.arange(seq_len, dtype=jnp.int32)
    angles = places.astype(jnp.float32)[:, None] * inv_freq[None, :]
    repeats = local_width // half_dim
    cosine = jnp.tile(jnp.cos(angles), (1, repeats))
    sine_part = jnp.tile(jnp.sin(angles), (1, repeats))
    scalars = jnp.stack([length, core])
    cache_pair, attended = attention(
        piece, qkv_server, cosine, sine_part, scalars, rows_dev
    )

    att_pair = jnp.concatenate([attended[0], send(attended[1], size, 1)], axis=-1)
    att_pair = att_pair.reshape(chips, rows_dev, 2 * local_width)

    def attn_part(j):
        rows = lax.dynamic_index_in_dim(att_pair, chip ^ j, 0, keepdims=False)
        return jnp.dot(rows, out_pair, preferred_element_type=jnp.float32)

    partial = [attn_part(j) for j in range(chips)]
    sent = [part.astype(jnp.bfloat16) for part in partial[1:]]
    got = [send(block, size, 2 * j + 2) for j, block in enumerate(sent)]
    joined = list(lax.optimization_barrier((*joined, *sent)))[:size]
    gate_up = join_rows(joined, me)
    gate_t, up_t = gate_up[0].T, gate_up[1].T
    gate_other = send(gate_t, size, 1)
    up_other = send(up_t, size, 1)
    attn_sum = partial[0]
    for block in got:
        attn_sum = attn_sum + block.astype(jnp.float32)
    middle = (tokens + attn_sum).astype(jnp.bfloat16)
    normed_moe = rms_scale(middle.astype(jnp.float32), moe_gain).astype(jnp.bfloat16)

    moe_rows = [normed_moe] + [send(normed_moe, size, 2 * j) for j in range(1, chips)]
    down_late, _ = lax.optimization_barrier((down_all, moe_rows[1]))
    down_t = down_late.transpose(3, 1, 0, 2).reshape(-1, model)
    down_other = send(down_t, size, 1)

    local_routes = lax.dynamic_slice_in_dim(routes[0], my_first, rows_dev, 0)
    local_valid = my_first + jnp.arange(rows_dev, dtype=jnp.int32) < length
    logits = jnp.dot(normed_moe, router, preferred_element_type=jnp.float32)
    expert_ids = jnp.arange(router.shape[1], dtype=jnp.int32)
    logit_first = jnp.sum(
        jnp.where(local_routes[:, 0:1] == expert_ids[None, :], logits, 0.0), axis=1
    )
    logit_second = jnp.sum(
        jnp.where(local_routes[:, 1:2] == expert_ids[None, :], logits, 0.0), axis=1
    )
    other_logit = jnp.where(local_routes[:, 0] == 0, logit_second, logit_first)
    local_routed = jnp.any(local_routes == 0, axis=1)
    route_w = jnp.where(local_routed, jax.nn.sigmoid(logits[:, 0] - other_logit), 0.0)

    sums = expert(
        moe_rows, (gate_t, up_t, down_t), (gate_other, up_other, down_other)
    )
    expert_sum = sums[0].astype(jnp.float32)
    for j in range(1, chips):
        expert_sum = expert_sum + send(sums[j], size, 2 * j).astype(jnp.float32)
    expert_sum = jnp.where(local_routed[:, None], expert_sum, 0.0)
    result = middle.astype(jnp.float32) + route_w[:, None] * expert_sum
    hidden_out = jnp.where(local_valid[:, None], result, 0.0).astype(jnp.bfloat16)[None]
    return (
        server_qkv,
        server_out,
        gate_t.T,
        up_t.T,
        down_t.T,
        hidden_out,
        cache_pair[None],
    )


def solution(mesh):
    placed = (
        P("dp", "tensor", None),
        P("dp"),
        P("dp"),
        P("dp", None, None),
        P(("tensor", "dp"), None, None),
        P(("tensor", "dp"), None),
        P("tensor", None),
        P("tensor", None),
        P("tensor", None),
        P(),
        P(),
        P(),
    )
    return jax.shard_map(
        shards,
        mesh=mesh,
        in_specs=placed,
        out_specs=(
            P(None, None, "tensor"),
            P("tensor", None),
            P(None, "tensor"),
            P(None, "tensor"),
            P(None, "tensor"),
            P("dp", "tensor", None),
            P("dp", None, None, "tensor"),
        ),
        check_vma=False,
    )
```

```python
import jax
import jax.numpy as jnp
from jax import lax
from jax.experimental import pallas as pl
from jax.experimental.pallas import tpu as pltpu
from jax.sharding import PartitionSpec as P

HEAD_DIM = 64


def swap_pairs(size, step):
    return [(i, i ^ step) for i in range(size)]


def send(block, size, step):
    return lax.ppermute(block, "tensor", swap_pairs(size, step))


def split_heads(qkv, parts):
    _, rows, width = qkv.shape
    part = width // parts

    def kernel(x_ref, o_ref):
        for t in range(parts):
            for j in range(3):
                o_ref[t, j] = x_ref[j, :, t * part : (t + 1) * part].astype(jnp.bfloat16)

    return pl.pallas_call(
        kernel,
        out_shape=jax.ShapeDtypeStruct((parts, 3, rows, part), jnp.bfloat16),
        name="split_heads",
    )(qkv)


def split_rows(matrix, parts, plane, rows):
    width = matrix.shape[1]
    part = width // parts

    def kernel(p_ref, x_ref, o_ref):
        for t in range(parts):
            o_ref[t] = x_ref[:, t * part : (t + 1) * part].astype(jnp.bfloat16)

    return pl.pallas_call(
        kernel,
        out_shape=jax.ShapeDtypeStruct((parts, rows, part), jnp.bfloat16),
        grid_spec=pltpu.PrefetchScalarGridSpec(
            num_scalar_prefetch=1,
            grid=(1,),
            in_specs=[pl.BlockSpec((rows, width), lambda i, p: (p[0], 0))],
            out_specs=pl.BlockSpec((parts, rows, part), lambda i, p: (0, 0, 0)),
        ),
        compiler_params=pltpu.CompilerParams(vmem_limit_bytes=32 * 1024 * 1024),
        name="split_rows",
    )(plane.reshape(1), matrix)


def split_columns(gate, up, down_tail, parts, me):
    rows, width = gate.shape
    tail = down_tail.shape[0]
    part = width // parts
    window = min(width, (part + 127) // 128 * 128 + 128)
    chunk = 48 if rows % 48 == 0 else 16

    def kernel(me_ref, gate_ref, up_ref, tail_ref, *o_refs):
        step = pl.program_id(0)
        groups = chunk // 16

        def columns(x_ref, k):
            left = (me_ref[0] ^ k) * part
            base = jnp.minimum(lax.div(left, 128) * 128, width - window)
            cols = x_ref[:, pl.ds(pl.multiple_of(base, 128), window)]
            cols = pltpu.roll(cols, window - (left - base), 1)[:, :part]
            return cols.astype(jnp.bfloat16).reshape(-1, 16, part)

        for k in range(parts):
            o_refs[k][pl.ds(step * groups, groups)] = columns(gate_ref, k)
            o_refs[k][pl.ds(step * groups + rows // 16, groups)] = columns(up_ref, k)

        @pl.when(step == 0)
        def _():
            for k in range(parts):
                o_refs[k][rows // 8 : (2 * rows + tail) // 16] = columns(tail_ref, k)

    return pl.pallas_call(
        kernel,
        out_shape=[jax.ShapeDtypeStruct(((2 * rows + tail) // 16, 16, part), jnp.bfloat16)]
        * parts,
        grid_spec=pltpu.PrefetchScalarGridSpec(
            num_scalar_prefetch=1,
            grid=(rows // chunk,),
            in_specs=[pl.BlockSpec((chunk, width), lambda i, m: (i, 0))] * 2
            + [pl.BlockSpec((tail, width), lambda i, m: (0, 0))],
            out_specs=[
                pl.BlockSpec(((2 * rows + tail) // 16, 16, part), lambda i, m: (0, 0, 0))
            ]
            * parts,
        ),
        compiler_params=pltpu.CompilerParams(vmem_limit_bytes=40 * 1024 * 1024),
        name="split_columns",
    )(me.reshape(1), gate, up, down_tail)


def copy_rows(moves, outs_shape, sources, me, name):
    count = len(sources)
    outs = len(outs_shape)

    def kernel(me_ref, *refs):
        ins, o_refs, sem = refs[:count], refs[count : count + outs], refs[count + outs]
        copies = [
            pltpu.make_async_copy(source, o_refs[out].at[pl.ds(first, groups)], sem.at[i])
            for i, (source, out, first, groups) in enumerate(moves(me_ref[0], ins))
        ]
        for copy in copies:
            copy.start()
        for copy in copies:
            copy.wait()

    return pl.pallas_call(
        kernel,
        out_shape=[jax.ShapeDtypeStruct(shape, jnp.bfloat16) for shape in outs_shape],
        grid_spec=pltpu.PrefetchScalarGridSpec(
            num_scalar_prefetch=1,
            grid=(1,),
            in_specs=[pl.BlockSpec(memory_space=pl.ANY)] * count,
            out_specs=[pl.BlockSpec(shape, lambda i, m: (0, 0, 0)) for shape in outs_shape],
            scratch_shapes=[pltpu.SemaphoreType.DMA((160,))],
        ),
        compiler_params=pltpu.CompilerParams(vmem_limit_bytes=40 * 1024 * 1024),
        name=name,
    )(me.reshape(1), *sources)


def join_blocks(blocks, me):
    rows, width = blocks[0].shape
    groups = rows // 16

    def moves(index, ins):
        return [(ref, 0, (index ^ k) * groups, groups) for k, ref in enumerate(ins)]

    blocks = [block.reshape(groups, 16, width) for block in blocks]
    shape = (len(blocks) * groups, 16, width)
    return copy_rows(moves, [shape], blocks, me, "join_blocks")[0].reshape(-1, width)


def join_gate_up(blocks, me, rows):
    width = blocks[0].shape[2]
    groups = rows // 16

    def moves(index, ins):
        return [
            (ref.at[pl.ds(i * groups, groups)], i, (index ^ k) * groups, groups)
            for i in range(2)
            for k, ref in enumerate(ins)
        ]

    shape = (len(blocks) * groups, 16, width)
    joined = copy_rows(moves, [shape, shape], blocks, me, "join_gate_up")
    return [matrix.reshape(-1, width) for matrix in joined]


def join_down(gathered, blocks, me, rows):
    planes, count, part_rows, width = gathered.shape
    groups, part_groups = rows // 16, part_rows // 16
    rest = groups - planes * part_groups
    gathered = gathered.reshape(planes, count, part_groups, 16, width)

    def moves(index, ins):
        found = [
            (ins[0].at[p, t], 0, t * groups + p * part_groups, part_groups)
            for p in range(planes)
            for t in range(count)
        ]
        return found + [
            (
                ref.at[pl.ds(2 * groups, rest)],
                0,
                (index ^ k) * groups + planes * part_groups,
                rest,
            )
            for k, ref in enumerate(ins[1:])
        ]

    shape = (count * groups, 16, width)
    return copy_rows(moves, [shape], [gathered, *blocks], me, "join_down")[0].reshape(-1, width)


def expert(blocks, gate_w, up_w, down_w):
    count = len(blocks)
    rows, model = blocks[0].shape
    units = gate_w.shape[1]

    def kernel(*refs):
        x_in, w_in = refs[:count], refs[count : count + 3]
        outs = refs[count + 3 : 2 * count + 3]
        x_all, w_all, x_sem, w_sem = refs[2 * count + 3 :]
        x_copies = [
            pltpu.make_async_copy(x_in[j], x_all.at[pl.ds(j * rows, rows), :], x_sem.at[j])
            for j in range(count)
        ]
        w_copies = [pltpu.make_async_copy(w_in[j], w_all.at[j], w_sem.at[j]) for j in range(3)]
        for copy in x_copies + w_copies:
            copy.start()
        for copy in x_copies:
            copy.wait()
        x = x_all[...]
        w_copies[0].wait()
        gate = jnp.dot(x, w_all[0], preferred_element_type=jnp.float32)
        w_copies[1].wait()
        up = jnp.dot(x, w_all[1], preferred_element_type=jnp.float32)
        act = (gate / (1.0 + jnp.exp(-gate)) * up).astype(jnp.bfloat16)
        w_copies[2].wait()
        for j in range(count):
            outs[j][...] = dot_nt(act[j * rows : (j + 1) * rows], w_all[2]).astype(jnp.bfloat16)

    return pl.pallas_call(
        kernel,
        out_shape=[jax.ShapeDtypeStruct((rows, model), jnp.bfloat16)] * count,
        in_specs=[pl.BlockSpec(memory_space=pl.ANY)] * (count + 3),
        out_specs=[pl.BlockSpec(memory_space=pltpu.VMEM)] * count,
        scratch_shapes=[
            pltpu.VMEM((count * rows, model), jnp.bfloat16),
            pltpu.VMEM((3, model, units), jnp.bfloat16),
            pltpu.SemaphoreType.DMA((count,)),
            pltpu.SemaphoreType.DMA((3,)),
        ],
        compiler_params=pltpu.CompilerParams(vmem_limit_bytes=56 * 1024 * 1024),
        cost_estimate=pl.CostEstimate(
            flops=6 * count * rows * model * units,
            bytes_accessed=6 * model * units,
            transcendentals=count * rows * units,
        ),
        name="expert",
    )(*blocks, gate_w, up_w, down_w)


def dot_nt(a, b):
    return lax.dot_general(a, b, (((1,), (1,)), ((), ())), preferred_element_type=jnp.float32)


def attention(tokens, weights, cosine, sine, scalars, rows_dev):
    seq, model = tokens.shape
    width = weights.shape[2]
    heads = width // HEAD_DIM
    block = min(256, seq)
    steps = seq // block
    half = HEAD_DIM // 2

    def kernel(s_ref, x_ref, w_ref, cos_ref, sin_ref, kv_ref, att_ref, k_all, v_all):
        step = pl.program_id(0)
        lane = lax.broadcasted_iota(jnp.int32, (block, width), 1)
        low = lax.rem(lane, HEAD_DIM) < half
        head_of = lax.div(lane, HEAD_DIM)
        x = x_ref[...]

        def rotated(j):
            m = jnp.dot(x, w_ref[j], preferred_element_type=jnp.float32)
            turned = jnp.where(
                low, -pltpu.roll(m, width - half, 1), pltpu.roll(m, half, 1)
            )
            return m * cos_ref[...] + turned * sin_ref[...]

        row = step * block + lax.broadcasted_iota(jnp.int32, (block, width), 0)
        valid = row < s_ref[0]
        start = pl.multiple_of(step * block, block)
        key = rotated(1)
        k_all[pl.ds(start, block), :] = key.astype(jnp.bfloat16)
        kv_ref[0] = jnp.where(valid, key, 0.0).astype(jnp.bfloat16)
        value = jnp.dot(x, w_ref[2], preferred_element_type=jnp.float32)
        v_all[pl.ds(start, block), :] = value.astype(jnp.bfloat16)
        kv_ref[1] = jnp.where(valid, value, 0.0).astype(jnp.bfloat16)
        query = rotated(0).astype(jnp.bfloat16).astype(jnp.float32) * HEAD_DIM ** (-0.5)

        for here in range(steps):

            @pl.when(step == here)
            def _():
                lo = here * block
                causal = lax.broadcasted_iota(
                    jnp.int32, (block, block), 0
                ) >= lax.broadcasted_iota(jnp.int32, (block, block), 1)
                out = jnp.zeros((block, width), jnp.float32)
                for h in range(heads):
                    q = jnp.where(head_of == h, query, 0.0).astype(jnp.bfloat16)
                    diag = jnp.where(causal, dot_nt(q, k_all[lo : lo + block, :]), -1e30)
                    top = jnp.max(diag, axis=-1, keepdims=True)
                    if lo:
                        past = dot_nt(q, k_all[:lo, :])
                        top = jnp.maximum(top, jnp.max(past, axis=-1, keepdims=True))
                        past = jnp.exp(past - top)
                    diag = jnp.exp(diag - top)
                    total = jnp.sum(diag, axis=-1, keepdims=True)
                    if lo:
                        total = total + jnp.sum(past, axis=-1, keepdims=True)
                    inv = 1.0 / total
                    res = jnp.dot(
                        (diag * inv).astype(jnp.bfloat16),
                        v_all[lo : lo + block, :],
                        preferred_element_type=jnp.float32,
                    )
                    if lo:
                        res = res + jnp.dot(
                            (past * inv).astype(jnp.bfloat16),
                            v_all[:lo, :],
                            preferred_element_type=jnp.float32,
                        )
                    out = jnp.where(head_of == h, res, out)
                out = out.astype(jnp.bfloat16)
                for piece in range(block // rows_dev):
                    dev = here * (block // rows_dev) + piece
                    slot = jnp.where(s_ref[1] == dev % 2, 0, 1)
                    att_ref[slot, (dev // 2) * rows_dev : (dev // 2 + 1) * rows_dev, :] = out[
                        piece * rows_dev : (piece + 1) * rows_dev
                    ]

    return pl.pallas_call(
        kernel,
        out_shape=(
            jax.ShapeDtypeStruct((2, seq, width), jnp.bfloat16),
            jax.ShapeDtypeStruct((2, seq // 2, width), jnp.bfloat16),
        ),
        grid_spec=pltpu.PrefetchScalarGridSpec(
            num_scalar_prefetch=1,
            grid=(steps,),
            in_specs=[
                pl.BlockSpec((block, model), lambda i, s: (i, 0)),
                pl.BlockSpec((3, model, width), lambda i, s: (0, 0, 0)),
                pl.BlockSpec((block, width), lambda i, s: (i, 0)),
                pl.BlockSpec((block, width), lambda i, s: (i, 0)),
            ],
            out_specs=(
                pl.BlockSpec((2, block, width), lambda i, s: (0, i, 0)),
                pl.BlockSpec((2, seq // 2, width), lambda i, s: (0, 0, 0)),
            ),
            scratch_shapes=[
                pltpu.VMEM((seq, width), jnp.bfloat16),
                pltpu.VMEM((seq, width), jnp.bfloat16),
            ],
        ),
        compiler_params=pltpu.CompilerParams(vmem_limit_bytes=48 * 1024 * 1024),
        cost_estimate=pl.CostEstimate(
            flops=6 * seq * model * width + 4 * seq * seq * width,
            bytes_accessed=2 * (seq * model + 3 * model * width),
            transcendentals=seq * seq * heads,
        ),
        name="attention",
    )(scalars, tokens, weights, cosine, sine)


def rms_scale(values, gain_row):
    mean_sq = jnp.mean(values * values, axis=-1, keepdims=True)
    return values * lax.rsqrt(mean_sq + 1e-05) * gain_row


def shards(
    hidden_in,
    prompt_len,
    start_pos,
    routes,
    trainer_qkv,
    trainer_out,
    trainer_gate,
    trainer_up,
    trainer_down,
    attn_gain,
    moe_gain,
    router,
):
    size = lax.axis_size("tensor")
    replicas = lax.axis_size("dp")
    chips = size // 2
    me = lax.axis_index("tensor").astype(jnp.int32)
    plane = lax.axis_index("dp").astype(jnp.int32)
    chip, core = me // 2, me % 2
    rows_dev, model = hidden_in.shape[1], hidden_in.shape[2]
    seq_len = rows_dev * size
    length = prompt_len[0]
    offset = start_pos[0]
    my_first = me * rows_dev

    mat_rows = trainer_down.shape[0]
    part_rows = mat_rows // (16 * replicas) * 16
    local_width = trainer_qkv.shape[2] // size
    qkv_parts = split_heads(trainer_qkv.transpose(1, 0, 2), size)
    qkv_cols = lax.all_to_all(qkv_parts, "tensor", 0, 0, tiled=True)
    parts = split_columns(
        trainer_gate, trainer_up, trainer_down[part_rows * replicas :], size, me
    )
    tokens = hidden_in[0].astype(jnp.float32)
    normed = rms_scale(tokens, attn_gain).astype(jnp.bfloat16)
    qkv_cols, normed, *parts = lax.optimization_barrier((qkv_cols, normed, *parts))
    qkv_all = lax.all_gather(qkv_cols, "dp", axis=0)
    qkv_server = qkv_all.transpose(2, 1, 0, 3, 4).reshape(3, model, local_width)
    server_qkv = qkv_server.transpose(1, 0, 2)
    down_parts = split_rows(trainer_down, size, plane, part_rows)
    down_cols = lax.all_to_all(down_parts, "tensor", 0, 0, tiled=True)
    down_all = lax.all_gather(down_cols, "dp", axis=0)

    same_core = [normed] + [send(normed, size, 2 * j) for j in range(1, chips)]
    out_cast, _ = lax.optimization_barrier((trainer_out.astype(jnp.bfloat16), same_core[1]))
    server_out = lax.all_gather(out_cast, "dp", axis=0, tiled=True)
    other_core = send(jnp.stack(same_core), size, 1)
    blocks = []
    for j in range(chips):
        blocks += [same_core[j], other_core[j]]
    piece = join_blocks(blocks, me)

    even, odd = list(range(2, size, 2)), list(range(1, size, 2))
    early = [send(parts[k], size, k) for k in even]
    late = list(lax.optimization_barrier((*[parts[k] for k in odd], *early)))
    early = late[len(odd) :]
    late = [send(block, size, k) for block, k in zip(late, odd)]

    out_pair = jnp.concatenate([server_out, send(server_out, size, 1)], axis=0)

    half_dim = HEAD_DIM // 2
    inv_freq = jnp.power(
        10000.0, jnp.arange(half_dim, dtype=jnp.float32) * (-2.0 / HEAD_DIM)
    )
    places = offset + jnp.arange(seq_len, dtype=jnp.int32)
    angles = places.astype(jnp.float32)[:, None] * inv_freq[None, :]
    repeats = local_width // half_dim
    cosine = jnp.tile(jnp.cos(angles), (1, repeats))
    sine_part = jnp.tile(jnp.sin(angles), (1, repeats))
    scalars = jnp.stack([length, core])
    qkv_here, _, *early = lax.optimization_barrier((qkv_server, down_cols, *early))
    cache_pair, attended = attention(
        piece, qkv_here, cosine, sine_part, scalars, rows_dev
    )

    att_pair = jnp.concatenate([attended[0], send(attended[1], size, 1)], axis=-1)
    att_pair, *late = lax.optimization_barrier((att_pair, *late))
    att_pair = att_pair.reshape(chips, rows_dev, 2 * local_width)
    joined = [parts[0]] * size
    for block, k in zip(early + late, even + odd):
        joined[k] = block

    def attn_part(j):
        rows = lax.dynamic_index_in_dim(att_pair, chip ^ j, 0, keepdims=False)
        return jnp.dot(rows, out_pair, preferred_element_type=jnp.float32)

    partial = [attn_part(j) for j in range(chips)]
    sent = [part.astype(jnp.bfloat16) for part in partial[1:]]
    got = [send(block, size, 2 * j + 2) for j, block in enumerate(sent)]
    attn_sum = partial[0]
    for block in got:
        attn_sum = attn_sum + block.astype(jnp.float32)
    middle = (tokens + attn_sum).astype(jnp.bfloat16)
    normed_moe = rms_scale(middle.astype(jnp.float32), moe_gain).astype(jnp.bfloat16)

    moe_rows = [normed_moe] + [send(normed_moe, size, 2 * j) for j in range(1, chips)]
    moe_other = send(jnp.stack(moe_rows), size, 1)
    gate, up = join_gate_up(joined, me, mat_rows)
    down = join_down(down_all, joined, me, mat_rows)

    local_routes = lax.dynamic_slice_in_dim(routes[0], my_first, rows_dev, 0)
    local_valid = my_first + jnp.arange(rows_dev, dtype=jnp.int32) < length
    logits = jnp.dot(normed_moe, router, preferred_element_type=jnp.float32)
    expert_ids = jnp.arange(router.shape[1], dtype=jnp.int32)
    logit_first = jnp.sum(
        jnp.where(local_routes[:, 0:1] == expert_ids[None, :], logits, 0.0), axis=1
    )
    logit_second = jnp.sum(
        jnp.where(local_routes[:, 1:2] == expert_ids[None, :], logits, 0.0), axis=1
    )
    other_logit = jnp.where(local_routes[:, 0] == 0, logit_second, logit_first)
    local_routed = jnp.any(local_routes == 0, axis=1)
    route_w = jnp.where(local_routed, jax.nn.sigmoid(logits[:, 0] - other_logit), 0.0)

    sums_mine = expert(moe_rows, gate, up, down)
    sums_other = expert([moe_other[j] for j in range(chips)], gate, up, down)
    from_other = send(jnp.stack(sums_other), size, 1)
    sums = [
        block.astype(jnp.float32) + from_other[j].astype(jnp.float32)
        for j, block in enumerate(sums_mine)
    ]
    expert_sum = sums[0]
    for j in range(1, chips):
        expert_sum = expert_sum + send(sums[j].astype(jnp.bfloat16), size, 2 * j).astype(
            jnp.float32
        )
    expert_sum = jnp.where(local_routed[:, None], expert_sum, 0.0)
    result = middle.astype(jnp.float32) + route_w[:, None] * expert_sum
    hidden_out = jnp.where(local_valid[:, None], result, 0.0).astype(jnp.bfloat16)[None]
    return (
        server_qkv,
        server_out,
        gate,
        up,
        down,
        hidden_out,
        cache_pair[None],
    )


def solution(mesh):
    placed = (
        P("dp", "tensor", None),
        P("dp"),
        P("dp"),
        P("dp", None, None),
        P(("tensor", "dp"), None, None),
        P(("tensor", "dp"), None),
        P("tensor", None),
        P("tensor", None),
        P("tensor", None),
        P(),
        P(),
        P(),
    )
    return jax.shard_map(
        shards,
        mesh=mesh,
        in_specs=placed,
        out_specs=(
            P(None, None, "tensor"),
            P("tensor", None),
            P(None, "tensor"),
            P(None, "tensor"),
            P(None, "tensor"),
            P("dp", "tensor", None),
            P("dp", None, None, "tensor"),
        ),
        check_vma=False,
    )
```

```python
import jax
import jax.numpy as jnp
from jax import lax
from jax.experimental import pallas as pl
from jax.experimental.pallas import tpu as pltpu
from jax.sharding import PartitionSpec as P

HEAD_DIM = 64


def swap_pairs(size, step):
    return [(i, i ^ step) for i in range(size)]


def send(block, size, step):
    return lax.ppermute(block, "tensor", swap_pairs(size, step))


def split_heads(qkv, parts):
    _, rows, width = qkv.shape
    part = width // parts

    def kernel(x_ref, o_ref):
        for t in range(parts):
            for j in range(3):
                o_ref[t, j] = x_ref[j, :, t * part : (t + 1) * part].astype(jnp.bfloat16)

    return pl.pallas_call(
        kernel,
        out_shape=jax.ShapeDtypeStruct((parts, 3, rows, part), jnp.bfloat16),
        name="split_heads",
    )(qkv)


def split_rows(matrix, parts, plane, rows):
    width = matrix.shape[1]
    part = width // parts

    def kernel(p_ref, x_ref, o_ref):
        for t in range(parts):
            o_ref[t] = x_ref[:, t * part : (t + 1) * part].astype(jnp.bfloat16)

    return pl.pallas_call(
        kernel,
        out_shape=jax.ShapeDtypeStruct((parts, rows, part), jnp.bfloat16),
        grid_spec=pltpu.PrefetchScalarGridSpec(
            num_scalar_prefetch=1,
            grid=(1,),
            in_specs=[pl.BlockSpec((rows, width), lambda i, p: (p[0], 0))],
            out_specs=pl.BlockSpec((parts, rows, part), lambda i, p: (0, 0, 0)),
        ),
        compiler_params=pltpu.CompilerParams(vmem_limit_bytes=32 * 1024 * 1024),
        name="split_rows",
    )(plane.reshape(1), matrix)


def split_columns(gate, up, down_tail, parts, me):
    rows, width = gate.shape
    tail = down_tail.shape[0]
    part = width // parts
    window = min(width, (part + 127) // 128 * 128 + 128)
    chunk = 48 if rows % 48 == 0 else 16

    def kernel(me_ref, gate_ref, up_ref, tail_ref, *o_refs):
        step = pl.program_id(0)
        groups = chunk // 16

        def columns(x_ref, k):
            left = (me_ref[0] ^ k) * part
            base = jnp.minimum(lax.div(left, 128) * 128, width - window)
            cols = x_ref[:, pl.ds(pl.multiple_of(base, 128), window)]
            cols = pltpu.roll(cols, window - (left - base), 1)[:, :part]
            return cols.astype(jnp.bfloat16).reshape(-1, 16, part)

        for k in range(parts):
            o_refs[k][pl.ds(step * groups, groups)] = columns(gate_ref, k)
            o_refs[k][pl.ds(step * groups + rows // 16, groups)] = columns(up_ref, k)

        @pl.when(step == 0)
        def _():
            for k in range(parts):
                o_refs[k][rows // 8 : (2 * rows + tail) // 16] = columns(tail_ref, k)

    return pl.pallas_call(
        kernel,
        out_shape=[jax.ShapeDtypeStruct(((2 * rows + tail) // 16, 16, part), jnp.bfloat16)]
        * parts,
        grid_spec=pltpu.PrefetchScalarGridSpec(
            num_scalar_prefetch=1,
            grid=(rows // chunk,),
            in_specs=[pl.BlockSpec((chunk, width), lambda i, m: (i, 0))] * 2
            + [pl.BlockSpec((tail, width), lambda i, m: (0, 0))],
            out_specs=[
                pl.BlockSpec(((2 * rows + tail) // 16, 16, part), lambda i, m: (0, 0, 0))
            ]
            * parts,
        ),
        compiler_params=pltpu.CompilerParams(vmem_limit_bytes=40 * 1024 * 1024),
        name="split_columns",
    )(me.reshape(1), gate, up, down_tail)


def copy_rows(moves, outs_shape, sources, me, name):
    count = len(sources)
    outs = len(outs_shape)

    def kernel(me_ref, *refs):
        ins, o_refs, sem = refs[:count], refs[count : count + outs], refs[count + outs]
        copies = [
            pltpu.make_async_copy(source, o_refs[out].at[pl.ds(first, groups)], sem.at[i])
            for i, (source, out, first, groups) in enumerate(moves(me_ref[0], ins))
        ]
        for copy in copies:
            copy.start()
        for copy in copies:
            copy.wait()

    return pl.pallas_call(
        kernel,
        out_shape=[jax.ShapeDtypeStruct(shape, jnp.bfloat16) for shape in outs_shape],
        grid_spec=pltpu.PrefetchScalarGridSpec(
            num_scalar_prefetch=1,
            grid=(1,),
            in_specs=[pl.BlockSpec(memory_space=pl.ANY)] * count,
            out_specs=[pl.BlockSpec(shape, lambda i, m: (0, 0, 0)) for shape in outs_shape],
            scratch_shapes=[pltpu.SemaphoreType.DMA((160,))],
        ),
        compiler_params=pltpu.CompilerParams(vmem_limit_bytes=40 * 1024 * 1024),
        name=name,
    )(me.reshape(1), *sources)


def join_blocks(blocks, me):
    rows, width = blocks[0].shape
    groups = rows // 16

    def moves(index, ins):
        return [(ref, 0, (index ^ k) * groups, groups) for k, ref in enumerate(ins)]

    blocks = [block.reshape(groups, 16, width) for block in blocks]
    shape = (len(blocks) * groups, 16, width)
    return copy_rows(moves, [shape], blocks, me, "join_blocks")[0].reshape(-1, width)


def join_gate_up(blocks, me, rows):
    width = blocks[0].shape[2]
    groups = rows // 16

    def moves(index, ins):
        return [
            (ref.at[pl.ds(i * groups, groups)], i, (index ^ k) * groups, groups)
            for i in range(2)
            for k, ref in enumerate(ins)
        ]

    shape = (len(blocks) * groups, 16, width)
    joined = copy_rows(moves, [shape, shape], blocks, me, "join_gate_up")
    return [matrix.reshape(-1, width) for matrix in joined]


def join_down(gathered, blocks, me, rows):
    planes, count, part_rows, width = gathered.shape
    groups, part_groups = rows // 16, part_rows // 16
    rest = groups - planes * part_groups
    gathered = gathered.reshape(planes, count, part_groups, 16, width)

    def moves(index, ins):
        found = [
            (ins[0].at[p, t], 0, t * groups + p * part_groups, part_groups)
            for p in range(planes)
            for t in range(count)
        ]
        return found + [
            (
                ref.at[pl.ds(2 * groups, rest)],
                0,
                (index ^ k) * groups + planes * part_groups,
                rest,
            )
            for k, ref in enumerate(ins[1:])
        ]

    shape = (count * groups, 16, width)
    return copy_rows(moves, [shape], [gathered, *blocks], me, "join_down")[0].reshape(-1, width)


def expert(mine, other, gate_w, up_w, down_w):
    rows, model = mine.shape
    units = gate_w.shape[1]
    block = min(512, rows)

    def kernel(mine_in, other_in, gate_in, up_in, down_in, mine_out, other_out, x_all, w_all, sem):
        x_copies = [
            pltpu.make_async_copy(mine_in, x_all.at[0], sem.at[0]),
            pltpu.make_async_copy(other_in, x_all.at[1], sem.at[1]),
        ]
        w_copies = [
            pltpu.make_async_copy(w_in, w_all.at[j], sem.at[2 + j])
            for j, w_in in enumerate((gate_in, up_in, down_in))
        ]
        for copy in [x_copies[1], w_copies[0], w_copies[1], w_copies[2], x_copies[0]]:
            copy.start()
        for step, side in enumerate((1, 0)):
            out = (mine_out, other_out)[side]
            x_copies[side].wait()
            for first in range(0, rows, block):
                x = x_all[side, first : first + block]
                if step == 0 and first == 0:
                    w_copies[0].wait()
                gate = jnp.dot(x, w_all[0], preferred_element_type=jnp.float32)
                if step == 0 and first == 0:
                    w_copies[1].wait()
                up = jnp.dot(x, w_all[1], preferred_element_type=jnp.float32)
                act = (gate / (1.0 + jnp.exp(-gate)) * up).astype(jnp.bfloat16)
                if step == 0 and first == 0:
                    w_copies[2].wait()
                out[first : first + block] = dot_nt(act, w_all[2]).astype(jnp.bfloat16)

    return pl.pallas_call(
        kernel,
        out_shape=[jax.ShapeDtypeStruct((rows, model), jnp.bfloat16)] * 2,
        in_specs=[pl.BlockSpec(memory_space=pl.ANY)] * 5,
        out_specs=[pl.BlockSpec(memory_space=pltpu.VMEM)] * 2,
        scratch_shapes=[
            pltpu.VMEM((2, rows, model), jnp.bfloat16),
            pltpu.VMEM((3, model, units), jnp.bfloat16),
            pltpu.SemaphoreType.DMA((5,)),
        ],
        compiler_params=pltpu.CompilerParams(vmem_limit_bytes=56 * 1024 * 1024),
        cost_estimate=pl.CostEstimate(
            flops=12 * rows * model * units,
            bytes_accessed=6 * model * units,
            transcendentals=2 * rows * units,
        ),
        name="expert",
    )(mine, other, gate_w, up_w, down_w)


def dot_nt(a, b):
    return lax.dot_general(a, b, (((1,), (1,)), ((), ())), preferred_element_type=jnp.float32)


def attention(tokens, weights, cosine, sine, scalars, rows_dev):
    seq, model = tokens.shape
    width = weights.shape[2]
    heads = width // HEAD_DIM
    block = min(256, seq)
    steps = seq // block
    half = HEAD_DIM // 2

    def kernel(s_ref, x_ref, w_ref, cos_ref, sin_ref, kv_ref, att_ref, k_all, v_all):
        step = pl.program_id(0)
        lane = lax.broadcasted_iota(jnp.int32, (block, width), 1)
        low = lax.rem(lane, HEAD_DIM) < half
        head_of = lax.div(lane, HEAD_DIM)
        x = x_ref[...]

        def rotated(j):
            m = jnp.dot(x, w_ref[j], preferred_element_type=jnp.float32)
            turned = jnp.where(
                low, -pltpu.roll(m, width - half, 1), pltpu.roll(m, half, 1)
            )
            return m * cos_ref[...] + turned * sin_ref[...]

        row = step * block + lax.broadcasted_iota(jnp.int32, (block, width), 0)
        valid = row < s_ref[0]
        start = pl.multiple_of(step * block, block)
        key = rotated(1)
        k_all[pl.ds(start, block), :] = key.astype(jnp.bfloat16)
        kv_ref[0] = jnp.where(valid, key, 0.0).astype(jnp.bfloat16)
        value = jnp.dot(x, w_ref[2], preferred_element_type=jnp.float32)
        v_all[pl.ds(start, block), :] = value.astype(jnp.bfloat16)
        kv_ref[1] = jnp.where(valid, value, 0.0).astype(jnp.bfloat16)
        query = rotated(0).astype(jnp.bfloat16).astype(jnp.float32) * HEAD_DIM ** (-0.5)

        for here in range(steps):

            @pl.when(step == here)
            def _():
                lo = here * block
                causal = lax.broadcasted_iota(
                    jnp.int32, (block, block), 0
                ) >= lax.broadcasted_iota(jnp.int32, (block, block), 1)
                out = jnp.zeros((block, width), jnp.float32)
                for h in range(heads):
                    q = jnp.where(head_of == h, query, 0.0).astype(jnp.bfloat16)
                    diag = jnp.where(causal, dot_nt(q, k_all[lo : lo + block, :]), -1e30)
                    top = jnp.max(diag, axis=-1, keepdims=True)
                    if lo:
                        past = dot_nt(q, k_all[:lo, :])
                        top = jnp.maximum(top, jnp.max(past, axis=-1, keepdims=True))
                        past = jnp.exp(past - top)
                    diag = jnp.exp(diag - top)
                    total = jnp.sum(diag, axis=-1, keepdims=True)
                    if lo:
                        total = total + jnp.sum(past, axis=-1, keepdims=True)
                    inv = 1.0 / total
                    res = jnp.dot(
                        (diag * inv).astype(jnp.bfloat16),
                        v_all[lo : lo + block, :],
                        preferred_element_type=jnp.float32,
                    )
                    if lo:
                        res = res + jnp.dot(
                            (past * inv).astype(jnp.bfloat16),
                            v_all[:lo, :],
                            preferred_element_type=jnp.float32,
                        )
                    out = jnp.where(head_of == h, res, out)
                out = out.astype(jnp.bfloat16)
                for piece in range(block // rows_dev):
                    dev = here * (block // rows_dev) + piece
                    slot = jnp.where(s_ref[1] == dev % 2, 0, 1)
                    att_ref[slot, (dev // 2) * rows_dev : (dev // 2 + 1) * rows_dev, :] = out[
                        piece * rows_dev : (piece + 1) * rows_dev
                    ]

    return pl.pallas_call(
        kernel,
        out_shape=(
            jax.ShapeDtypeStruct((2, seq, width), jnp.bfloat16),
            jax.ShapeDtypeStruct((2, seq // 2, width), jnp.bfloat16),
        ),
        grid_spec=pltpu.PrefetchScalarGridSpec(
            num_scalar_prefetch=1,
            grid=(steps,),
            in_specs=[
                pl.BlockSpec((block, model), lambda i, s: (i, 0)),
                pl.BlockSpec((3, model, width), lambda i, s: (0, 0, 0)),
                pl.BlockSpec((block, width), lambda i, s: (i, 0)),
                pl.BlockSpec((block, width), lambda i, s: (i, 0)),
            ],
            out_specs=(
                pl.BlockSpec((2, block, width), lambda i, s: (0, i, 0)),
                pl.BlockSpec((2, seq // 2, width), lambda i, s: (0, 0, 0)),
            ),
            scratch_shapes=[
                pltpu.VMEM((seq, width), jnp.bfloat16),
                pltpu.VMEM((seq, width), jnp.bfloat16),
            ],
        ),
        compiler_params=pltpu.CompilerParams(vmem_limit_bytes=48 * 1024 * 1024),
        cost_estimate=pl.CostEstimate(
            flops=6 * seq * model * width + 4 * seq * seq * width,
            bytes_accessed=2 * (seq * model + 3 * model * width),
            transcendentals=seq * seq * heads,
        ),
        name="attention",
    )(scalars, tokens, weights, cosine, sine)


def rms_scale(values, gain_row):
    mean_sq = jnp.mean(values * values, axis=-1, keepdims=True)
    return values * lax.rsqrt(mean_sq + 1e-05) * gain_row


def shards(
    hidden_in,
    prompt_len,
    start_pos,
    routes,
    trainer_qkv,
    trainer_out,
    trainer_gate,
    trainer_up,
    trainer_down,
    attn_gain,
    moe_gain,
    router,
):
    size = lax.axis_size("tensor")
    replicas = lax.axis_size("dp")
    chips = size // 2
    me = lax.axis_index("tensor").astype(jnp.int32)
    plane = lax.axis_index("dp").astype(jnp.int32)
    chip, core = me // 2, me % 2
    rows_dev, model = hidden_in.shape[1], hidden_in.shape[2]
    seq_len = rows_dev * size
    length = prompt_len[0]
    offset = start_pos[0]
    my_first = me * rows_dev

    mat_rows = trainer_down.shape[0]
    part_rows = mat_rows // (16 * replicas) * 16
    local_width = trainer_qkv.shape[2] // size
    qkv_parts = split_heads(trainer_qkv.transpose(1, 0, 2), size)
    qkv_cols = lax.all_to_all(qkv_parts, "tensor", 0, 0, tiled=True)
    parts = split_columns(
        trainer_gate, trainer_up, trainer_down[part_rows * replicas :], size, me
    )
    tokens = hidden_in[0].astype(jnp.float32)
    normed = rms_scale(tokens, attn_gain).astype(jnp.bfloat16)
    qkv_cols, normed, *parts = lax.optimization_barrier((qkv_cols, normed, *parts))
    qkv_all = lax.all_gather(qkv_cols, "dp", axis=0)
    down_parts = split_rows(trainer_down, size, plane, part_rows)
    down_cols = lax.all_to_all(down_parts, "tensor", 0, 0, tiled=True)
    same_core = [normed] + [send(normed, size, 2 * j) for j in range(1, chips)]
    other_core = send(jnp.stack(same_core), size, 1)
    blocks = []
    for j in range(chips):
        blocks += [same_core[j], other_core[j]]
    piece = join_blocks(blocks, me)

    even, odd = list(range(2, size, 2)), list(range(1, size, 2))
    early = [send(parts[k], size, k) for k in even]
    late = list(lax.optimization_barrier((*[parts[k] for k in odd], *early)))
    early = late[len(odd) :]
    late = [send(block, size, k) for block, k in zip(late, odd)]

    half_dim = HEAD_DIM // 2
    inv_freq = jnp.power(
        10000.0, jnp.arange(half_dim, dtype=jnp.float32) * (-2.0 / HEAD_DIM)
    )
    places = offset + jnp.arange(seq_len, dtype=jnp.int32)
    angles = places.astype(jnp.float32)[:, None] * jnp.tile(inv_freq, local_width // half_dim)
    cosine, sine_part = jnp.cos(angles), jnp.sin(angles)
    out_cast = trainer_out.astype(jnp.bfloat16)
    qkv_all, out_cast, piece, cosine, sine_part, down_cols, *early = lax.optimization_barrier(
        (qkv_all, out_cast, piece, cosine, sine_part, down_cols, *early)
    )
    server_out = lax.all_gather(out_cast, "dp", axis=0, tiled=True)
    qkv_server = qkv_all.transpose(2, 1, 0, 3, 4).reshape(3, model, local_width)
    server_qkv = qkv_server.transpose(1, 0, 2)
    scalars = jnp.stack([length, core])
    cache_pair, attended = attention(
        piece, qkv_server, cosine, sine_part, scalars, rows_dev
    )
    attended, down_cols, server_out = lax.optimization_barrier(
        (attended, down_cols, server_out)
    )
    down_all = lax.all_gather(down_cols, "dp", axis=0)
    attended, *late = lax.optimization_barrier((attended, *late))
    out_pair = jnp.concatenate([server_out, send(server_out, size, 1)], axis=0)

    att_pair = jnp.concatenate([attended[0], send(attended[1], size, 1)], axis=-1)
    att_pair = att_pair.reshape(chips, rows_dev, 2 * local_width)
    joined = [parts[0]] * size
    for block, k in zip(early + late, even + odd):
        joined[k] = block

    def attn_part(j):
        rows = lax.dynamic_index_in_dim(att_pair, chip ^ j, 0, keepdims=False)
        return jnp.dot(rows, out_pair, preferred_element_type=jnp.float32)

    partial = [attn_part(j) for j in range(chips)]
    sent = [part.astype(jnp.bfloat16) for part in partial[1:]]
    got = [send(block, size, 2 * j + 2) for j, block in enumerate(sent)]
    attn_sum = partial[0]
    for block in got:
        attn_sum = attn_sum + block.astype(jnp.float32)
    middle = (tokens + attn_sum).astype(jnp.bfloat16)
    normed_moe = rms_scale(middle.astype(jnp.float32), moe_gain).astype(jnp.bfloat16)

    moe_rows = [normed_moe] + [send(normed_moe, size, 2 * j) for j in range(1, chips)]
    gate, up = join_gate_up(joined, me, mat_rows)
    down = join_down(down_all, joined, me, mat_rows)
    *moe_rows, gate, up, down = lax.optimization_barrier((*moe_rows, gate, up, down))
    moe_mine = jnp.stack(moe_rows)
    moe_other = send(moe_mine, size, 1)

    local_routes = lax.dynamic_slice_in_dim(routes[0], my_first, rows_dev, 0)
    local_valid = my_first + jnp.arange(rows_dev, dtype=jnp.int32) < length
    logits = jnp.dot(normed_moe, router, preferred_element_type=jnp.float32)
    expert_ids = jnp.arange(router.shape[1], dtype=jnp.int32)
    logit_first = jnp.sum(
        jnp.where(local_routes[:, 0:1] == expert_ids[None, :], logits, 0.0), axis=1
    )
    logit_second = jnp.sum(
        jnp.where(local_routes[:, 1:2] == expert_ids[None, :], logits, 0.0), axis=1
    )
    other_logit = jnp.where(local_routes[:, 0] == 0, logit_second, logit_first)
    local_routed = jnp.any(local_routes == 0, axis=1)
    route_w = jnp.where(local_routed, jax.nn.sigmoid(logits[:, 0] - other_logit), 0.0)

    sums_mine, sums_other = expert(
        moe_mine.reshape(-1, model), moe_other.reshape(-1, model), gate, up, down
    )
    from_other = send(sums_other, size, 1)
    sums = [
        sums_mine[j * rows_dev : (j + 1) * rows_dev].astype(jnp.float32)
        + from_other[j * rows_dev : (j + 1) * rows_dev].astype(jnp.float32)
        for j in range(chips)
    ]
    expert_sum = sums[0]
    for j in range(1, chips):
        expert_sum = expert_sum + send(sums[j].astype(jnp.bfloat16), size, 2 * j).astype(
            jnp.float32
        )
    expert_sum = jnp.where(local_routed[:, None], expert_sum, 0.0)
    result = middle.astype(jnp.float32) + route_w[:, None] * expert_sum
    hidden_out = jnp.where(local_valid[:, None], result, 0.0).astype(jnp.bfloat16)[None]
    return (
        server_qkv,
        server_out,
        gate,
        up,
        down,
        hidden_out,
        cache_pair[None],
    )


def solution(mesh):
    placed = (
        P("dp", "tensor", None),
        P("dp"),
        P("dp"),
        P("dp", None, None),
        P(("tensor", "dp"), None, None),
        P(("tensor", "dp"), None),
        P("tensor", None),
        P("tensor", None),
        P("tensor", None),
        P(),
        P(),
        P(),
    )
    return jax.shard_map(
        shards,
        mesh=mesh,
        in_specs=placed,
        out_specs=(
            P(None, None, "tensor"),
            P("tensor", None),
            P(None, "tensor"),
            P(None, "tensor"),
            P(None, "tensor"),
            P("dp", "tensor", None),
            P("dp", None, None, "tensor"),
        ),
        check_vma=False,
    )
```

```python
import jax
import jax.numpy as jnp
from jax import lax
from jax.experimental import pallas as pl
from jax.experimental.pallas import tpu as pltpu
from jax.sharding import PartitionSpec as P

HEAD_DIM = 64


def swap_pairs(size, step):
    return [(i, i ^ step) for i in range(size)]


def send(block, size, step):
    return lax.ppermute(block, "tensor", swap_pairs(size, step))


def split_heads(qkv, parts):
    _, rows, width = qkv.shape
    part = width // parts

    def kernel(x_ref, o_ref):
        for t in range(parts):
            for j in range(3):
                o_ref[t, j] = x_ref[j, :, t * part : (t + 1) * part].astype(jnp.bfloat16)

    return pl.pallas_call(
        kernel,
        out_shape=jax.ShapeDtypeStruct((parts, 3, rows, part), jnp.bfloat16),
        name="split_heads",
    )(qkv)


def split_rows(matrix, parts, plane, rows):
    width = matrix.shape[1]
    part = width // parts

    def kernel(p_ref, x_ref, o_ref):
        for t in range(parts):
            o_ref[t] = x_ref[:, t * part : (t + 1) * part].astype(jnp.bfloat16)

    return pl.pallas_call(
        kernel,
        out_shape=jax.ShapeDtypeStruct((parts, rows, part), jnp.bfloat16),
        grid_spec=pltpu.PrefetchScalarGridSpec(
            num_scalar_prefetch=1,
            grid=(1,),
            in_specs=[pl.BlockSpec((rows, width), lambda i, p: (p[0], 0))],
            out_specs=pl.BlockSpec((parts, rows, part), lambda i, p: (0, 0, 0)),
        ),
        compiler_params=pltpu.CompilerParams(vmem_limit_bytes=32 * 1024 * 1024),
        name="split_rows",
    )(plane.reshape(1), matrix)


def split_columns(gate, up, down_tail, parts, me):
    rows, width = gate.shape
    tail = down_tail.shape[0]
    part = width // parts
    window = min(width, (part + 127) // 128 * 128 + 128)
    chunk = 48 if rows % 48 == 0 else 16

    def kernel(me_ref, gate_ref, up_ref, tail_ref, *o_refs):
        step = pl.program_id(0)
        groups = chunk // 16

        def columns(x_ref, k):
            left = (me_ref[0] ^ k) * part
            base = jnp.minimum(lax.div(left, 128) * 128, width - window)
            cols = x_ref[:, pl.ds(pl.multiple_of(base, 128), window)]
            cols = pltpu.roll(cols, window - (left - base), 1)[:, :part]
            return cols.astype(jnp.bfloat16).reshape(-1, 16, part)

        for k in range(parts):
            o_refs[k][pl.ds(step * groups, groups)] = columns(gate_ref, k)
            o_refs[k][pl.ds(step * groups + rows // 16, groups)] = columns(up_ref, k)

        @pl.when(step == 0)
        def _():
            for k in range(parts):
                o_refs[k][rows // 8 : (2 * rows + tail) // 16] = columns(tail_ref, k)

    return pl.pallas_call(
        kernel,
        out_shape=[jax.ShapeDtypeStruct(((2 * rows + tail) // 16, 16, part), jnp.bfloat16)]
        * parts,
        grid_spec=pltpu.PrefetchScalarGridSpec(
            num_scalar_prefetch=1,
            grid=(rows // chunk,),
            in_specs=[pl.BlockSpec((chunk, width), lambda i, m: (i, 0))] * 2
            + [pl.BlockSpec((tail, width), lambda i, m: (0, 0))],
            out_specs=[
                pl.BlockSpec(((2 * rows + tail) // 16, 16, part), lambda i, m: (0, 0, 0))
            ]
            * parts,
        ),
        compiler_params=pltpu.CompilerParams(vmem_limit_bytes=40 * 1024 * 1024),
        name="split_columns",
    )(me.reshape(1), gate, up, down_tail)


def copy_rows(moves, outs_shape, sources, me, name):
    count = len(sources)
    outs = len(outs_shape)

    def kernel(me_ref, *refs):
        ins, o_refs, sem = refs[:count], refs[count : count + outs], refs[count + outs]
        copies = [
            pltpu.make_async_copy(source, o_refs[out].at[pl.ds(first, groups)], sem.at[i])
            for i, (source, out, first, groups) in enumerate(moves(me_ref[0], ins))
        ]
        for copy in copies:
            copy.start()
        for copy in copies:
            copy.wait()

    return pl.pallas_call(
        kernel,
        out_shape=[jax.ShapeDtypeStruct(shape, jnp.bfloat16) for shape in outs_shape],
        grid_spec=pltpu.PrefetchScalarGridSpec(
            num_scalar_prefetch=1,
            grid=(1,),
            in_specs=[pl.BlockSpec(memory_space=pl.ANY)] * count,
            out_specs=[pl.BlockSpec(shape, lambda i, m: (0, 0, 0)) for shape in outs_shape],
            scratch_shapes=[pltpu.SemaphoreType.DMA((160,))],
        ),
        compiler_params=pltpu.CompilerParams(vmem_limit_bytes=40 * 1024 * 1024),
        name=name,
    )(me.reshape(1), *sources)


def join_blocks(blocks, me):
    rows, width = blocks[0].shape
    groups = rows // 16

    def moves(index, ins):
        return [(ref, 0, (index ^ k) * groups, groups) for k, ref in enumerate(ins)]

    blocks = [block.reshape(groups, 16, width) for block in blocks]
    shape = (len(blocks) * groups, 16, width)
    return copy_rows(moves, [shape], blocks, me, "join_blocks")[0].reshape(-1, width)


def join_gate_up(blocks, me, rows):
    width = blocks[0].shape[2]
    groups = rows // 16

    def moves(index, ins):
        return [
            (ref.at[pl.ds(i * groups, groups)], i, (index ^ k) * groups, groups)
            for i in range(2)
            for k, ref in enumerate(ins)
        ]

    shape = (len(blocks) * groups, 16, width)
    joined = copy_rows(moves, [shape, shape], blocks, me, "join_gate_up")
    return [matrix.reshape(-1, width) for matrix in joined]


def join_down(gathered, blocks, me, rows):
    planes, count, part_rows, width = gathered.shape
    groups, part_groups = rows // 16, part_rows // 16
    rest = groups - planes * part_groups
    gathered = gathered.reshape(planes, count, part_groups, 16, width)

    def moves(index, ins):
        found = [
            (ins[0].at[p, t], 0, t * groups + p * part_groups, part_groups)
            for p in range(planes)
            for t in range(count)
        ]
        return found + [
            (
                ref.at[pl.ds(2 * groups, rest)],
                0,
                (index ^ k) * groups + planes * part_groups,
                rest,
            )
            for k, ref in enumerate(ins[1:])
        ]

    shape = (count * groups, 16, width)
    return copy_rows(moves, [shape], [gathered, *blocks], me, "join_down")[0].reshape(-1, width)


def expert(mine, other, gate_w, up_w, down_w):
    rows, model = mine.shape
    units = gate_w.shape[1]
    block = min(512, rows)

    def kernel(mine_in, other_in, gate_in, up_in, down_in, mine_out, other_out, x_all, w_all, sem):
        x_copies = [
            pltpu.make_async_copy(mine_in, x_all.at[0], sem.at[0]),
            pltpu.make_async_copy(other_in, x_all.at[1], sem.at[1]),
        ]
        w_copies = [
            pltpu.make_async_copy(w_in, w_all.at[j], sem.at[2 + j])
            for j, w_in in enumerate((gate_in, up_in, down_in))
        ]
        for copy in [x_copies[1], w_copies[0], w_copies[1], w_copies[2], x_copies[0]]:
            copy.start()
        for step, side in enumerate((1, 0)):
            out = (mine_out, other_out)[side]
            x_copies[side].wait()
            for first in range(0, rows, block):
                x = x_all[side, first : first + block]
                if step == 0 and first == 0:
                    w_copies[0].wait()
                gate = jnp.dot(x, w_all[0], preferred_element_type=jnp.float32)
                if step == 0 and first == 0:
                    w_copies[1].wait()
                up = jnp.dot(x, w_all[1], preferred_element_type=jnp.float32)
                act = (gate / (1.0 + jnp.exp(-gate)) * up).astype(jnp.bfloat16)
                if step == 0 and first == 0:
                    w_copies[2].wait()
                out[first : first + block] = dot_nt(act, w_all[2]).astype(jnp.bfloat16)

    return pl.pallas_call(
        kernel,
        out_shape=[jax.ShapeDtypeStruct((rows, model), jnp.bfloat16)] * 2,
        in_specs=[pl.BlockSpec(memory_space=pl.ANY)] * 5,
        out_specs=[pl.BlockSpec(memory_space=pltpu.VMEM)] * 2,
        scratch_shapes=[
            pltpu.VMEM((2, rows, model), jnp.bfloat16),
            pltpu.VMEM((3, model, units), jnp.bfloat16),
            pltpu.SemaphoreType.DMA((5,)),
        ],
        compiler_params=pltpu.CompilerParams(vmem_limit_bytes=56 * 1024 * 1024),
        cost_estimate=pl.CostEstimate(
            flops=12 * rows * model * units,
            bytes_accessed=6 * model * units,
            transcendentals=2 * rows * units,
        ),
        name="expert",
    )(mine, other, gate_w, up_w, down_w)


def dot_nt(a, b):
    return lax.dot_general(a, b, (((1,), (1,)), ((), ())), preferred_element_type=jnp.float32)


def attention(tokens, weights, cosine, sine, scalars, rows_dev):
    seq, model = tokens.shape
    width = weights.shape[2]
    heads = width // HEAD_DIM
    block = min(256, seq)
    steps = seq // block
    half = HEAD_DIM // 2

    def kernel(s_ref, x_ref, w_ref, cos_ref, sin_ref, kv_ref, att_ref, k_all, v_all):
        step = pl.program_id(0)
        lane = lax.broadcasted_iota(jnp.int32, (block, width), 1)
        low = lax.rem(lane, HEAD_DIM) < half
        head_of = lax.div(lane, HEAD_DIM)
        x = x_ref[...]

        def rotated(j):
            m = jnp.dot(x, w_ref[j], preferred_element_type=jnp.float32)
            turned = jnp.where(
                low, -pltpu.roll(m, width - half, 1), pltpu.roll(m, half, 1)
            )
            return m * cos_ref[...] + turned * sin_ref[...]

        row = step * block + lax.broadcasted_iota(jnp.int32, (block, width), 0)
        valid = row < s_ref[0]
        start = pl.multiple_of(step * block, block)
        key = rotated(1)
        k_all[pl.ds(start, block), :] = key.astype(jnp.bfloat16)
        kv_ref[0] = jnp.where(valid, key, 0.0).astype(jnp.bfloat16)
        value = jnp.dot(x, w_ref[2], preferred_element_type=jnp.float32)
        v_all[pl.ds(start, block), :] = value.astype(jnp.bfloat16)
        kv_ref[1] = jnp.where(valid, value, 0.0).astype(jnp.bfloat16)
        query = rotated(0).astype(jnp.bfloat16).astype(jnp.float32) * HEAD_DIM ** (-0.5)

        for here in range(steps):

            @pl.when(step == here)
            def _():
                lo = here * block
                causal = lax.broadcasted_iota(
                    jnp.int32, (block, block), 0
                ) >= lax.broadcasted_iota(jnp.int32, (block, block), 1)
                out = jnp.zeros((block, width), jnp.float32)
                for h in range(heads):
                    q = jnp.where(head_of == h, query, 0.0).astype(jnp.bfloat16)
                    diag = jnp.where(causal, dot_nt(q, k_all[lo : lo + block, :]), -1e30)
                    top = jnp.max(diag, axis=-1, keepdims=True)
                    if lo:
                        past = dot_nt(q, k_all[:lo, :])
                        top = jnp.maximum(top, jnp.max(past, axis=-1, keepdims=True))
                        past = jnp.exp(past - top)
                    diag = jnp.exp(diag - top)
                    total = jnp.sum(diag, axis=-1, keepdims=True)
                    if lo:
                        total = total + jnp.sum(past, axis=-1, keepdims=True)
                    inv = 1.0 / total
                    res = jnp.dot(
                        (diag * inv).astype(jnp.bfloat16),
                        v_all[lo : lo + block, :],
                        preferred_element_type=jnp.float32,
                    )
                    if lo:
                        res = res + jnp.dot(
                            (past * inv).astype(jnp.bfloat16),
                            v_all[:lo, :],
                            preferred_element_type=jnp.float32,
                        )
                    out = jnp.where(head_of == h, res, out)
                out = out.astype(jnp.bfloat16)
                for piece in range(block // rows_dev):
                    dev = here * (block // rows_dev) + piece
                    slot = jnp.where(s_ref[1] == dev % 2, 0, 1)
                    att_ref[slot, (dev // 2) * rows_dev : (dev // 2 + 1) * rows_dev, :] = out[
                        piece * rows_dev : (piece + 1) * rows_dev
                    ]

    return pl.pallas_call(
        kernel,
        out_shape=(
            jax.ShapeDtypeStruct((2, seq, width), jnp.bfloat16),
            jax.ShapeDtypeStruct((2, seq // 2, width), jnp.bfloat16),
        ),
        grid_spec=pltpu.PrefetchScalarGridSpec(
            num_scalar_prefetch=1,
            grid=(steps,),
            in_specs=[
                pl.BlockSpec((block, model), lambda i, s: (i, 0)),
                pl.BlockSpec((3, model, width), lambda i, s: (0, 0, 0)),
                pl.BlockSpec((block, width), lambda i, s: (i, 0)),
                pl.BlockSpec((block, width), lambda i, s: (i, 0)),
            ],
            out_specs=(
                pl.BlockSpec((2, block, width), lambda i, s: (0, i, 0)),
                pl.BlockSpec((2, seq // 2, width), lambda i, s: (0, 0, 0)),
            ),
            scratch_shapes=[
                pltpu.VMEM((seq, width), jnp.bfloat16),
                pltpu.VMEM((seq, width), jnp.bfloat16),
            ],
        ),
        compiler_params=pltpu.CompilerParams(vmem_limit_bytes=48 * 1024 * 1024),
        cost_estimate=pl.CostEstimate(
            flops=6 * seq * model * width + 4 * seq * seq * width,
            bytes_accessed=2 * (seq * model + 3 * model * width),
            transcendentals=seq * seq * heads,
        ),
        name="attention",
    )(scalars, tokens, weights, cosine, sine)


def rms_scale(values, gain_row):
    mean_sq = jnp.mean(values * values, axis=-1, keepdims=True)
    return values * lax.rsqrt(mean_sq + 1e-05) * gain_row


def shards(
    hidden_in,
    prompt_len,
    start_pos,
    routes,
    trainer_qkv,
    trainer_out,
    trainer_gate,
    trainer_up,
    trainer_down,
    attn_gain,
    moe_gain,
    router,
):
    size = lax.axis_size("tensor")
    replicas = lax.axis_size("dp")
    chips = size // 2
    me = lax.axis_index("tensor").astype(jnp.int32)
    plane = lax.axis_index("dp").astype(jnp.int32)
    chip, core = me // 2, me % 2
    rows_dev, model = hidden_in.shape[1], hidden_in.shape[2]
    seq_len = rows_dev * size
    length = prompt_len[0]
    offset = start_pos[0]
    my_first = me * rows_dev

    mat_rows = trainer_down.shape[0]
    part_rows = mat_rows // (16 * replicas) * 16
    local_width = trainer_qkv.shape[2] // size
    qkv_parts = split_heads(trainer_qkv.transpose(1, 0, 2), size)
    qkv_cols = lax.all_to_all(qkv_parts, "tensor", 0, 0, tiled=True)
    parts = split_columns(
        trainer_gate, trainer_up, trainer_down[part_rows * replicas :], size, me
    )
    tokens = hidden_in[0].astype(jnp.float32)
    normed = rms_scale(tokens, attn_gain).astype(jnp.bfloat16)
    qkv_cols, normed, *parts = lax.optimization_barrier((qkv_cols, normed, *parts))
    qkv_all = lax.all_gather(qkv_cols, "dp", axis=0)
    down_parts = split_rows(trainer_down, size, plane, part_rows)
    down_cols = lax.all_to_all(down_parts, "tensor", 0, 0, tiled=True)
    same_core = [normed] + [send(normed, size, 2 * j) for j in range(1, chips)]
    other_core = send(jnp.stack(same_core), size, 1)
    blocks = []
    for j in range(chips):
        blocks += [same_core[j], other_core[j]]
    piece = join_blocks(blocks, me)

    first = [1, 2, 4][: size.bit_length() - 1]
    rest = [k for k in range(3, size) if k not in first]
    early = [send(parts[k], size, k) for k in first]
    late = list(lax.optimization_barrier((*[parts[k] for k in rest], *early)))
    early = late[len(rest) :]
    late = [send(block, size, k) for block, k in zip(late, rest)]

    half_dim = HEAD_DIM // 2
    inv_freq = jnp.power(
        10000.0, jnp.arange(half_dim, dtype=jnp.float32) * (-2.0 / HEAD_DIM)
    )
    places = offset + jnp.arange(seq_len, dtype=jnp.int32)
    angles = places.astype(jnp.float32)[:, None] * jnp.tile(inv_freq, local_width // half_dim)
    cosine, sine_part = jnp.cos(angles), jnp.sin(angles)
    server_out = lax.all_gather(trainer_out.astype(jnp.bfloat16), "dp", axis=0, tiled=True)
    qkv_all, down_cols = lax.optimization_barrier((qkv_all, down_cols))
    down_all = lax.all_gather(down_cols, "dp", axis=0)
    qkv_all, piece, cosine, sine_part, *early = lax.optimization_barrier(
        (qkv_all, piece, cosine, sine_part, *early)
    )
    qkv_server = qkv_all.transpose(2, 1, 0, 3, 4).reshape(3, model, local_width)
    server_qkv = qkv_server.transpose(1, 0, 2)
    scalars = jnp.stack([length, core])
    cache_pair, attended = attention(
        piece, qkv_server, cosine, sine_part, scalars, rows_dev
    )
    half = len(late) // 2
    attended, *late[:half] = lax.optimization_barrier((attended, *late[:half]))
    out_pair = jnp.concatenate([server_out, send(server_out, size, 1)], axis=0)

    att_pair = jnp.concatenate([attended[0], send(attended[1], size, 1)], axis=-1)
    att_pair, *late[half:] = lax.optimization_barrier((att_pair, *late[half:]))
    att_pair = att_pair.reshape(chips, rows_dev, 2 * local_width)
    joined = [parts[0]] * size
    for block, k in zip(early + late, first + rest):
        joined[k] = block

    def attn_part(j):
        rows = lax.dynamic_index_in_dim(att_pair, chip ^ j, 0, keepdims=False)
        return jnp.dot(rows, out_pair, preferred_element_type=jnp.float32)

    partial = [attn_part(j) for j in range(chips)]
    sent = [part.astype(jnp.bfloat16) for part in partial[1:]]
    got = [send(block, size, 2 * j + 2) for j, block in enumerate(sent)]
    attn_sum = partial[0]
    for block in got:
        attn_sum = attn_sum + block.astype(jnp.float32)
    middle = (tokens + attn_sum).astype(jnp.bfloat16)
    normed_moe = rms_scale(middle.astype(jnp.float32), moe_gain).astype(jnp.bfloat16)

    moe_rows = [normed_moe] + [send(normed_moe, size, 2 * j) for j in range(1, chips)]
    gate, up = join_gate_up(joined, me, mat_rows)
    down = join_down(down_all, joined, me, mat_rows)
    *moe_rows, gate, up, down = lax.optimization_barrier((*moe_rows, gate, up, down))
    moe_mine = jnp.stack(moe_rows)
    moe_other = send(moe_mine, size, 1)

    local_routes = lax.dynamic_slice_in_dim(routes[0], my_first, rows_dev, 0)
    local_valid = my_first + jnp.arange(rows_dev, dtype=jnp.int32) < length
    logits = jnp.dot(normed_moe, router, preferred_element_type=jnp.float32)
    expert_ids = jnp.arange(router.shape[1], dtype=jnp.int32)
    logit_first = jnp.sum(
        jnp.where(local_routes[:, 0:1] == expert_ids[None, :], logits, 0.0), axis=1
    )
    logit_second = jnp.sum(
        jnp.where(local_routes[:, 1:2] == expert_ids[None, :], logits, 0.0), axis=1
    )
    other_logit = jnp.where(local_routes[:, 0] == 0, logit_second, logit_first)
    local_routed = jnp.any(local_routes == 0, axis=1)
    route_w = jnp.where(local_routed, jax.nn.sigmoid(logits[:, 0] - other_logit), 0.0)

    sums_mine, sums_other = expert(
        moe_mine.reshape(-1, model), moe_other.reshape(-1, model), gate, up, down
    )
    from_other = send(sums_other, size, 1)
    sums = [
        sums_mine[j * rows_dev : (j + 1) * rows_dev].astype(jnp.float32)
        + from_other[j * rows_dev : (j + 1) * rows_dev].astype(jnp.float32)
        for j in range(chips)
    ]
    expert_sum = sums[0]
    for j in range(1, chips):
        expert_sum = expert_sum + send(sums[j].astype(jnp.bfloat16), size, 2 * j).astype(
            jnp.float32
        )
    expert_sum = jnp.where(local_routed[:, None], expert_sum, 0.0)
    result = middle.astype(jnp.float32) + route_w[:, None] * expert_sum
    hidden_out = jnp.where(local_valid[:, None], result, 0.0).astype(jnp.bfloat16)[None]
    return (
        server_qkv,
        server_out,
        gate,
        up,
        down,
        hidden_out,
        cache_pair[None],
    )


def solution(mesh):
    placed = (
        P("dp", "tensor", None),
        P("dp"),
        P("dp"),
        P("dp", None, None),
        P(("tensor", "dp"), None, None),
        P(("tensor", "dp"), None),
        P("tensor", None),
        P("tensor", None),
        P("tensor", None),
        P(),
        P(),
        P(),
    )
    return jax.shard_map(
        shards,
        mesh=mesh,
        in_specs=placed,
        out_specs=(
            P(None, None, "tensor"),
            P("tensor", None),
            P(None, "tensor"),
            P(None, "tensor"),
            P(None, "tensor"),
            P("dp", "tensor", None),
            P("dp", None, None, "tensor"),
        ),
        check_vma=False,
    )
```

```python
import jax
import jax.numpy as jnp
from jax import lax
from jax.experimental import pallas as pl
from jax.experimental.layout import Layout, with_layout_constraint
from jax.experimental.pallas import tpu as pltpu
from jax.sharding import PartitionSpec as P

HEAD_DIM = 64


def swap_pairs(size, step):
    return [(i, i ^ step) for i in range(size)]


def send(block, size, step):
    return lax.ppermute(block, "tensor", swap_pairs(size, step))


def add_up(total, blocks):
    for block in blocks:
        total = total + block.astype(jnp.float32)
    return total


def split_heads(qkv, parts):
    _, rows, width = qkv.shape
    part = width // parts

    def kernel(x_ref, o_ref):
        for t in range(parts):
            for j in range(3):
                o_ref[t, j] = x_ref[j, :, t * part : (t + 1) * part].astype(jnp.bfloat16)

    return pl.pallas_call(
        kernel,
        out_shape=jax.ShapeDtypeStruct((parts, 3, rows, part), jnp.bfloat16),
        name="split_heads",
    )(qkv)


def split_rows(matrix, parts, plane, rows):
    width = matrix.shape[1]
    part = width // parts

    def kernel(p_ref, x_ref, o_ref):
        for t in range(parts):
            o_ref[t] = x_ref[:, t * part : (t + 1) * part].astype(jnp.bfloat16)

    return pl.pallas_call(
        kernel,
        out_shape=jax.ShapeDtypeStruct((parts, rows, part), jnp.bfloat16),
        grid_spec=pltpu.PrefetchScalarGridSpec(
            num_scalar_prefetch=1,
            grid=(1,),
            in_specs=[pl.BlockSpec((rows, width), lambda i, p: (p[0], 0))],
            out_specs=pl.BlockSpec((parts, rows, part), lambda i, p: (0, 0, 0)),
        ),
        compiler_params=pltpu.CompilerParams(vmem_limit_bytes=32 * 1024 * 1024),
        name="split_rows",
    )(plane.reshape(1), matrix)


def split_columns(gate, up, down_tail, parts, me):
    rows, width = gate.shape
    tail = down_tail.shape[0]
    part = width // parts
    window = min(width, (part + 127) // 128 * 128 + 128)
    chunk = 48 if rows % 48 == 0 else 16

    def kernel(me_ref, gate_ref, up_ref, tail_ref, *o_refs):
        step = pl.program_id(0)
        groups = chunk // 16

        def columns(x_ref, k):
            left = (me_ref[0] ^ k) * part
            base = jnp.minimum(lax.div(left, 128) * 128, width - window)
            cols = x_ref[:, pl.ds(pl.multiple_of(base, 128), window)]
            cols = pltpu.roll(cols, window - (left - base), 1)[:, :part]
            return cols.astype(jnp.bfloat16).reshape(-1, 16, part)

        for k in range(parts):
            o_refs[k][pl.ds(step * groups, groups)] = columns(gate_ref, k)
            o_refs[k][pl.ds(step * groups + rows // 16, groups)] = columns(up_ref, k)

        @pl.when(step == 0)
        def _():
            for k in range(parts):
                o_refs[k][rows // 8 : (2 * rows + tail) // 16] = columns(tail_ref, k)

    return pl.pallas_call(
        kernel,
        out_shape=[jax.ShapeDtypeStruct(((2 * rows + tail) // 16, 16, part), jnp.bfloat16)]
        * parts,
        grid_spec=pltpu.PrefetchScalarGridSpec(
            num_scalar_prefetch=1,
            grid=(rows // chunk,),
            in_specs=[pl.BlockSpec((chunk, width), lambda i, m: (i, 0))] * 2
            + [pl.BlockSpec((tail, width), lambda i, m: (0, 0))],
            out_specs=[
                pl.BlockSpec(((2 * rows + tail) // 16, 16, part), lambda i, m: (0, 0, 0))
            ]
            * parts,
        ),
        compiler_params=pltpu.CompilerParams(vmem_limit_bytes=40 * 1024 * 1024),
        name="split_columns",
    )(me.reshape(1), gate, up, down_tail)


def copy_rows(moves, outs_shape, sources, me, name):
    count = len(sources)
    outs = len(outs_shape)

    def kernel(me_ref, *refs):
        ins, o_refs, sem = refs[:count], refs[count : count + outs], refs[count + outs]
        copies = [
            pltpu.make_async_copy(source, o_refs[out].at[pl.ds(first, groups)], sem.at[i])
            for i, (source, out, first, groups) in enumerate(moves(me_ref[0], ins))
        ]
        for copy in copies:
            copy.start()
        for copy in copies:
            copy.wait()

    return pl.pallas_call(
        kernel,
        out_shape=[jax.ShapeDtypeStruct(shape, jnp.bfloat16) for shape in outs_shape],
        grid_spec=pltpu.PrefetchScalarGridSpec(
            num_scalar_prefetch=1,
            grid=(1,),
            in_specs=[pl.BlockSpec(memory_space=pl.ANY)] * count,
            out_specs=[pl.BlockSpec(shape, lambda i, m: (0, 0, 0)) for shape in outs_shape],
            scratch_shapes=[pltpu.SemaphoreType.DMA((160,))],
        ),
        compiler_params=pltpu.CompilerParams(vmem_limit_bytes=40 * 1024 * 1024),
        name=name,
    )(me.reshape(1), *sources)


def join_blocks(blocks, me):
    rows, width = blocks[0].shape
    groups = rows // 16

    def moves(index, ins):
        return [(ref, 0, (index ^ k) * groups, groups) for k, ref in enumerate(ins)]

    blocks = [block.reshape(groups, 16, width) for block in blocks]
    shape = (len(blocks) * groups, 16, width)
    return copy_rows(moves, [shape], blocks, me, "join_blocks")[0].reshape(-1, width)


def join_gate_up(blocks, me, rows):
    width = blocks[0].shape[2]
    groups = rows // 16

    def moves(index, ins):
        return [
            (ref.at[pl.ds(i * groups, groups)], i, (index ^ k) * groups, groups)
            for i in range(2)
            for k, ref in enumerate(ins)
        ]

    shape = (len(blocks) * groups, 16, width)
    joined = copy_rows(moves, [shape, shape], blocks, me, "join_gate_up")
    return [matrix.reshape(-1, width) for matrix in joined]


def join_down(gathered, blocks, me, rows):
    planes, count, part_rows, width = gathered.shape
    groups, part_groups = rows // 16, part_rows // 16
    rest = groups - planes * part_groups
    gathered = gathered.reshape(planes, count, part_groups, 16, width)

    def moves(index, ins):
        found = [
            (ins[0].at[p, t], 0, t * groups + p * part_groups, part_groups)
            for p in range(planes)
            for t in range(count)
        ]
        return found + [
            (
                ref.at[pl.ds(2 * groups, rest)],
                0,
                (index ^ k) * groups + planes * part_groups,
                rest,
            )
            for k, ref in enumerate(ins[1:])
        ]

    shape = (count * groups, 16, width)
    return copy_rows(moves, [shape], [gathered, *blocks], me, "join_down")[0].reshape(-1, width)


def expert(mine, other, gate_w, up_w, down_w):
    rows, model = mine.shape
    units = gate_w.shape[1]
    block = min(512, 2 * rows)

    def kernel(mine_in, other_in, gate_in, up_in, down_in, mine_out, other_out, x_all, w_all, sem):
        copies = [
            pltpu.make_async_copy(source, place, sem.at[i])
            for i, (source, place) in enumerate(
                (
                    (other_in, x_all.at[pl.ds(0, rows), :]),
                    (mine_in, x_all.at[pl.ds(rows, rows), :]),
                    (gate_in, w_all.at[0]),
                    (up_in, w_all.at[1]),
                    (down_in, w_all.at[2]),
                )
            )
        ]
        for copy in copies:
            copy.start()
        copies[0].wait()
        copies[1].wait()
        for place in range(0, 2 * rows, block):
            x = x_all[place : place + block]
            if place == 0:
                copies[2].wait()
            gate = jnp.dot(x, w_all[0], preferred_element_type=jnp.float32)
            if place == 0:
                copies[3].wait()
            up = jnp.dot(x, w_all[1], preferred_element_type=jnp.float32)
            act = (gate / (1.0 + jnp.exp(-gate)) * up).astype(jnp.bfloat16)
            if place == 0:
                copies[4].wait()
            res = dot_nt(act, w_all[2]).astype(jnp.bfloat16)
            if block == 2 * rows:
                other_out[...] = res[:rows]
                mine_out[...] = res[rows:]
            elif place < rows:
                other_out[place : place + block] = res
            else:
                mine_out[place - rows : place - rows + block] = res

    return pl.pallas_call(
        kernel,
        out_shape=[jax.ShapeDtypeStruct((rows, model), jnp.bfloat16)] * 2,
        in_specs=[pl.BlockSpec(memory_space=pl.ANY)] * 5,
        out_specs=[pl.BlockSpec(memory_space=pltpu.VMEM)] * 2,
        scratch_shapes=[
            pltpu.VMEM((2 * rows, model), jnp.bfloat16),
            pltpu.VMEM((3, model, units), jnp.bfloat16),
            pltpu.SemaphoreType.DMA((5,)),
        ],
        compiler_params=pltpu.CompilerParams(vmem_limit_bytes=56 * 1024 * 1024),
        cost_estimate=pl.CostEstimate(
            flops=12 * rows * model * units,
            bytes_accessed=6 * model * units,
            transcendentals=2 * rows * units,
        ),
        name="expert",
    )(mine, other, gate_w, up_w, down_w)


def dot_nt(a, b):
    return lax.dot_general(a, b, (((1,), (1,)), ((), ())), preferred_element_type=jnp.float32)


def attention(tokens, weights, cosine, sine, scalars, rows_dev):
    seq, model = tokens.shape
    width = weights.shape[2]
    heads = width // HEAD_DIM
    block = min(256, seq)
    steps = seq // block
    half = HEAD_DIM // 2

    def kernel(s_ref, x_ref, w_ref, cos_ref, sin_ref, kv_ref, att_ref, k_all, v_all):
        step = pl.program_id(0)
        lane = lax.broadcasted_iota(jnp.int32, (block, width), 1)
        low = lax.rem(lane, HEAD_DIM) < half
        head_of = lax.div(lane, HEAD_DIM)
        x = x_ref[...]

        def rotated(j):
            m = jnp.dot(x, w_ref[j], preferred_element_type=jnp.float32)
            turned = jnp.where(
                low, -pltpu.roll(m, width - half, 1), pltpu.roll(m, half, 1)
            )
            return m * cos_ref[...] + turned * sin_ref[...]

        row = step * block + lax.broadcasted_iota(jnp.int32, (block, width), 0)
        valid = row < s_ref[0]
        start = pl.multiple_of(step * block, block)
        key = rotated(1)
        k_all[pl.ds(start, block), :] = key.astype(jnp.bfloat16)
        kv_ref[0] = jnp.where(valid, key, 0.0).astype(jnp.bfloat16)
        value = jnp.dot(x, w_ref[2], preferred_element_type=jnp.float32)
        v_all[pl.ds(start, block), :] = value.astype(jnp.bfloat16)
        kv_ref[1] = jnp.where(valid, value, 0.0).astype(jnp.bfloat16)
        query = rotated(0).astype(jnp.bfloat16).astype(jnp.float32) * HEAD_DIM ** (-0.5)

        for here in range(steps):

            @pl.when(step == here)
            def _():
                lo = here * block
                causal = lax.broadcasted_iota(
                    jnp.int32, (block, block), 0
                ) >= lax.broadcasted_iota(jnp.int32, (block, block), 1)
                out = jnp.zeros((block, width), jnp.float32)
                for h in range(heads):
                    q = jnp.where(head_of == h, query, 0.0).astype(jnp.bfloat16)
                    diag = jnp.where(causal, dot_nt(q, k_all[lo : lo + block, :]), -1e30)
                    top = jnp.max(diag, axis=-1, keepdims=True)
                    if lo:
                        past = dot_nt(q, k_all[:lo, :])
                        top = jnp.maximum(top, jnp.max(past, axis=-1, keepdims=True))
                        past = jnp.exp(past - top)
                    diag = jnp.exp(diag - top)
                    total = jnp.sum(diag, axis=-1, keepdims=True)
                    if lo:
                        total = total + jnp.sum(past, axis=-1, keepdims=True)
                    inv = 1.0 / total
                    res = jnp.dot(
                        (diag * inv).astype(jnp.bfloat16),
                        v_all[lo : lo + block, :],
                        preferred_element_type=jnp.float32,
                    )
                    if lo:
                        res = res + jnp.dot(
                            (past * inv).astype(jnp.bfloat16),
                            v_all[:lo, :],
                            preferred_element_type=jnp.float32,
                        )
                    out = jnp.where(head_of == h, res, out)
                out = out.astype(jnp.bfloat16)
                for piece in range(block // rows_dev):
                    dev = here * (block // rows_dev) + piece
                    slot = jnp.where(s_ref[1] == dev % 2, 0, 1)
                    att_ref[slot, (dev // 2) * rows_dev : (dev // 2 + 1) * rows_dev, :] = out[
                        piece * rows_dev : (piece + 1) * rows_dev
                    ]

    return pl.pallas_call(
        kernel,
        out_shape=(
            jax.ShapeDtypeStruct((2, seq, width), jnp.bfloat16),
            jax.ShapeDtypeStruct((2, seq // 2, width), jnp.bfloat16),
        ),
        grid_spec=pltpu.PrefetchScalarGridSpec(
            num_scalar_prefetch=1,
            grid=(steps,),
            in_specs=[
                pl.BlockSpec((block, model), lambda i, s: (i, 0)),
                pl.BlockSpec((3, model, width), lambda i, s: (0, 0, 0)),
                pl.BlockSpec((block, width), lambda i, s: (i, 0)),
                pl.BlockSpec((block, width), lambda i, s: (i, 0)),
            ],
            out_specs=(
                pl.BlockSpec((2, block, width), lambda i, s: (0, i, 0)),
                pl.BlockSpec((2, seq // 2, width), lambda i, s: (0, 0, 0)),
            ),
            scratch_shapes=[
                pltpu.VMEM((seq, width), jnp.bfloat16),
                pltpu.VMEM((seq, width), jnp.bfloat16),
            ],
        ),
        compiler_params=pltpu.CompilerParams(vmem_limit_bytes=48 * 1024 * 1024),
        cost_estimate=pl.CostEstimate(
            flops=6 * seq * model * width + 4 * seq * seq * width,
            bytes_accessed=2 * (seq * model + 3 * model * width),
            transcendentals=seq * seq * heads,
        ),
        name="attention",
    )(scalars, tokens, weights, cosine, sine)


def rms_scale(values, gain_row):
    mean_sq = jnp.mean(values * values, axis=-1, keepdims=True)
    return values * lax.rsqrt(mean_sq + 1e-05) * gain_row


def shards(
    hidden_in,
    prompt_len,
    start_pos,
    routes,
    trainer_qkv,
    trainer_out,
    trainer_gate,
    trainer_up,
    trainer_down,
    attn_gain,
    moe_gain,
    router,
):
    size = lax.axis_size("tensor")
    replicas = lax.axis_size("dp")
    chips = size // 2
    me = lax.axis_index("tensor").astype(jnp.int32)
    plane = lax.axis_index("dp").astype(jnp.int32)
    chip, core = me // 2, me % 2
    rows_dev, model = hidden_in.shape[1], hidden_in.shape[2]
    seq_len = rows_dev * size
    length = prompt_len[0]
    offset = start_pos[0]
    my_first = me * rows_dev

    mat_rows = trainer_down.shape[0]
    part_rows = mat_rows // (16 * replicas) * 16
    local_width = trainer_qkv.shape[2] // size
    qkv_parts = split_heads(trainer_qkv.transpose(1, 0, 2), size)
    qkv_cols = lax.all_to_all(qkv_parts, "tensor", 0, 0, tiled=True)
    parts = split_columns(
        trainer_gate, trainer_up, trainer_down[part_rows * replicas :], size, me
    )
    tokens = hidden_in[0].astype(jnp.float32)
    normed = rms_scale(tokens, attn_gain).astype(jnp.bfloat16)
    qkv_cols, normed, *parts = lax.optimization_barrier((qkv_cols, normed, *parts))
    qkv_all = lax.all_gather(qkv_cols, "dp", axis=0)
    down_parts = split_rows(trainer_down, size, plane, part_rows)
    down_cols = lax.all_to_all(down_parts, "tensor", 0, 0, tiled=True)
    same_core = [normed] + [send(normed, size, 2 * j) for j in range(1, chips)]
    other_core = send(jnp.stack(same_core), size, 1)
    blocks = []
    for j in range(chips):
        blocks += [same_core[j], other_core[j]]
    piece = join_blocks(blocks, me)

    first = [1, 2, 4][: size.bit_length() - 1]
    rest = [k for k in range(3, size) if k not in first]
    early = [send(parts[k], size, k) for k in first]
    late = list(lax.optimization_barrier((*[parts[k] for k in rest], *early)))
    early = late[len(rest) :]
    late = [send(block, size, k) for block, k in zip(late, rest)]

    half_dim = HEAD_DIM // 2
    inv_freq = jnp.power(
        10000.0, jnp.arange(half_dim, dtype=jnp.float32) * (-2.0 / HEAD_DIM)
    )
    places = offset + jnp.arange(seq_len, dtype=jnp.int32)
    angles = places.astype(jnp.float32)[:, None] * jnp.tile(inv_freq, local_width // half_dim)
    cosine, sine_part = jnp.cos(angles), jnp.sin(angles)
    server_out = lax.all_gather(trainer_out.astype(jnp.bfloat16), "dp", axis=0, tiled=True)
    qkv_all, down_cols = lax.optimization_barrier((qkv_all, down_cols))
    down_all = lax.all_gather(down_cols, "dp", axis=0)
    qkv_all, piece, cosine, sine_part, *early = lax.optimization_barrier(
        (qkv_all, piece, cosine, sine_part, *early)
    )
    qkv_server = qkv_all.transpose(2, 1, 0, 3, 4).reshape(3, model, local_width)
    server_qkv = qkv_server.transpose(1, 0, 2)
    scalars = jnp.stack([length, core])
    cache_pair, attended = attention(
        piece, qkv_server, cosine, sine_part, scalars, rows_dev
    )
    half = len(late) // 2
    attended, *late[:half] = lax.optimization_barrier((attended, *late[:half]))
    out_pair = jnp.concatenate([server_out, send(server_out, size, 1)], axis=0)

    att_pair = jnp.concatenate([attended[0], send(attended[1], size, 1)], axis=-1)
    att_pair, *late[half:] = lax.optimization_barrier((att_pair, *late[half:]))
    joined = [parts[0]] * size
    for block, k in zip(early + late, first + rest):
        joined[k] = block

    pieces = 2
    rows = rows_dev // pieces
    att_pair = att_pair.reshape(chips, pieces, rows, 2 * local_width)

    def attn_part(j, h):
        here = lax.dynamic_index_in_dim(att_pair, chip ^ j, 0, keepdims=False)[h]
        return jnp.dot(here, out_pair, preferred_element_type=jnp.float32)

    gate, up = join_gate_up(joined, me, mat_rows)
    flipped = [gate, up]
    middles, normed_moes, moe_rows = [], [], []
    got = []
    for h in range(pieces):
        sent = [attn_part(j, h).astype(jnp.bfloat16) for j in range(1, chips)]
        if h:
            sent = list(lax.optimization_barrier((*sent, *got)))[: chips - 1]
            flipped[h], *normed_moes = lax.optimization_barrier((flipped[h], *normed_moes))
        got = [send(block, size, 2 * j + 2) for j, block in enumerate(sent)]
        attn_sum = add_up(attn_part(0, h), got)
        flipped[h] = with_layout_constraint(flipped[h], Layout((1, 0)))
        attn_sum, flipped[h], *normed_moes = lax.optimization_barrier(
            (attn_sum, flipped[h], *normed_moes)
        )
        middles.append((tokens[h * rows : (h + 1) * rows] + attn_sum).astype(jnp.bfloat16))
        normed = rms_scale(middles[h].astype(jnp.float32), moe_gain).astype(jnp.bfloat16)
        normed_moes.append(normed)
        if h:
            normed, *moe_rows[h - 1] = lax.optimization_barrier((normed, *moe_rows[h - 1]))
        moe_rows.append([normed] + [send(normed, size, 2 * j) for j in range(1, chips)])
        if h == 0:
            down = join_down(down_all, joined, me, mat_rows)
            *moe_rows[0], gate, up, down = lax.optimization_barrier(
                (*moe_rows[0], gate, up, down)
            )
    middle = jnp.concatenate(middles, axis=0)
    normed_moe = jnp.concatenate(normed_moes, axis=0)

    local_routes = lax.dynamic_slice_in_dim(routes[0], my_first, rows_dev, 0)
    local_valid = my_first + jnp.arange(rows_dev, dtype=jnp.int32) < length
    logits = jnp.dot(normed_moe, router, preferred_element_type=jnp.float32)
    expert_ids = jnp.arange(router.shape[1], dtype=jnp.int32)
    logit_first = jnp.sum(
        jnp.where(local_routes[:, 0:1] == expert_ids[None, :], logits, 0.0), axis=1
    )
    logit_second = jnp.sum(
        jnp.where(local_routes[:, 1:2] == expert_ids[None, :], logits, 0.0), axis=1
    )
    other_logit = jnp.where(local_routes[:, 0] == 0, logit_second, logit_first)
    local_routed = jnp.any(local_routes == 0, axis=1)
    route_w = jnp.where(local_routed, jax.nn.sigmoid(logits[:, 0] - other_logit), 0.0)

    expert_sums, back = [], []
    for h in range(pieces):
        moe_mine = jnp.stack(moe_rows[h])
        moe_other = send(moe_mine, size, 1)
        sums_mine, sums_other = expert(
            moe_mine.reshape(-1, model), moe_other.reshape(-1, model), gate, up, down
        )
        if h:
            sums_other, *back = lax.optimization_barrier((sums_other, *back))
            expert_sums.append(add_up(total, back))
        else:
            sums_other, *moe_rows[1] = lax.optimization_barrier((sums_other, *moe_rows[1]))
        from_other = send(sums_other, size, 1)
        sums = [
            sums_mine[j * rows : (j + 1) * rows].astype(jnp.float32)
            + from_other[j * rows : (j + 1) * rows].astype(jnp.float32)
            for j in range(chips)
        ]
        total = sums[0]
        sent = [block.astype(jnp.bfloat16) for block in sums[1:]]
        back = [send(block, size, 2 * j + 2) for j, block in enumerate(sent)]
    expert_sums.append(add_up(total, back))
    down_late, _ = lax.optimization_barrier((down, sent[0]))
    expert_sum = jnp.concatenate(expert_sums, axis=0)
    expert_sum = jnp.where(local_routed[:, None], expert_sum, 0.0)
    result = middle.astype(jnp.float32) + route_w[:, None] * expert_sum
    hidden_out = jnp.where(local_valid[:, None], result, 0.0).astype(jnp.bfloat16)[None]
    return (
        server_qkv,
        server_out,
        *flipped,
        down_late,
        hidden_out,
        cache_pair[None],
    )


def solution(mesh):
    placed = (
        P("dp", "tensor", None),
        P("dp"),
        P("dp"),
        P("dp", None, None),
        P(("tensor", "dp"), None, None),
        P(("tensor", "dp"), None),
        P("tensor", None),
        P("tensor", None),
        P("tensor", None),
        P(),
        P(),
        P(),
    )
    return jax.shard_map(
        shards,
        mesh=mesh,
        in_specs=placed,
        out_specs=(
            P(None, None, "tensor"),
            P("tensor", None),
            P(None, "tensor"),
            P(None, "tensor"),
            P(None, "tensor"),
            P("dp", "tensor", None),
            P("dp", None, None, "tensor"),
        ),
        check_vma=False,
    )
```

```python
import jax
import jax.numpy as jnp
from jax import lax
from jax.experimental import pallas as pl
from jax.experimental.layout import Layout, with_layout_constraint
from jax.experimental.pallas import tpu as pltpu
from jax.sharding import PartitionSpec as P

HEAD_DIM = 64


def swap_pairs(size, step):
    return [(i, i ^ step) for i in range(size)]


def send(block, size, step):
    return lax.ppermute(block, "tensor", swap_pairs(size, step))


def add_up(total, blocks):
    for block in blocks:
        total = total + block.astype(jnp.float32)
    return total


def split_heads(qkv, parts):
    _, rows, width = qkv.shape
    part = width // parts

    def kernel(x_ref, o_ref):
        for t in range(parts):
            for j in range(3):
                o_ref[t, j] = x_ref[j, :, t * part : (t + 1) * part].astype(jnp.bfloat16)

    return pl.pallas_call(
        kernel,
        out_shape=jax.ShapeDtypeStruct((parts, 3, rows, part), jnp.bfloat16),
        name="split_heads",
    )(qkv)


def split_rows(matrix, parts, plane, rows):
    width = matrix.shape[1]
    part = width // parts

    def kernel(p_ref, x_ref, o_ref):
        for t in range(parts):
            o_ref[t] = x_ref[:, t * part : (t + 1) * part].astype(jnp.bfloat16)

    return pl.pallas_call(
        kernel,
        out_shape=jax.ShapeDtypeStruct((parts, rows, part), jnp.bfloat16),
        grid_spec=pltpu.PrefetchScalarGridSpec(
            num_scalar_prefetch=1,
            grid=(1,),
            in_specs=[pl.BlockSpec((rows, width), lambda i, p: (p[0], 0))],
            out_specs=pl.BlockSpec((parts, rows, part), lambda i, p: (0, 0, 0)),
        ),
        compiler_params=pltpu.CompilerParams(vmem_limit_bytes=32 * 1024 * 1024),
        name="split_rows",
    )(plane.reshape(1), matrix)


def split_columns(gate, up, down_tail, parts, me):
    rows, width = gate.shape
    tail = down_tail.shape[0]
    part = width // parts
    window = min(width, (part + 127) // 128 * 128 + 128)
    chunk = 48 if rows % 48 == 0 else 16

    def kernel(me_ref, gate_ref, up_ref, tail_ref, *o_refs):
        step = pl.program_id(0)
        groups = chunk // 16

        def columns(x_ref, k):
            left = (me_ref[0] ^ k) * part
            base = jnp.minimum(lax.div(left, 128) * 128, width - window)
            cols = x_ref[:, pl.ds(pl.multiple_of(base, 128), window)]
            cols = pltpu.roll(cols, window - (left - base), 1)[:, :part]
            return cols.astype(jnp.bfloat16).reshape(-1, 16, part)

        for k in range(parts):
            o_refs[k][pl.ds(step * groups, groups)] = columns(gate_ref, k)
            o_refs[k][pl.ds(step * groups + rows // 16, groups)] = columns(up_ref, k)

        @pl.when(step == 0)
        def _():
            for k in range(parts):
                o_refs[k][rows // 8 : (2 * rows + tail) // 16] = columns(tail_ref, k)

    return pl.pallas_call(
        kernel,
        out_shape=[jax.ShapeDtypeStruct(((2 * rows + tail) // 16, 16, part), jnp.bfloat16)]
        * parts,
        grid_spec=pltpu.PrefetchScalarGridSpec(
            num_scalar_prefetch=1,
            grid=(rows // chunk,),
            in_specs=[pl.BlockSpec((chunk, width), lambda i, m: (i, 0))] * 2
            + [pl.BlockSpec((tail, width), lambda i, m: (0, 0))],
            out_specs=[
                pl.BlockSpec(((2 * rows + tail) // 16, 16, part), lambda i, m: (0, 0, 0))
            ]
            * parts,
        ),
        compiler_params=pltpu.CompilerParams(vmem_limit_bytes=40 * 1024 * 1024),
        name="split_columns",
    )(me.reshape(1), gate, up, down_tail)


def copy_rows(moves, outs_shape, sources, me, name):
    count = len(sources)
    outs = len(outs_shape)

    def kernel(me_ref, *refs):
        ins, o_refs, sem = refs[:count], refs[count : count + outs], refs[count + outs]
        copies = [
            pltpu.make_async_copy(source, o_refs[out].at[pl.ds(first, groups)], sem.at[i])
            for i, (source, out, first, groups) in enumerate(moves(me_ref[0], ins))
        ]
        for copy in copies:
            copy.start()
        for copy in copies:
            copy.wait()

    return pl.pallas_call(
        kernel,
        out_shape=[jax.ShapeDtypeStruct(shape, jnp.bfloat16) for shape in outs_shape],
        grid_spec=pltpu.PrefetchScalarGridSpec(
            num_scalar_prefetch=1,
            grid=(1,),
            in_specs=[pl.BlockSpec(memory_space=pl.ANY)] * count,
            out_specs=[pl.BlockSpec(shape, lambda i, m: (0, 0, 0)) for shape in outs_shape],
            scratch_shapes=[pltpu.SemaphoreType.DMA((160,))],
        ),
        compiler_params=pltpu.CompilerParams(vmem_limit_bytes=40 * 1024 * 1024),
        name=name,
    )(me.reshape(1), *sources)


def join_blocks(blocks, me):
    rows, width = blocks[0].shape
    groups = rows // 16

    def moves(index, ins):
        return [(ref, 0, (index ^ k) * groups, groups) for k, ref in enumerate(ins)]

    blocks = [block.reshape(groups, 16, width) for block in blocks]
    shape = (len(blocks) * groups, 16, width)
    return copy_rows(moves, [shape], blocks, me, "join_blocks")[0].reshape(-1, width)


def join_gate_up(blocks, me, rows):
    width = blocks[0].shape[2]
    groups = rows // 16

    def moves(index, ins):
        return [
            (ref.at[pl.ds(i * groups, groups)], i, (index ^ k) * groups, groups)
            for i in range(2)
            for k, ref in enumerate(ins)
        ]

    shape = (len(blocks) * groups, 16, width)
    joined = copy_rows(moves, [shape, shape], blocks, me, "join_gate_up")
    return [matrix.reshape(-1, width) for matrix in joined]


def join_down(gathered, blocks, me, rows):
    planes, count, part_rows, width = gathered.shape
    groups, part_groups = rows // 16, part_rows // 16
    rest = groups - planes * part_groups
    gathered = gathered.reshape(planes, count, part_groups, 16, width)

    def moves(index, ins):
        found = [
            (ins[0].at[p, t], 0, t * groups + p * part_groups, part_groups)
            for p in range(planes)
            for t in range(count)
        ]
        return found + [
            (
                ref.at[pl.ds(2 * groups, rest)],
                0,
                (index ^ k) * groups + planes * part_groups,
                rest,
            )
            for k, ref in enumerate(ins[1:])
        ]

    shape = (count * groups, 16, width)
    return copy_rows(moves, [shape], [gathered, *blocks], me, "join_down")[0].reshape(-1, width)


def project(mine, other, own_w, other_w, chip, rows_dev, pieces):
    total, width = mine.shape
    chips = total // rows_dev
    model = own_w.shape[1]
    rows = rows_dev // pieces

    def kernel(chip_ref, mine_ref, other_ref, own_ref, other_w_ref, *outs):
        def ordered(ref):
            places = [
                pl.multiple_of((chip_ref[0] ^ j) * rows_dev, rows_dev) for j in range(chips)
            ]
            return jnp.concatenate([ref[pl.ds(place, rows_dev), :] for place in places], axis=0)

        res = jnp.dot(ordered(mine_ref), own_ref[...], preferred_element_type=jnp.float32)
        res = res + jnp.dot(
            ordered(other_ref), other_w_ref[...], preferred_element_type=jnp.float32
        )
        for h in range(pieces):
            outs[h][...] = res[h * rows : (h + 1) * rows]
            for j in range(1, chips):
                first = j * rows_dev + h * rows
                outs[pieces + h * (chips - 1) + j - 1][...] = res[first : first + rows].astype(
                    jnp.bfloat16
                )
        outs[-1][...] = own_ref[...]

    whole = [
        pl.BlockSpec(shape, lambda i, c: (0, 0))
        for shape in (mine.shape, other.shape, own_w.shape, other_w.shape)
    ]
    sent = [(rows, model)] * (pieces * (chips - 1))
    res = pl.pallas_call(
        kernel,
        out_shape=[jax.ShapeDtypeStruct((rows, model), jnp.float32)] * pieces
        + [jax.ShapeDtypeStruct(shape, jnp.bfloat16) for shape in sent + [own_w.shape]],
        grid_spec=pltpu.PrefetchScalarGridSpec(
            num_scalar_prefetch=1,
            grid=(1,),
            in_specs=whole,
            out_specs=[
                pl.BlockSpec(shape, lambda i, c: (0, 0))
                for shape in [(rows, model)] * pieces + sent + [own_w.shape]
            ],
        ),
        compiler_params=pltpu.CompilerParams(vmem_limit_bytes=56 * 1024 * 1024),
        name="project",
    )(chip.reshape(1), mine, other, own_w, other_w)
    sent = [res[pieces + h * (chips - 1) :][: chips - 1] for h in range(pieces)]
    return res[:pieces], sent, res[-1]


def expert(mine, other, gate_w, up_w, down_w):
    rows, model = mine.shape
    units = gate_w.shape[1]
    block = min(512, 2 * rows)

    def kernel(mine_in, other_in, gate_in, up_in, down_in, mine_out, other_out, x_all, w_all, sem):
        copies = [
            pltpu.make_async_copy(source, place, sem.at[i])
            for i, (source, place) in enumerate(
                (
                    (other_in, x_all.at[pl.ds(0, rows), :]),
                    (mine_in, x_all.at[pl.ds(rows, rows), :]),
                    (gate_in, w_all.at[0]),
                    (up_in, w_all.at[1]),
                    (down_in, w_all.at[2]),
                )
            )
        ]
        for copy in copies:
            copy.start()
        copies[0].wait()
        copies[1].wait()
        for place in range(0, 2 * rows, block):
            x = x_all[place : place + block]
            if place == 0:
                copies[2].wait()
            gate = jnp.dot(x, w_all[0], preferred_element_type=jnp.float32)
            if place == 0:
                copies[3].wait()
            up = jnp.dot(x, w_all[1], preferred_element_type=jnp.float32)
            act = (gate / (1.0 + jnp.exp(-gate)) * up).astype(jnp.bfloat16)
            if place == 0:
                copies[4].wait()
            res = dot_nt(act, w_all[2]).astype(jnp.bfloat16)
            if block == 2 * rows:
                other_out[...] = res[:rows]
                mine_out[...] = res[rows:]
            elif place < rows:
                other_out[place : place + block] = res
            else:
                mine_out[place - rows : place - rows + block] = res

    return pl.pallas_call(
        kernel,
        out_shape=[jax.ShapeDtypeStruct((rows, model), jnp.bfloat16)] * 2,
        in_specs=[pl.BlockSpec(memory_space=pl.ANY)] * 5,
        out_specs=[pl.BlockSpec(memory_space=pltpu.VMEM)] * 2,
        scratch_shapes=[
            pltpu.VMEM((2 * rows, model), jnp.bfloat16),
            pltpu.VMEM((3, model, units), jnp.bfloat16),
            pltpu.SemaphoreType.DMA((5,)),
        ],
        compiler_params=pltpu.CompilerParams(vmem_limit_bytes=56 * 1024 * 1024),
        cost_estimate=pl.CostEstimate(
            flops=12 * rows * model * units,
            bytes_accessed=6 * model * units,
            transcendentals=2 * rows * units,
        ),
        name="expert",
    )(mine, other, gate_w, up_w, down_w)


def dot_nt(a, b):
    return lax.dot_general(a, b, (((1,), (1,)), ((), ())), preferred_element_type=jnp.float32)


def attention(tokens, weights, cosine, sine, scalars, rows_dev):
    seq, model = tokens.shape
    width = weights.shape[2]
    heads = width // HEAD_DIM
    block = min(256, seq)
    steps = seq // block
    half = HEAD_DIM // 2

    def kernel(s_ref, x_ref, w_ref, cos_ref, sin_ref, kv_ref, att_ref, k_all, v_all):
        step = pl.program_id(0)
        lane = lax.broadcasted_iota(jnp.int32, (block, width), 1)
        low = lax.rem(lane, HEAD_DIM) < half
        head_of = lax.div(lane, HEAD_DIM)
        x = x_ref[...]

        def rotated(j):
            m = jnp.dot(x, w_ref[j], preferred_element_type=jnp.float32)
            turned = jnp.where(
                low, -pltpu.roll(m, width - half, 1), pltpu.roll(m, half, 1)
            )
            return m * cos_ref[...] + turned * sin_ref[...]

        row = step * block + lax.broadcasted_iota(jnp.int32, (block, width), 0)
        valid = row < s_ref[0]
        start = pl.multiple_of(step * block, block)
        key = rotated(1)
        k_all[pl.ds(start, block), :] = key.astype(jnp.bfloat16)
        kv_ref[0] = jnp.where(valid, key, 0.0).astype(jnp.bfloat16)
        value = jnp.dot(x, w_ref[2], preferred_element_type=jnp.float32)
        v_all[pl.ds(start, block), :] = value.astype(jnp.bfloat16)
        kv_ref[1] = jnp.where(valid, value, 0.0).astype(jnp.bfloat16)
        query = rotated(0).astype(jnp.bfloat16).astype(jnp.float32) * HEAD_DIM ** (-0.5)

        for here in range(steps):

            @pl.when(step == here)
            def _():
                lo = here * block
                causal = lax.broadcasted_iota(
                    jnp.int32, (block, block), 0
                ) >= lax.broadcasted_iota(jnp.int32, (block, block), 1)
                out = jnp.zeros((block, width), jnp.float32)
                for h in range(heads):
                    q = jnp.where(head_of == h, query, 0.0).astype(jnp.bfloat16)
                    diag = jnp.where(causal, dot_nt(q, k_all[lo : lo + block, :]), -1e30)
                    top = jnp.max(diag, axis=-1, keepdims=True)
                    if lo:
                        past = dot_nt(q, k_all[:lo, :])
                        top = jnp.maximum(top, jnp.max(past, axis=-1, keepdims=True))
                        past = jnp.exp(past - top)
                    diag = jnp.exp(diag - top)
                    total = jnp.sum(diag, axis=-1, keepdims=True)
                    if lo:
                        total = total + jnp.sum(past, axis=-1, keepdims=True)
                    inv = 1.0 / total
                    res = jnp.dot(
                        (diag * inv).astype(jnp.bfloat16),
                        v_all[lo : lo + block, :],
                        preferred_element_type=jnp.float32,
                    )
                    if lo:
                        res = res + jnp.dot(
                            (past * inv).astype(jnp.bfloat16),
                            v_all[:lo, :],
                            preferred_element_type=jnp.float32,
                        )
                    out = jnp.where(head_of == h, res, out)
                out = out.astype(jnp.bfloat16)
                for piece in range(block // rows_dev):
                    dev = here * (block // rows_dev) + piece
                    slot = jnp.where(s_ref[1] == dev % 2, 0, 1)
                    att_ref[slot, (dev // 2) * rows_dev : (dev // 2 + 1) * rows_dev, :] = out[
                        piece * rows_dev : (piece + 1) * rows_dev
                    ]

    return pl.pallas_call(
        kernel,
        out_shape=(
            jax.ShapeDtypeStruct((2, seq, width), jnp.bfloat16),
            jax.ShapeDtypeStruct((2, seq // 2, width), jnp.bfloat16),
        ),
        grid_spec=pltpu.PrefetchScalarGridSpec(
            num_scalar_prefetch=1,
            grid=(steps,),
            in_specs=[
                pl.BlockSpec((block, model), lambda i, s: (i, 0)),
                pl.BlockSpec((3, model, width), lambda i, s: (0, 0, 0)),
                pl.BlockSpec((block, width), lambda i, s: (i, 0)),
                pl.BlockSpec((block, width), lambda i, s: (i, 0)),
            ],
            out_specs=(
                pl.BlockSpec((2, block, width), lambda i, s: (0, i, 0)),
                pl.BlockSpec((2, seq // 2, width), lambda i, s: (0, 0, 0)),
            ),
            scratch_shapes=[
                pltpu.VMEM((seq, width), jnp.bfloat16),
                pltpu.VMEM((seq, width), jnp.bfloat16),
            ],
        ),
        compiler_params=pltpu.CompilerParams(vmem_limit_bytes=48 * 1024 * 1024),
        cost_estimate=pl.CostEstimate(
            flops=6 * seq * model * width + 4 * seq * seq * width,
            bytes_accessed=2 * (seq * model + 3 * model * width),
            transcendentals=seq * seq * heads,
        ),
        name="attention",
    )(scalars, tokens, weights, cosine, sine)


def rms_scale(values, gain_row):
    mean_sq = jnp.mean(values * values, axis=-1, keepdims=True)
    return values * lax.rsqrt(mean_sq + 1e-05) * gain_row


def shards(
    hidden_in,
    prompt_len,
    start_pos,
    routes,
    trainer_qkv,
    trainer_out,
    trainer_gate,
    trainer_up,
    trainer_down,
    attn_gain,
    moe_gain,
    router,
):
    size = lax.axis_size("tensor")
    replicas = lax.axis_size("dp")
    chips = size // 2
    me = lax.axis_index("tensor").astype(jnp.int32)
    plane = lax.axis_index("dp").astype(jnp.int32)
    chip, core = me // 2, me % 2
    rows_dev, model = hidden_in.shape[1], hidden_in.shape[2]
    seq_len = rows_dev * size
    length = prompt_len[0]
    offset = start_pos[0]
    my_first = me * rows_dev

    mat_rows = trainer_down.shape[0]
    part_rows = mat_rows // (16 * replicas) * 16
    local_width = trainer_qkv.shape[2] // size
    qkv_parts = split_heads(trainer_qkv.transpose(1, 0, 2), size)
    qkv_cols = lax.all_to_all(qkv_parts, "tensor", 0, 0, tiled=True)
    parts = split_columns(
        trainer_gate, trainer_up, trainer_down[part_rows * replicas :], size, me
    )
    tokens = hidden_in[0].astype(jnp.float32)
    normed = rms_scale(tokens, attn_gain).astype(jnp.bfloat16)
    qkv_cols, normed, *parts = lax.optimization_barrier((qkv_cols, normed, *parts))
    qkv_all = lax.all_gather(qkv_cols, "dp", axis=0)
    down_parts = split_rows(trainer_down, size, plane, part_rows)
    down_cols = lax.all_to_all(down_parts, "tensor", 0, 0, tiled=True)
    same_core = [normed] + [send(normed, size, 2 * j) for j in range(1, chips)]
    other_core = send(jnp.stack(same_core), size, 1)
    blocks = []
    for j in range(chips):
        blocks += [same_core[j], other_core[j]]
    piece = join_blocks(blocks, me)

    first = [1, 2, 4][: size.bit_length() - 1]
    rest = [k for k in range(3, size) if k not in first]
    early = [send(parts[k], size, k) for k in first]
    late = list(lax.optimization_barrier((*[parts[k] for k in rest], *early)))
    early = late[len(rest) :]
    late = [send(block, size, k) for block, k in zip(late, rest)]

    half_dim = HEAD_DIM // 2
    inv_freq = jnp.power(
        10000.0, jnp.arange(half_dim, dtype=jnp.float32) * (-2.0 / HEAD_DIM)
    )
    places = offset + jnp.arange(seq_len, dtype=jnp.int32)
    angles = places.astype(jnp.float32)[:, None] * jnp.tile(inv_freq, local_width // half_dim)
    cosine, sine_part = jnp.cos(angles), jnp.sin(angles)
    server_out = lax.all_gather(trainer_out.astype(jnp.bfloat16), "dp", axis=0, tiled=True)
    qkv_all, down_cols = lax.optimization_barrier((qkv_all, down_cols))
    down_all = lax.all_gather(down_cols, "dp", axis=0)
    qkv_all, piece, cosine, sine_part, *early = lax.optimization_barrier(
        (qkv_all, piece, cosine, sine_part, *early)
    )
    qkv_server = qkv_all.transpose(2, 1, 0, 3, 4).reshape(3, model, local_width)
    server_qkv = qkv_server.transpose(1, 0, 2)
    scalars = jnp.stack([length, core])
    cache_pair, attended = attention(
        piece, qkv_server, cosine, sine_part, scalars, rows_dev
    )
    half = len(late) // 2
    attended, *late[:half] = lax.optimization_barrier((attended, *late[:half]))
    pieces = 2
    rows = rows_dev // pieces
    out_other = send(server_out, size, 1)
    att_other = send(attended[1], size, 1)
    att_other, *late[half:] = lax.optimization_barrier((att_other, *late[half:]))
    own_part, partial, server_out = project(
        attended[0], att_other, server_out, out_other, chip, rows_dev, pieces
    )
    joined = [parts[0]] * size
    for block, k in zip(early + late, first + rest):
        joined[k] = block

    gate, up = join_gate_up(joined, me, mat_rows)
    down = join_down(down_all, joined, me, mat_rows)
    flipped = [gate, up]
    middles, normed_moes, moe_rows = [], [], []
    got = []
    for h in range(pieces):
        sent = partial[h]
        if h:
            sent = list(lax.optimization_barrier((*sent, *got)))[: chips - 1]
        got = [send(block, size, 2 * j + 2) for j, block in enumerate(sent)]
        if h:
            *got, down, normed_moes[0] = lax.optimization_barrier((*got, down, normed_moes[0]))
        attn_sum = add_up(own_part[h], got)
        if h:
            flipped[1], *normed_moes = lax.optimization_barrier((flipped[1], *normed_moes))
            flipped[1] = with_layout_constraint(flipped[1], Layout((1, 0)))
            *moe_rows[0], flipped[1] = lax.optimization_barrier((*moe_rows[0], flipped[1]))
        else:
            flipped[0] = with_layout_constraint(flipped[0], Layout((1, 0)))
            attn_sum, flipped[0] = lax.optimization_barrier((attn_sum, flipped[0]))
        middles.append((tokens[h * rows : (h + 1) * rows] + attn_sum).astype(jnp.bfloat16))
        normed = rms_scale(middles[h].astype(jnp.float32), moe_gain).astype(jnp.bfloat16)
        normed_moes.append(normed)
        if h:
            normed, *moe_rows[0] = lax.optimization_barrier((normed, *moe_rows[0]))
        moe_rows.append([normed] + [send(normed, size, 2 * j) for j in range(1, chips)])
    *moe_rows[0], gate, up, down = lax.optimization_barrier((*moe_rows[0], gate, up, down))
    middle = jnp.concatenate(middles, axis=0)
    normed_moe = jnp.concatenate(normed_moes, axis=0)

    local_routes = lax.dynamic_slice_in_dim(routes[0], my_first, rows_dev, 0)
    local_valid = my_first + jnp.arange(rows_dev, dtype=jnp.int32) < length
    logits = jnp.dot(normed_moe, router, preferred_element_type=jnp.float32)
    expert_ids = jnp.arange(router.shape[1], dtype=jnp.int32)
    logit_first = jnp.sum(
        jnp.where(local_routes[:, 0:1] == expert_ids[None, :], logits, 0.0), axis=1
    )
    logit_second = jnp.sum(
        jnp.where(local_routes[:, 1:2] == expert_ids[None, :], logits, 0.0), axis=1
    )
    other_logit = jnp.where(local_routes[:, 0] == 0, logit_second, logit_first)
    local_routed = jnp.any(local_routes == 0, axis=1)
    route_w = jnp.where(local_routed, jax.nn.sigmoid(logits[:, 0] - other_logit), 0.0)

    expert_sums, back = [], []
    for h in range(pieces):
        moe_mine = jnp.stack(moe_rows[h])
        moe_other = send(moe_mine, size, 1)
        sums_mine, sums_other = expert(
            moe_mine.reshape(-1, model), moe_other.reshape(-1, model), gate, up, down
        )
        if h:
            sums_other, *back = lax.optimization_barrier((sums_other, *back))
            expert_sums.append(add_up(total, back))
        else:
            sums_other, *moe_rows[1] = lax.optimization_barrier((sums_other, *moe_rows[1]))
        from_other = send(sums_other, size, 1)
        sums = [
            sums_mine[j * rows : (j + 1) * rows].astype(jnp.float32)
            + from_other[j * rows : (j + 1) * rows].astype(jnp.float32)
            for j in range(chips)
        ]
        total = sums[0]
        sent = [block.astype(jnp.bfloat16) for block in sums[1:]]
        back = [send(block, size, 2 * j + 2) for j, block in enumerate(sent)]
    expert_sums.append(add_up(total, back))
    down_late, _ = lax.optimization_barrier((down, sent[0]))
    expert_sum = jnp.concatenate(expert_sums, axis=0)
    expert_sum = jnp.where(local_routed[:, None], expert_sum, 0.0)
    result = middle.astype(jnp.float32) + route_w[:, None] * expert_sum
    hidden_out = jnp.where(local_valid[:, None], result, 0.0).astype(jnp.bfloat16)[None]
    return (
        server_qkv,
        server_out,
        *flipped,
        down_late,
        hidden_out,
        cache_pair[None],
    )


def solution(mesh):
    placed = (
        P("dp", "tensor", None),
        P("dp"),
        P("dp"),
        P("dp", None, None),
        P(("tensor", "dp"), None, None),
        P(("tensor", "dp"), None),
        P("tensor", None),
        P("tensor", None),
        P("tensor", None),
        P(),
        P(),
        P(),
    )
    return jax.shard_map(
        shards,
        mesh=mesh,
        in_specs=placed,
        out_specs=(
            P(None, None, "tensor"),
            P("tensor", None),
            P(None, "tensor"),
            P(None, "tensor"),
            P(None, "tensor"),
            P("dp", "tensor", None),
            P("dp", None, None, "tensor"),
        ),
        check_vma=False,
    )
```

```python
import jax
import jax.numpy as jnp
from jax import lax
from jax.experimental import pallas as pl
from jax.experimental.layout import Layout, with_layout_constraint
from jax.experimental.pallas import tpu as pltpu
from jax.sharding import PartitionSpec as P

HEAD_DIM = 64


def swap_pairs(size, step):
    return [(i, i ^ step) for i in range(size)]


def send(block, size, step):
    return lax.ppermute(block, "tensor", swap_pairs(size, step))


def add_up(total, blocks):
    for block in blocks:
        total = total + block.astype(jnp.float32)
    return total


def split_heads(qkv, parts):
    _, rows, width = qkv.shape
    part = width // parts

    def kernel(x_ref, o_ref):
        for t in range(parts):
            for j in range(3):
                o_ref[t, j] = x_ref[j, :, t * part : (t + 1) * part].astype(jnp.bfloat16)

    return pl.pallas_call(
        kernel,
        out_shape=jax.ShapeDtypeStruct((parts, 3, rows, part), jnp.bfloat16),
        name="split_heads",
    )(qkv)


def split_rows(matrix, parts, plane, rows):
    width = matrix.shape[1]
    part = width // parts

    def kernel(p_ref, x_ref, o_ref):
        for t in range(parts):
            o_ref[t] = x_ref[:, t * part : (t + 1) * part].astype(jnp.bfloat16)

    return pl.pallas_call(
        kernel,
        out_shape=jax.ShapeDtypeStruct((parts, rows, part), jnp.bfloat16),
        grid_spec=pltpu.PrefetchScalarGridSpec(
            num_scalar_prefetch=1,
            grid=(1,),
            in_specs=[pl.BlockSpec((rows, width), lambda i, p: (p[0], 0))],
            out_specs=pl.BlockSpec((parts, rows, part), lambda i, p: (0, 0, 0)),
        ),
        compiler_params=pltpu.CompilerParams(vmem_limit_bytes=32 * 1024 * 1024),
        name="split_rows",
    )(plane.reshape(1), matrix)


def split_columns(gate, up, down_tail, parts, me):
    rows, width = gate.shape
    tail = down_tail.shape[0]
    part = width // parts
    window = min(width, (part + 127) // 128 * 128 + 128)
    chunk = 48 if rows % 48 == 0 else 16

    def kernel(me_ref, gate_ref, up_ref, tail_ref, *o_refs):
        step = pl.program_id(0)
        groups = chunk // 16

        def columns(x_ref, k):
            left = (me_ref[0] ^ k) * part
            base = jnp.minimum(lax.div(left, 128) * 128, width - window)
            cols = x_ref[:, pl.ds(pl.multiple_of(base, 128), window)]
            cols = pltpu.roll(cols, window - (left - base), 1)[:, :part]
            return cols.astype(jnp.bfloat16).reshape(-1, 16, part)

        for k in range(parts):
            o_refs[k][pl.ds(step * groups, groups)] = columns(gate_ref, k)
            o_refs[k][pl.ds(step * groups + rows // 16, groups)] = columns(up_ref, k)

        @pl.when(step == 0)
        def _():
            for k in range(parts):
                o_refs[k][rows // 8 : (2 * rows + tail) // 16] = columns(tail_ref, k)

    return pl.pallas_call(
        kernel,
        out_shape=[jax.ShapeDtypeStruct(((2 * rows + tail) // 16, 16, part), jnp.bfloat16)]
        * parts,
        grid_spec=pltpu.PrefetchScalarGridSpec(
            num_scalar_prefetch=1,
            grid=(rows // chunk,),
            in_specs=[pl.BlockSpec((chunk, width), lambda i, m: (i, 0))] * 2
            + [pl.BlockSpec((tail, width), lambda i, m: (0, 0))],
            out_specs=[
                pl.BlockSpec(((2 * rows + tail) // 16, 16, part), lambda i, m: (0, 0, 0))
            ]
            * parts,
        ),
        compiler_params=pltpu.CompilerParams(vmem_limit_bytes=40 * 1024 * 1024),
        name="split_columns",
    )(me.reshape(1), gate, up, down_tail)


def copy_rows(moves, outs_shape, sources, me, name):
    count = len(sources)
    outs = len(outs_shape)

    def kernel(me_ref, *refs):
        ins, o_refs, sem = refs[:count], refs[count : count + outs], refs[count + outs]
        copies = [
            pltpu.make_async_copy(source, o_refs[out].at[pl.ds(first, groups)], sem.at[i])
            for i, (source, out, first, groups) in enumerate(moves(me_ref[0], ins))
        ]
        for copy in copies:
            copy.start()
        for copy in copies:
            copy.wait()

    return pl.pallas_call(
        kernel,
        out_shape=[jax.ShapeDtypeStruct(shape, jnp.bfloat16) for shape in outs_shape],
        grid_spec=pltpu.PrefetchScalarGridSpec(
            num_scalar_prefetch=1,
            grid=(1,),
            in_specs=[pl.BlockSpec(memory_space=pl.ANY)] * count,
            out_specs=[pl.BlockSpec(shape, lambda i, m: (0, 0, 0)) for shape in outs_shape],
            scratch_shapes=[pltpu.SemaphoreType.DMA((160,))],
        ),
        compiler_params=pltpu.CompilerParams(vmem_limit_bytes=40 * 1024 * 1024),
        name=name,
    )(me.reshape(1), *sources)


def join_blocks(blocks, me):
    rows, width = blocks[0].shape
    groups = rows // 16

    def moves(index, ins):
        return [(ref, 0, (index ^ k) * groups, groups) for k, ref in enumerate(ins)]

    blocks = [block.reshape(groups, 16, width) for block in blocks]
    shape = (len(blocks) * groups, 16, width)
    return copy_rows(moves, [shape], blocks, me, "join_blocks")[0].reshape(-1, width)


def join_gate_up(blocks, me, rows):
    width = blocks[0].shape[2]
    groups = rows // 16

    def moves(index, ins):
        return [
            (ref.at[pl.ds(i * groups, groups)], i, (index ^ k) * groups, groups)
            for i in range(2)
            for k, ref in enumerate(ins)
        ]

    shape = (len(blocks) * groups, 16, width)
    joined = copy_rows(moves, [shape, shape], blocks, me, "join_gate_up")
    return [matrix.reshape(-1, width) for matrix in joined]


def join_down(gathered, blocks, me, rows):
    planes, count, part_rows, width = gathered.shape
    groups, part_groups = rows // 16, part_rows // 16
    rest = groups - planes * part_groups
    gathered = gathered.reshape(planes, count, part_groups, 16, width)

    def moves(index, ins):
        found = [
            (ins[0].at[p, t], 0, t * groups + p * part_groups, part_groups)
            for p in range(planes)
            for t in range(count)
        ]
        return found + [
            (
                ref.at[pl.ds(2 * groups, rest)],
                0,
                (index ^ k) * groups + planes * part_groups,
                rest,
            )
            for k, ref in enumerate(ins[1:])
        ]

    shape = (count * groups, 16, width)
    return copy_rows(moves, [shape], [gathered, *blocks], me, "join_down")[0].reshape(-1, width)


def project(mine, other, own_w, other_w, chip, rows_dev, pieces):
    total, width = mine.shape
    chips = total // rows_dev
    model = own_w.shape[1]
    rows = rows_dev // pieces

    def kernel(chip_ref, mine_ref, other_ref, own_ref, other_w_ref, *outs):
        def ordered(ref):
            places = [
                pl.multiple_of((chip_ref[0] ^ j) * rows_dev, rows_dev) for j in range(chips)
            ]
            return jnp.concatenate([ref[pl.ds(place, rows_dev), :] for place in places], axis=0)

        res = jnp.dot(ordered(mine_ref), own_ref[...], preferred_element_type=jnp.float32)
        res = res + jnp.dot(
            ordered(other_ref), other_w_ref[...], preferred_element_type=jnp.float32
        )
        for h in range(pieces):
            outs[h][...] = res[h * rows : (h + 1) * rows]
            for j in range(1, chips):
                first = j * rows_dev + h * rows
                outs[pieces + h * (chips - 1) + j - 1][...] = res[first : first + rows].astype(
                    jnp.bfloat16
                )
        outs[-1][...] = own_ref[...]

    whole = [
        pl.BlockSpec(shape, lambda i, c: (0, 0))
        for shape in (mine.shape, other.shape, own_w.shape, other_w.shape)
    ]
    sent = [(rows, model)] * (pieces * (chips - 1))
    res = pl.pallas_call(
        kernel,
        out_shape=[jax.ShapeDtypeStruct((rows, model), jnp.float32)] * pieces
        + [jax.ShapeDtypeStruct(shape, jnp.bfloat16) for shape in sent + [own_w.shape]],
        grid_spec=pltpu.PrefetchScalarGridSpec(
            num_scalar_prefetch=1,
            grid=(1,),
            in_specs=whole,
            out_specs=[
                pl.BlockSpec(shape, lambda i, c: (0, 0))
                for shape in [(rows, model)] * pieces + sent + [own_w.shape]
            ],
        ),
        compiler_params=pltpu.CompilerParams(vmem_limit_bytes=56 * 1024 * 1024),
        name="project",
    )(chip.reshape(1), mine, other, own_w, other_w)
    sent = [res[pieces + h * (chips - 1) :][: chips - 1] for h in range(pieces)]
    return res[:pieces], sent, res[-1]


def expert(mine, other, gate_w, up_w, down_w):
    rows, model = mine.shape
    units = gate_w.shape[1]
    block = min(512, 2 * rows)

    def kernel(mine_in, other_in, gate_in, up_in, down_in, mine_out, other_out, x_all, w_all, sem):
        copies = [
            pltpu.make_async_copy(source, place, sem.at[i])
            for i, (source, place) in enumerate(
                (
                    (other_in, x_all.at[pl.ds(0, rows), :]),
                    (mine_in, x_all.at[pl.ds(rows, rows), :]),
                    (gate_in, w_all.at[0]),
                    (up_in, w_all.at[1]),
                    (down_in, w_all.at[2]),
                )
            )
        ]
        for copy in copies:
            copy.start()
        copies[0].wait()
        copies[1].wait()
        for place in range(0, 2 * rows, block):
            x = x_all[place : place + block]
            if place == 0:
                copies[2].wait()
            gate = jnp.dot(x, w_all[0], preferred_element_type=jnp.float32)
            if place == 0:
                copies[3].wait()
            up = jnp.dot(x, w_all[1], preferred_element_type=jnp.float32)
            act = (gate / (1.0 + jnp.exp(-gate)) * up).astype(jnp.bfloat16)
            if place == 0:
                copies[4].wait()
            res = dot_nt(act, w_all[2]).astype(jnp.bfloat16)
            if block == 2 * rows:
                other_out[...] = res[:rows]
                mine_out[...] = res[rows:]
            elif place < rows:
                other_out[place : place + block] = res
            else:
                mine_out[place - rows : place - rows + block] = res

    return pl.pallas_call(
        kernel,
        out_shape=[jax.ShapeDtypeStruct((rows, model), jnp.bfloat16)] * 2,
        in_specs=[pl.BlockSpec(memory_space=pl.ANY)] * 5,
        out_specs=[pl.BlockSpec(memory_space=pltpu.VMEM)] * 2,
        scratch_shapes=[
            pltpu.VMEM((2 * rows, model), jnp.bfloat16),
            pltpu.VMEM((3, model, units), jnp.bfloat16),
            pltpu.SemaphoreType.DMA((5,)),
        ],
        compiler_params=pltpu.CompilerParams(vmem_limit_bytes=56 * 1024 * 1024),
        cost_estimate=pl.CostEstimate(
            flops=12 * rows * model * units,
            bytes_accessed=6 * model * units,
            transcendentals=2 * rows * units,
        ),
        name="expert",
    )(mine, other, gate_w, up_w, down_w)


def dot_nt(a, b):
    return lax.dot_general(a, b, (((1,), (1,)), ((), ())), preferred_element_type=jnp.float32)


def attention(tokens, weights, cosine, sine, scalars, rows_dev):
    seq, model = tokens.shape
    width = weights.shape[2]
    heads = width // HEAD_DIM
    block = min(256, seq)
    steps = seq // block
    half = HEAD_DIM // 2

    def kernel(s_ref, x_ref, w_ref, cos_ref, sin_ref, kv_ref, att_ref, k_all, v_all):
        step = pl.program_id(0)
        lane = lax.broadcasted_iota(jnp.int32, (block, width), 1)
        low = lax.rem(lane, HEAD_DIM) < half
        head_of = lax.div(lane, HEAD_DIM)
        x = x_ref[...]

        def rotated(j):
            m = jnp.dot(x, w_ref[j], preferred_element_type=jnp.float32)
            turned = jnp.where(
                low, -pltpu.roll(m, width - half, 1), pltpu.roll(m, half, 1)
            )
            return m * cos_ref[...] + turned * sin_ref[...]

        row = step * block + lax.broadcasted_iota(jnp.int32, (block, width), 0)
        valid = row < s_ref[0]
        start = pl.multiple_of(step * block, block)
        key = rotated(1)
        k_all[pl.ds(start, block), :] = key.astype(jnp.bfloat16)
        kv_ref[0] = jnp.where(valid, key, 0.0).astype(jnp.bfloat16)
        value = jnp.dot(x, w_ref[2], preferred_element_type=jnp.float32)
        v_all[pl.ds(start, block), :] = value.astype(jnp.bfloat16)
        kv_ref[1] = jnp.where(valid, value, 0.0).astype(jnp.bfloat16)
        query = rotated(0).astype(jnp.bfloat16).astype(jnp.float32) * HEAD_DIM ** (-0.5)

        for here in range(steps):

            @pl.when(step == here)
            def _():
                lo = here * block
                causal = lax.broadcasted_iota(
                    jnp.int32, (block, block), 0
                ) >= lax.broadcasted_iota(jnp.int32, (block, block), 1)
                out = jnp.zeros((block, width), jnp.float32)
                for h in range(heads):
                    q = jnp.where(head_of == h, query, 0.0).astype(jnp.bfloat16)
                    diag = jnp.where(causal, dot_nt(q, k_all[lo : lo + block, :]), -1e30)
                    top = jnp.max(diag, axis=-1, keepdims=True)
                    if lo:
                        past = dot_nt(q, k_all[:lo, :])
                        top = jnp.maximum(top, jnp.max(past, axis=-1, keepdims=True))
                        past = jnp.exp(past - top)
                    diag = jnp.exp(diag - top)
                    total = jnp.sum(diag, axis=-1, keepdims=True)
                    if lo:
                        total = total + jnp.sum(past, axis=-1, keepdims=True)
                    inv = 1.0 / total
                    res = jnp.dot(
                        (diag * inv).astype(jnp.bfloat16),
                        v_all[lo : lo + block, :],
                        preferred_element_type=jnp.float32,
                    )
                    if lo:
                        res = res + jnp.dot(
                            (past * inv).astype(jnp.bfloat16),
                            v_all[:lo, :],
                            preferred_element_type=jnp.float32,
                        )
                    out = jnp.where(head_of == h, res, out)
                out = out.astype(jnp.bfloat16)
                for piece in range(block // rows_dev):
                    dev = here * (block // rows_dev) + piece
                    slot = jnp.where(s_ref[1] == dev % 2, 0, 1)
                    att_ref[slot, (dev // 2) * rows_dev : (dev // 2 + 1) * rows_dev, :] = out[
                        piece * rows_dev : (piece + 1) * rows_dev
                    ]

    return pl.pallas_call(
        kernel,
        out_shape=(
            jax.ShapeDtypeStruct((2, seq, width), jnp.bfloat16),
            jax.ShapeDtypeStruct((2, seq // 2, width), jnp.bfloat16),
        ),
        grid_spec=pltpu.PrefetchScalarGridSpec(
            num_scalar_prefetch=1,
            grid=(steps,),
            in_specs=[
                pl.BlockSpec((block, model), lambda i, s: (i, 0)),
                pl.BlockSpec((3, model, width), lambda i, s: (0, 0, 0)),
                pl.BlockSpec((block, width), lambda i, s: (i, 0)),
                pl.BlockSpec((block, width), lambda i, s: (i, 0)),
            ],
            out_specs=(
                pl.BlockSpec((2, block, width), lambda i, s: (0, i, 0)),
                pl.BlockSpec((2, seq // 2, width), lambda i, s: (0, 0, 0)),
            ),
            scratch_shapes=[
                pltpu.VMEM((seq, width), jnp.bfloat16),
                pltpu.VMEM((seq, width), jnp.bfloat16),
            ],
        ),
        compiler_params=pltpu.CompilerParams(vmem_limit_bytes=48 * 1024 * 1024),
        cost_estimate=pl.CostEstimate(
            flops=6 * seq * model * width + 4 * seq * seq * width,
            bytes_accessed=2 * (seq * model + 3 * model * width),
            transcendentals=seq * seq * heads,
        ),
        name="attention",
    )(scalars, tokens, weights, cosine, sine)


def rms_scale(values, gain_row):
    mean_sq = jnp.mean(values * values, axis=-1, keepdims=True)
    return values * lax.rsqrt(mean_sq + 1e-05) * gain_row


def shards(
    hidden_in,
    prompt_len,
    start_pos,
    routes,
    trainer_qkv,
    trainer_out,
    trainer_gate,
    trainer_up,
    trainer_down,
    attn_gain,
    moe_gain,
    router,
):
    size = lax.axis_size("tensor")
    replicas = lax.axis_size("dp")
    chips = size // 2
    me = lax.axis_index("tensor").astype(jnp.int32)
    plane = lax.axis_index("dp").astype(jnp.int32)
    chip, core = me // 2, me % 2
    rows_dev, model = hidden_in.shape[1], hidden_in.shape[2]
    seq_len = rows_dev * size
    length = prompt_len[0]
    offset = start_pos[0]
    my_first = me * rows_dev

    mat_rows = trainer_down.shape[0]
    part_rows = mat_rows // (16 * replicas) * 16
    local_width = trainer_qkv.shape[2] // size
    qkv_parts = split_heads(trainer_qkv.transpose(1, 0, 2), size)
    qkv_cols = lax.all_to_all(qkv_parts, "tensor", 0, 0, tiled=True)
    parts = split_columns(
        trainer_gate, trainer_up, trainer_down[part_rows * replicas :], size, me
    )
    tokens = hidden_in[0].astype(jnp.float32)
    normed = rms_scale(tokens, attn_gain).astype(jnp.bfloat16)
    qkv_cols, normed, *parts = lax.optimization_barrier((qkv_cols, normed, *parts))
    qkv_all = lax.all_gather(qkv_cols, "dp", axis=0)
    down_parts = split_rows(trainer_down, size, plane, part_rows)
    down_cols = lax.all_to_all(down_parts, "tensor", 0, 0, tiled=True)
    same_core = [normed] + [send(normed, size, 2 * j) for j in range(1, chips)]
    other_core = send(jnp.stack(same_core), size, 1)
    blocks = []
    for j in range(chips):
        blocks += [same_core[j], other_core[j]]
    piece = join_blocks(blocks, me)

    first = [1, 2, 4][: size.bit_length() - 1]
    rest = [k for k in range(3, size) if k not in first]
    early = [send(parts[k], size, k) for k in first]
    late = list(lax.optimization_barrier((*[parts[k] for k in rest], *early)))
    early = late[len(rest) :]
    late = [send(block, size, k) for block, k in zip(late, rest)]

    half_dim = HEAD_DIM // 2
    inv_freq = jnp.power(
        10000.0, jnp.arange(half_dim, dtype=jnp.float32) * (-2.0 / HEAD_DIM)
    )
    places = offset + jnp.arange(seq_len, dtype=jnp.int32)
    angles = places.astype(jnp.float32)[:, None] * jnp.tile(inv_freq, local_width // half_dim)
    cosine, sine_part = jnp.cos(angles), jnp.sin(angles)
    server_out = lax.all_gather(trainer_out.astype(jnp.bfloat16), "dp", axis=0, tiled=True)
    qkv_all, server_out, down_cols, piece, cosine, sine_part, *early = lax.optimization_barrier(
        (qkv_all, server_out, down_cols, piece, cosine, sine_part, *early)
    )
    down_all = lax.all_gather(down_cols, "dp", axis=0)
    qkv_server = qkv_all.transpose(2, 1, 0, 3, 4).reshape(3, model, local_width)
    server_qkv = qkv_server.transpose(1, 0, 2)
    scalars = jnp.stack([length, core])
    cache_pair, attended = attention(
        piece, qkv_server, cosine, sine_part, scalars, rows_dev
    )
    half = len(late) // 2
    attended, *late[:half] = lax.optimization_barrier((attended, *late[:half]))
    pieces = 2
    rows = rows_dev // pieces
    out_other = send(server_out, size, 1)
    att_other = send(attended[1], size, 1)
    att_other, *late[half:] = lax.optimization_barrier((att_other, *late[half:]))
    own_part, partial, server_out = project(
        attended[0], att_other, server_out, out_other, chip, rows_dev, pieces
    )
    joined = [parts[0]] * size
    for block, k in zip(early + late, first + rest):
        joined[k] = block

    gate, up = join_gate_up(joined, me, mat_rows)
    down = join_down(down_all, joined, me, mat_rows)
    flipped = [gate, up]
    middles, normed_moes, moe_rows = [], [], []
    got = []
    for h in range(pieces):
        sent = partial[h]
        if h:
            sent = list(lax.optimization_barrier((*sent, *got)))[: chips - 1]
        got = [send(block, size, 2 * j + 2) for j, block in enumerate(sent)]
        if h:
            *got, down, normed_moes[0] = lax.optimization_barrier((*got, down, normed_moes[0]))
        attn_sum = add_up(own_part[h], got)
        if h:
            flipped[1], *normed_moes = lax.optimization_barrier((flipped[1], *normed_moes))
            flipped[1] = with_layout_constraint(flipped[1], Layout((1, 0)))
            *moe_rows[0], flipped[1] = lax.optimization_barrier((*moe_rows[0], flipped[1]))
        else:
            attn_sum, gate, up = lax.optimization_barrier((attn_sum, gate, up))
        middles.append((tokens[h * rows : (h + 1) * rows] + attn_sum).astype(jnp.bfloat16))
        normed = rms_scale(middles[h].astype(jnp.float32), moe_gain).astype(jnp.bfloat16)
        normed_moes.append(normed)
        if h:
            normed, *moe_rows[0] = lax.optimization_barrier((normed, *moe_rows[0]))
        moe_rows.append([normed] + [send(normed, size, 2 * j) for j in range(1, chips)])
    *moe_rows[0], gate, up, down = lax.optimization_barrier((*moe_rows[0], gate, up, down))
    middle = jnp.concatenate(middles, axis=0)
    normed_moe = jnp.concatenate(normed_moes, axis=0)

    local_routes = lax.dynamic_slice_in_dim(routes[0], my_first, rows_dev, 0)
    local_valid = my_first + jnp.arange(rows_dev, dtype=jnp.int32) < length
    logits = jnp.dot(normed_moe, router, preferred_element_type=jnp.float32)
    expert_ids = jnp.arange(router.shape[1], dtype=jnp.int32)
    logit_first = jnp.sum(
        jnp.where(local_routes[:, 0:1] == expert_ids[None, :], logits, 0.0), axis=1
    )
    logit_second = jnp.sum(
        jnp.where(local_routes[:, 1:2] == expert_ids[None, :], logits, 0.0), axis=1
    )
    other_logit = jnp.where(local_routes[:, 0] == 0, logit_second, logit_first)
    local_routed = jnp.any(local_routes == 0, axis=1)
    route_w = jnp.where(local_routed, jax.nn.sigmoid(logits[:, 0] - other_logit), 0.0)

    expert_sums, back = [], []
    for h in range(pieces):
        moe_mine = jnp.stack(moe_rows[h])
        moe_other = send(moe_mine, size, 1)
        sums_mine, sums_other = expert(
            moe_mine.reshape(-1, model), moe_other.reshape(-1, model), gate, up, down
        )
        if h:
            sums_other, *back = lax.optimization_barrier((sums_other, *back))
            expert_sums.append(add_up(total, back))
        else:
            sums_other, *moe_rows[1] = lax.optimization_barrier((sums_other, *moe_rows[1]))
        from_other = send(sums_other, size, 1)
        sums = [
            sums_mine[j * rows : (j + 1) * rows].astype(jnp.float32)
            + from_other[j * rows : (j + 1) * rows].astype(jnp.float32)
            for j in range(chips)
        ]
        total = sums[0]
        sent = [block.astype(jnp.bfloat16) for block in sums[1:]]
        back = [send(block, size, 2 * j + 2) for j, block in enumerate(sent)]
    expert_sums.append(add_up(total, back))
    down_late, gate_late, _ = lax.optimization_barrier((down, gate, sent[0]))
    expert_sum = jnp.concatenate(expert_sums, axis=0)
    expert_sum = jnp.where(local_routed[:, None], expert_sum, 0.0)
    result = middle.astype(jnp.float32) + route_w[:, None] * expert_sum
    hidden_out = jnp.where(local_valid[:, None], result, 0.0).astype(jnp.bfloat16)[None]
    return (
        server_qkv,
        server_out,
        gate_late,
        flipped[1],
        down_late,
        hidden_out,
        cache_pair[None],
    )


def solution(mesh):
    placed = (
        P("dp", "tensor", None),
        P("dp"),
        P("dp"),
        P("dp", None, None),
        P(("tensor", "dp"), None, None),
        P(("tensor", "dp"), None),
        P("tensor", None),
        P("tensor", None),
        P("tensor", None),
        P(),
        P(),
        P(),
    )
    return jax.shard_map(
        shards,
        mesh=mesh,
        in_specs=placed,
        out_specs=(
            P(None, None, "tensor"),
            P("tensor", None),
            P(None, "tensor"),
            P(None, "tensor"),
            P(None, "tensor"),
            P("dp", "tensor", None),
            P("dp", None, None, "tensor"),
        ),
        check_vma=False,
    )
```

```python
import jax
import jax.numpy as jnp
from jax import lax
from jax.experimental import pallas as pl
from jax.experimental.layout import Layout, with_layout_constraint
from jax.experimental.pallas import tpu as pltpu
from jax.sharding import PartitionSpec as P

HEAD_DIM = 64


def swap_pairs(size, step):
    return [(i, i ^ step) for i in range(size)]


def send(block, size, step):
    return lax.ppermute(block, "tensor", swap_pairs(size, step))


def add_up(total, blocks):
    for block in blocks:
        total = total + block.astype(jnp.float32)
    return total


def split_heads(qkv, parts):
    _, rows, width = qkv.shape
    part = width // parts

    def kernel(x_ref, o_ref):
        for t in range(parts):
            for j in range(3):
                o_ref[t, j] = x_ref[j, :, t * part : (t + 1) * part].astype(jnp.bfloat16)

    return pl.pallas_call(
        kernel,
        out_shape=jax.ShapeDtypeStruct((parts, 3, rows, part), jnp.bfloat16),
        name="split_heads",
    )(qkv)


def split_rows(matrix, parts, plane, rows):
    width = matrix.shape[1]
    part = width // parts

    def kernel(p_ref, x_ref, o_ref):
        for t in range(parts):
            o_ref[t] = x_ref[:, t * part : (t + 1) * part].astype(jnp.bfloat16)

    return pl.pallas_call(
        kernel,
        out_shape=jax.ShapeDtypeStruct((parts, rows, part), jnp.bfloat16),
        grid_spec=pltpu.PrefetchScalarGridSpec(
            num_scalar_prefetch=1,
            grid=(1,),
            in_specs=[pl.BlockSpec((rows, width), lambda i, p: (p[0], 0))],
            out_specs=pl.BlockSpec((parts, rows, part), lambda i, p: (0, 0, 0)),
        ),
        compiler_params=pltpu.CompilerParams(vmem_limit_bytes=32 * 1024 * 1024),
        name="split_rows",
    )(plane.reshape(1), matrix)


def split_columns(gate, up, down_tail, parts, me):
    rows, width = gate.shape
    tail = down_tail.shape[0]
    part = width // parts
    window = min(width, (part + 127) // 128 * 128 + 128)
    chunk = 48 if rows % 48 == 0 else 16

    def kernel(me_ref, gate_ref, up_ref, tail_ref, *o_refs):
        step = pl.program_id(0)
        groups = chunk // 16

        def columns(x_ref, k):
            left = (me_ref[0] ^ k) * part
            base = jnp.minimum(lax.div(left, 128) * 128, width - window)
            cols = x_ref[:, pl.ds(pl.multiple_of(base, 128), window)]
            cols = pltpu.roll(cols, window - (left - base), 1)[:, :part]
            return cols.astype(jnp.bfloat16).reshape(-1, 16, part)

        for k in range(parts):
            o_refs[k][pl.ds(step * groups, groups)] = columns(gate_ref, k)
            o_refs[k][pl.ds(step * groups + rows // 16, groups)] = columns(up_ref, k)

        @pl.when(step == 0)
        def _():
            for k in range(parts):
                o_refs[k][rows // 8 : (2 * rows + tail) // 16] = columns(tail_ref, k)

    return pl.pallas_call(
        kernel,
        out_shape=[jax.ShapeDtypeStruct(((2 * rows + tail) // 16, 16, part), jnp.bfloat16)]
        * parts,
        grid_spec=pltpu.PrefetchScalarGridSpec(
            num_scalar_prefetch=1,
            grid=(rows // chunk,),
            in_specs=[pl.BlockSpec((chunk, width), lambda i, m: (i, 0))] * 2
            + [pl.BlockSpec((tail, width), lambda i, m: (0, 0))],
            out_specs=[
                pl.BlockSpec(((2 * rows + tail) // 16, 16, part), lambda i, m: (0, 0, 0))
            ]
            * parts,
        ),
        compiler_params=pltpu.CompilerParams(vmem_limit_bytes=40 * 1024 * 1024),
        name="split_columns",
    )(me.reshape(1), gate, up, down_tail)


def copy_rows(moves, outs_shape, sources, me, name):
    count = len(sources)
    outs = len(outs_shape)

    def kernel(me_ref, *refs):
        ins, o_refs, sem = refs[:count], refs[count : count + outs], refs[count + outs]
        copies = [
            pltpu.make_async_copy(source, o_refs[out].at[pl.ds(first, groups)], sem.at[i])
            for i, (source, out, first, groups) in enumerate(moves(me_ref[0], ins))
        ]
        for copy in copies:
            copy.start()
        for copy in copies:
            copy.wait()

    return pl.pallas_call(
        kernel,
        out_shape=[jax.ShapeDtypeStruct(shape, jnp.bfloat16) for shape in outs_shape],
        grid_spec=pltpu.PrefetchScalarGridSpec(
            num_scalar_prefetch=1,
            grid=(1,),
            in_specs=[pl.BlockSpec(memory_space=pl.ANY)] * count,
            out_specs=[pl.BlockSpec(shape, lambda i, m: (0, 0, 0)) for shape in outs_shape],
            scratch_shapes=[pltpu.SemaphoreType.DMA((160,))],
        ),
        compiler_params=pltpu.CompilerParams(vmem_limit_bytes=40 * 1024 * 1024),
        name=name,
    )(me.reshape(1), *sources)


def join_blocks(blocks, me):
    rows, width = blocks[0].shape
    groups = rows // 16

    def moves(index, ins):
        return [(ref, 0, (index ^ k) * groups, groups) for k, ref in enumerate(ins)]

    blocks = [block.reshape(groups, 16, width) for block in blocks]
    shape = (len(blocks) * groups, 16, width)
    return copy_rows(moves, [shape], blocks, me, "join_blocks")[0].reshape(-1, width)


def join_gate_up(blocks, me, rows):
    width = blocks[0].shape[2]
    groups = rows // 16

    def moves(index, ins):
        return [
            (ref.at[pl.ds(i * groups, groups)], i, (index ^ k) * groups, groups)
            for i in range(2)
            for k, ref in enumerate(ins)
        ]

    shape = (len(blocks) * groups, 16, width)
    joined = copy_rows(moves, [shape, shape], blocks, me, "join_gate_up")
    return [matrix.reshape(-1, width) for matrix in joined]


def join_down(gathered, blocks, me, rows):
    planes, count, part_rows, width = gathered.shape
    groups, part_groups = rows // 16, part_rows // 16
    rest = groups - planes * part_groups
    gathered = gathered.reshape(planes, count, part_groups, 16, width)

    def moves(index, ins):
        found = [
            (ins[0].at[p, t], 0, t * groups + p * part_groups, part_groups)
            for p in range(planes)
            for t in range(count)
        ]
        return found + [
            (
                ref.at[pl.ds(2 * groups, rest)],
                0,
                (index ^ k) * groups + planes * part_groups,
                rest,
            )
            for k, ref in enumerate(ins[1:])
        ]

    shape = (count * groups, 16, width)
    return copy_rows(moves, [shape], [gathered, *blocks], me, "join_down")[0].reshape(-1, width)


def project(mine, other, own_w, other_w, chip, rows_dev, pieces):
    total, width = mine.shape
    chips = total // rows_dev
    model = own_w.shape[1]
    rows = rows_dev // pieces

    def kernel(chip_ref, mine_ref, other_ref, own_ref, other_w_ref, *outs):
        def ordered(ref):
            places = [
                pl.multiple_of((chip_ref[0] ^ j) * rows_dev, rows_dev) for j in range(chips)
            ]
            return jnp.concatenate([ref[pl.ds(place, rows_dev), :] for place in places], axis=0)

        res = jnp.dot(ordered(mine_ref), own_ref[...], preferred_element_type=jnp.float32)
        res = res + jnp.dot(
            ordered(other_ref), other_w_ref[...], preferred_element_type=jnp.float32
        )
        for h in range(pieces):
            outs[h][...] = res[h * rows : (h + 1) * rows]
            for j in range(1, chips):
                first = j * rows_dev + h * rows
                outs[pieces + h * (chips - 1) + j - 1][...] = res[first : first + rows].astype(
                    jnp.bfloat16
                )
        outs[-1][...] = own_ref[...]

    whole = [
        pl.BlockSpec(shape, lambda i, c: (0, 0))
        for shape in (mine.shape, other.shape, own_w.shape, other_w.shape)
    ]
    sent = [(rows, model)] * (pieces * (chips - 1))
    res = pl.pallas_call(
        kernel,
        out_shape=[jax.ShapeDtypeStruct((rows, model), jnp.float32)] * pieces
        + [jax.ShapeDtypeStruct(shape, jnp.bfloat16) for shape in sent + [own_w.shape]],
        grid_spec=pltpu.PrefetchScalarGridSpec(
            num_scalar_prefetch=1,
            grid=(1,),
            in_specs=whole,
            out_specs=[
                pl.BlockSpec(shape, lambda i, c: (0, 0))
                for shape in [(rows, model)] * pieces + sent + [own_w.shape]
            ],
        ),
        compiler_params=pltpu.CompilerParams(vmem_limit_bytes=56 * 1024 * 1024),
        name="project",
    )(chip.reshape(1), mine, other, own_w, other_w)
    sent = [res[pieces + h * (chips - 1) :][: chips - 1] for h in range(pieces)]
    return res[:pieces], sent, res[-1]


def expert(mine, other, gate_w, up_w, down_w):
    rows, model = mine.shape
    units = gate_w.shape[1]
    block = min(512, 2 * rows)

    def kernel(mine_in, other_in, gate_in, up_in, down_in, mine_out, other_out, x_all, w_all, sem):
        copies = [
            pltpu.make_async_copy(source, place, sem.at[i])
            for i, (source, place) in enumerate(
                (
                    (other_in, x_all.at[pl.ds(0, rows), :]),
                    (mine_in, x_all.at[pl.ds(rows, rows), :]),
                    (gate_in, w_all.at[0]),
                    (up_in, w_all.at[1]),
                    (down_in, w_all.at[2]),
                )
            )
        ]
        for copy in copies:
            copy.start()
        copies[0].wait()
        copies[1].wait()
        for place in range(0, 2 * rows, block):
            x = x_all[place : place + block]
            if place == 0:
                copies[2].wait()
            gate = jnp.dot(x, w_all[0], preferred_element_type=jnp.float32)
            if place == 0:
                copies[3].wait()
            up = jnp.dot(x, w_all[1], preferred_element_type=jnp.float32)
            act = (gate / (1.0 + jnp.exp(-gate)) * up).astype(jnp.bfloat16)
            if place == 0:
                copies[4].wait()
            res = dot_nt(act, w_all[2]).astype(jnp.bfloat16)
            if block == 2 * rows:
                other_out[...] = res[:rows]
                mine_out[...] = res[rows:]
            elif place < rows:
                other_out[place : place + block] = res
            else:
                mine_out[place - rows : place - rows + block] = res

    return pl.pallas_call(
        kernel,
        out_shape=[jax.ShapeDtypeStruct((rows, model), jnp.bfloat16)] * 2,
        in_specs=[pl.BlockSpec(memory_space=pl.ANY)] * 5,
        out_specs=[pl.BlockSpec(memory_space=pltpu.VMEM)] * 2,
        scratch_shapes=[
            pltpu.VMEM((2 * rows, model), jnp.bfloat16),
            pltpu.VMEM((3, model, units), jnp.bfloat16),
            pltpu.SemaphoreType.DMA((5,)),
        ],
        compiler_params=pltpu.CompilerParams(vmem_limit_bytes=56 * 1024 * 1024),
        cost_estimate=pl.CostEstimate(
            flops=12 * rows * model * units,
            bytes_accessed=6 * model * units,
            transcendentals=2 * rows * units,
        ),
        name="expert",
    )(mine, other, gate_w, up_w, down_w)


def dot_nt(a, b):
    return lax.dot_general(a, b, (((1,), (1,)), ((), ())), preferred_element_type=jnp.float32)


def attention(tokens, weights, cosine, sine, scalars, rows_dev):
    seq, model = tokens.shape
    width = weights.shape[2]
    heads = width // HEAD_DIM
    block = min(256, seq)
    steps = seq // block
    half = HEAD_DIM // 2

    def kernel(s_ref, x_ref, w_ref, cos_ref, sin_ref, kv_ref, att_ref, k_all, v_all):
        step = pl.program_id(0)
        lane = lax.broadcasted_iota(jnp.int32, (block, width), 1)
        low = lax.rem(lane, HEAD_DIM) < half
        head_of = lax.div(lane, HEAD_DIM)
        x = x_ref[...]

        def rotated(j):
            m = jnp.dot(x, w_ref[j], preferred_element_type=jnp.float32)
            turned = jnp.where(
                low, -pltpu.roll(m, width - half, 1), pltpu.roll(m, half, 1)
            )
            return m * cos_ref[...] + turned * sin_ref[...]

        row = step * block + lax.broadcasted_iota(jnp.int32, (block, width), 0)
        valid = row < s_ref[0]
        start = pl.multiple_of(step * block, block)
        key = rotated(1)
        k_all[pl.ds(start, block), :] = key.astype(jnp.bfloat16)
        kv_ref[0] = jnp.where(valid, key, 0.0).astype(jnp.bfloat16)
        value = jnp.dot(x, w_ref[2], preferred_element_type=jnp.float32)
        v_all[pl.ds(start, block), :] = value.astype(jnp.bfloat16)
        kv_ref[1] = jnp.where(valid, value, 0.0).astype(jnp.bfloat16)
        query = rotated(0).astype(jnp.bfloat16).astype(jnp.float32) * HEAD_DIM ** (-0.5)

        for here in range(steps):

            @pl.when(step == here)
            def _():
                lo = here * block
                causal = lax.broadcasted_iota(
                    jnp.int32, (block, block), 0
                ) >= lax.broadcasted_iota(jnp.int32, (block, block), 1)
                out = jnp.zeros((block, width), jnp.float32)
                for h in range(heads):
                    q = jnp.where(head_of == h, query, 0.0).astype(jnp.bfloat16)
                    diag = jnp.where(causal, dot_nt(q, k_all[lo : lo + block, :]), -1e30)
                    top = jnp.max(diag, axis=-1, keepdims=True)
                    if lo:
                        past = dot_nt(q, k_all[:lo, :])
                        top = jnp.maximum(top, jnp.max(past, axis=-1, keepdims=True))
                        past = jnp.exp(past - top)
                    diag = jnp.exp(diag - top)
                    total = jnp.sum(diag, axis=-1, keepdims=True)
                    if lo:
                        total = total + jnp.sum(past, axis=-1, keepdims=True)
                    inv = 1.0 / total
                    res = jnp.dot(
                        (diag * inv).astype(jnp.bfloat16),
                        v_all[lo : lo + block, :],
                        preferred_element_type=jnp.float32,
                    )
                    if lo:
                        res = res + jnp.dot(
                            (past * inv).astype(jnp.bfloat16),
                            v_all[:lo, :],
                            preferred_element_type=jnp.float32,
                        )
                    out = jnp.where(head_of == h, res, out)
                out = out.astype(jnp.bfloat16)
                for piece in range(block // rows_dev):
                    dev = here * (block // rows_dev) + piece
                    slot = jnp.where(s_ref[1] == dev % 2, 0, 1)
                    att_ref[slot, (dev // 2) * rows_dev : (dev // 2 + 1) * rows_dev, :] = out[
                        piece * rows_dev : (piece + 1) * rows_dev
                    ]

    return pl.pallas_call(
        kernel,
        out_shape=(
            jax.ShapeDtypeStruct((2, seq, width), jnp.bfloat16),
            jax.ShapeDtypeStruct((2, seq // 2, width), jnp.bfloat16),
        ),
        grid_spec=pltpu.PrefetchScalarGridSpec(
            num_scalar_prefetch=1,
            grid=(steps,),
            in_specs=[
                pl.BlockSpec((block, model), lambda i, s: (i, 0)),
                pl.BlockSpec((3, model, width), lambda i, s: (0, 0, 0)),
                pl.BlockSpec((block, width), lambda i, s: (i, 0)),
                pl.BlockSpec((block, width), lambda i, s: (i, 0)),
            ],
            out_specs=(
                pl.BlockSpec((2, block, width), lambda i, s: (0, i, 0)),
                pl.BlockSpec((2, seq // 2, width), lambda i, s: (0, 0, 0)),
            ),
            scratch_shapes=[
                pltpu.VMEM((seq, width), jnp.bfloat16),
                pltpu.VMEM((seq, width), jnp.bfloat16),
            ],
        ),
        compiler_params=pltpu.CompilerParams(vmem_limit_bytes=48 * 1024 * 1024),
        cost_estimate=pl.CostEstimate(
            flops=6 * seq * model * width + 4 * seq * seq * width,
            bytes_accessed=2 * (seq * model + 3 * model * width),
            transcendentals=seq * seq * heads,
        ),
        name="attention",
    )(scalars, tokens, weights, cosine, sine)


def rms_scale(values, gain_row):
    mean_sq = jnp.mean(values * values, axis=-1, keepdims=True)
    return values * lax.rsqrt(mean_sq + 1e-05) * gain_row


def shards(
    hidden_in,
    prompt_len,
    start_pos,
    routes,
    trainer_qkv,
    trainer_out,
    trainer_gate,
    trainer_up,
    trainer_down,
    attn_gain,
    moe_gain,
    router,
):
    size = lax.axis_size("tensor")
    replicas = lax.axis_size("dp")
    chips = size // 2
    me = lax.axis_index("tensor").astype(jnp.int32)
    plane = lax.axis_index("dp").astype(jnp.int32)
    chip, core = me // 2, me % 2
    rows_dev, model = hidden_in.shape[1], hidden_in.shape[2]
    seq_len = rows_dev * size
    length = prompt_len[0]
    offset = start_pos[0]
    my_first = me * rows_dev

    mat_rows = trainer_down.shape[0]
    part_rows = mat_rows // (16 * replicas) * 16
    local_width = trainer_qkv.shape[2] // size
    qkv_parts = split_heads(trainer_qkv.transpose(1, 0, 2), size)
    qkv_cols = lax.all_to_all(qkv_parts, "tensor", 0, 0, tiled=True)
    parts = split_columns(
        trainer_gate, trainer_up, trainer_down[part_rows * replicas :], size, me
    )
    tokens = hidden_in[0].astype(jnp.float32)
    normed = rms_scale(tokens, attn_gain).astype(jnp.bfloat16)
    qkv_cols, normed, *parts = lax.optimization_barrier((qkv_cols, normed, *parts))
    qkv_all = lax.all_gather(qkv_cols, "dp", axis=0)
    down_parts = split_rows(trainer_down, size, plane, part_rows)
    down_cols = lax.all_to_all(down_parts, "tensor", 0, 0, tiled=True)
    same_core = [normed] + [send(normed, size, 2 * j) for j in range(1, chips)]
    other_core = send(jnp.stack(same_core), size, 1)
    blocks = []
    for j in range(chips):
        blocks += [same_core[j], other_core[j]]
    piece = join_blocks(blocks, me)

    first = [1, 2, 4][: size.bit_length() - 1]
    rest = [k for k in range(3, size) if k not in first]
    rest = sorted(rest, key=lambda k: k % 2)
    early = [send(parts[k], size, k) for k in first]
    after = list(lax.optimization_barrier((*[parts[k] for k in rest], *early)))
    early = after[len(rest) :] + [send(after[0], size, rest[0])]
    late = list(lax.optimization_barrier((*after[1 : len(rest)], *early)))
    early = late[len(rest) - 1 :]
    late = [send(block, size, k) for block, k in zip(late, rest[1:])]

    half_dim = HEAD_DIM // 2
    inv_freq = jnp.power(
        10000.0, jnp.arange(half_dim, dtype=jnp.float32) * (-2.0 / HEAD_DIM)
    )
    places = offset + jnp.arange(seq_len, dtype=jnp.int32)
    angles = places.astype(jnp.float32)[:, None] * jnp.tile(inv_freq, local_width // half_dim)
    cosine, sine_part = jnp.cos(angles), jnp.sin(angles)
    server_out = lax.all_gather(trainer_out.astype(jnp.bfloat16), "dp", axis=0, tiled=True)
    qkv_all, server_out, down_cols, piece, cosine, sine_part, *early = lax.optimization_barrier(
        (qkv_all, server_out, down_cols, piece, cosine, sine_part, *early)
    )
    down_all = lax.all_gather(down_cols, "dp", axis=0)
    qkv_server = qkv_all.transpose(2, 1, 0, 3, 4).reshape(3, model, local_width)
    server_qkv = qkv_server.transpose(1, 0, 2)
    scalars = jnp.stack([length, core])
    cache_pair, attended = attention(
        piece, qkv_server, cosine, sine_part, scalars, rows_dev
    )
    half = len(late) // 2
    attended, *late[:half] = lax.optimization_barrier((attended, *late[:half]))
    pieces = 2
    rows = rows_dev // pieces
    out_other = send(server_out, size, 1)
    att_other = send(attended[1], size, 1)
    att_other, *late[half:] = lax.optimization_barrier((att_other, *late[half:]))
    own_part, partial, server_out = project(
        attended[0], att_other, server_out, out_other, chip, rows_dev, pieces
    )
    joined = [parts[0]] * size
    for block, k in zip(early + late, first + rest):
        joined[k] = block

    gate, up = join_gate_up(joined, me, mat_rows)
    down = join_down(down_all, joined, me, mat_rows)
    flipped = [gate, up]
    middles, normed_moes, moe_rows = [], [], []
    got = []
    for h in range(pieces):
        sent = partial[h]
        if h:
            sent = list(lax.optimization_barrier((*sent, *got)))[: chips - 1]
        got = [send(block, size, 2 * j + 2) for j, block in enumerate(sent)]
        if h:
            *got, down, normed_moes[0] = lax.optimization_barrier((*got, down, normed_moes[0]))
        attn_sum = add_up(own_part[h], got)
        if h:
            flipped[1], *normed_moes = lax.optimization_barrier((flipped[1], *normed_moes))
            flipped[1] = with_layout_constraint(flipped[1], Layout((1, 0)))
            *moe_rows[0], flipped[1] = lax.optimization_barrier((*moe_rows[0], flipped[1]))
        else:
            attn_sum, gate, up = lax.optimization_barrier((attn_sum, gate, up))
        middles.append((tokens[h * rows : (h + 1) * rows] + attn_sum).astype(jnp.bfloat16))
        normed = rms_scale(middles[h].astype(jnp.float32), moe_gain).astype(jnp.bfloat16)
        normed_moes.append(normed)
        if h:
            normed, *moe_rows[0] = lax.optimization_barrier((normed, *moe_rows[0]))
        moe_rows.append([normed] + [send(normed, size, 2 * j) for j in range(1, chips)])
    *moe_rows[0], gate, up, down = lax.optimization_barrier((*moe_rows[0], gate, up, down))
    middle = jnp.concatenate(middles, axis=0)
    normed_moe = jnp.concatenate(normed_moes, axis=0)

    local_routes = lax.dynamic_slice_in_dim(routes[0], my_first, rows_dev, 0)
    local_valid = my_first + jnp.arange(rows_dev, dtype=jnp.int32) < length
    logits = jnp.dot(normed_moe, router, preferred_element_type=jnp.float32)
    expert_ids = jnp.arange(router.shape[1], dtype=jnp.int32)
    logit_first = jnp.sum(
        jnp.where(local_routes[:, 0:1] == expert_ids[None, :], logits, 0.0), axis=1
    )
    logit_second = jnp.sum(
        jnp.where(local_routes[:, 1:2] == expert_ids[None, :], logits, 0.0), axis=1
    )
    other_logit = jnp.where(local_routes[:, 0] == 0, logit_second, logit_first)
    local_routed = jnp.any(local_routes == 0, axis=1)
    route_w = jnp.where(local_routed, jax.nn.sigmoid(logits[:, 0] - other_logit), 0.0)

    expert_sums, back = [], []
    for h in range(pieces):
        moe_mine = jnp.stack(moe_rows[h])
        moe_other = send(moe_mine, size, 1)
        sums_mine, sums_other = expert(
            moe_mine.reshape(-1, model), moe_other.reshape(-1, model), gate, up, down
        )
        if h:
            sums_other, *back = lax.optimization_barrier((sums_other, *back))
            expert_sums.append(add_up(total, back))
        else:
            sums_other, *moe_rows[1] = lax.optimization_barrier((sums_other, *moe_rows[1]))
        from_other = send(sums_other, size, 1)
        sums = [
            sums_mine[j * rows : (j + 1) * rows].astype(jnp.float32)
            + from_other[j * rows : (j + 1) * rows].astype(jnp.float32)
            for j in range(chips)
        ]
        total = sums[0]
        sent = [block.astype(jnp.bfloat16) for block in sums[1:]]
        back = [send(block, size, 2 * j + 2) for j, block in enumerate(sent)]
    expert_sums.append(add_up(total, back))
    down_late, gate_late, _ = lax.optimization_barrier((down, gate, sent[0]))
    expert_sum = jnp.concatenate(expert_sums, axis=0)
    expert_sum = jnp.where(local_routed[:, None], expert_sum, 0.0)
    result = middle.astype(jnp.float32) + route_w[:, None] * expert_sum
    hidden_out = jnp.where(local_valid[:, None], result, 0.0).astype(jnp.bfloat16)[None]
    return (
        server_qkv,
        server_out,
        gate_late,
        flipped[1],
        down_late,
        hidden_out,
        cache_pair[None],
    )


def solution(mesh):
    placed = (
        P("dp", "tensor", None),
        P("dp"),
        P("dp"),
        P("dp", None, None),
        P(("tensor", "dp"), None, None),
        P(("tensor", "dp"), None),
        P("tensor", None),
        P("tensor", None),
        P("tensor", None),
        P(),
        P(),
        P(),
    )
    return jax.shard_map(
        shards,
        mesh=mesh,
        in_specs=placed,
        out_specs=(
            P(None, None, "tensor"),
            P("tensor", None),
            P(None, "tensor"),
            P(None, "tensor"),
            P(None, "tensor"),
            P("dp", "tensor", None),
            P("dp", None, None, "tensor"),
        ),
        check_vma=False,
    )
```

```python
import jax
import jax.numpy as jnp
from jax import lax
from jax.experimental import pallas as pl
from jax.experimental.layout import Layout, with_layout_constraint
from jax.experimental.pallas import tpu as pltpu
from jax.sharding import PartitionSpec as P

HEAD_DIM = 64


def swap_pairs(size, step):
    return [(i, i ^ step) for i in range(size)]


def send(block, size, step):
    return lax.ppermute(block, "tensor", swap_pairs(size, step))


def add_up(total, blocks):
    for block in blocks:
        total = total + block.astype(jnp.float32)
    return total


def split_heads(qkv, parts):
    _, rows, width = qkv.shape
    part = width // parts

    def kernel(x_ref, o_ref):
        for t in range(parts):
            for j in range(3):
                o_ref[t, j] = x_ref[j, :, t * part : (t + 1) * part].astype(jnp.bfloat16)

    return pl.pallas_call(
        kernel,
        out_shape=jax.ShapeDtypeStruct((parts, 3, rows, part), jnp.bfloat16),
        name="split_heads",
    )(qkv)


def split_rows(matrix, parts, plane, rows):
    width = matrix.shape[1]
    part = width // parts

    def kernel(p_ref, x_ref, o_ref):
        for t in range(parts):
            o_ref[t] = x_ref[:, t * part : (t + 1) * part].astype(jnp.bfloat16)

    return pl.pallas_call(
        kernel,
        out_shape=jax.ShapeDtypeStruct((parts, rows, part), jnp.bfloat16),
        grid_spec=pltpu.PrefetchScalarGridSpec(
            num_scalar_prefetch=1,
            grid=(1,),
            in_specs=[pl.BlockSpec((rows, width), lambda i, p: (p[0], 0))],
            out_specs=pl.BlockSpec((parts, rows, part), lambda i, p: (0, 0, 0)),
        ),
        compiler_params=pltpu.CompilerParams(vmem_limit_bytes=32 * 1024 * 1024),
        name="split_rows",
    )(plane.reshape(1), matrix)


def split_columns(gate, up, down_tail, parts, me):
    rows, width = gate.shape
    tail = down_tail.shape[0]
    part = width // parts
    window = min(width, (part + 127) // 128 * 128 + 128)
    chunk = 48 if rows % 48 == 0 else 16

    def kernel(me_ref, gate_ref, up_ref, tail_ref, *o_refs):
        step = pl.program_id(0)
        groups = chunk // 16

        def columns(x_ref, k):
            left = (me_ref[0] ^ k) * part
            base = jnp.minimum(lax.div(left, 128) * 128, width - window)
            cols = x_ref[:, pl.ds(pl.multiple_of(base, 128), window)]
            cols = pltpu.roll(cols, window - (left - base), 1)[:, :part]
            return cols.astype(jnp.bfloat16).reshape(-1, 16, part)

        for k in range(parts):
            o_refs[k][pl.ds(step * groups, groups)] = columns(gate_ref, k)
            o_refs[k][pl.ds(step * groups + rows // 16, groups)] = columns(up_ref, k)

        @pl.when(step == 0)
        def _():
            for k in range(parts):
                o_refs[k][rows // 8 : (2 * rows + tail) // 16] = columns(tail_ref, k)

    return pl.pallas_call(
        kernel,
        out_shape=[pltpu.HBM(((2 * rows + tail) // 16, 16, part), jnp.bfloat16)] * parts,
        grid_spec=pltpu.PrefetchScalarGridSpec(
            num_scalar_prefetch=1,
            grid=(rows // chunk,),
            in_specs=[pl.BlockSpec((chunk, width), lambda i, m: (i, 0))] * 2
            + [pl.BlockSpec((tail, width), lambda i, m: (0, 0))],
            out_specs=[
                pl.BlockSpec(((2 * rows + tail) // 16, 16, part), lambda i, m: (0, 0, 0))
            ]
            * parts,
        ),
        compiler_params=pltpu.CompilerParams(vmem_limit_bytes=40 * 1024 * 1024),
        name="split_columns",
    )(me.reshape(1), gate, up, down_tail)


def copy_rows(moves, outs_shape, sources, me, name):
    count = len(sources)
    outs = len(outs_shape)

    def kernel(me_ref, *refs):
        ins, o_refs, sem = refs[:count], refs[count : count + outs], refs[count + outs]
        copies = [
            pltpu.make_async_copy(source, o_refs[out].at[pl.ds(first, groups)], sem.at[i])
            for i, (source, out, first, groups) in enumerate(moves(me_ref[0], ins))
        ]
        for copy in copies:
            copy.start()
        for copy in copies:
            copy.wait()

    return pl.pallas_call(
        kernel,
        out_shape=[pltpu.HBM(shape, jnp.bfloat16) for shape in outs_shape],
        grid_spec=pltpu.PrefetchScalarGridSpec(
            num_scalar_prefetch=1,
            grid=(1,),
            in_specs=[pl.BlockSpec(memory_space=pl.ANY)] * count,
            out_specs=[pl.BlockSpec(shape, lambda i, m: (0, 0, 0)) for shape in outs_shape],
            scratch_shapes=[pltpu.SemaphoreType.DMA((160,))],
        ),
        compiler_params=pltpu.CompilerParams(vmem_limit_bytes=40 * 1024 * 1024),
        name=name,
    )(me.reshape(1), *sources)


def join_blocks(blocks, me):
    rows, width = blocks[0].shape
    groups = rows // 16

    def moves(index, ins):
        return [(ref, 0, (index ^ k) * groups, groups) for k, ref in enumerate(ins)]

    blocks = [block.reshape(groups, 16, width) for block in blocks]
    shape = (len(blocks) * groups, 16, width)
    return copy_rows(moves, [shape], blocks, me, "join_blocks")[0].reshape(-1, width)


def join_gate_up(blocks, me, rows):
    width = blocks[0].shape[2]
    groups = rows // 16

    def moves(index, ins):
        return [
            (ref.at[pl.ds(i * groups, groups)], i, (index ^ k) * groups, groups)
            for i in range(2)
            for k, ref in enumerate(ins)
        ]

    shape = (len(blocks) * groups, 16, width)
    joined = copy_rows(moves, [shape, shape], blocks, me, "join_gate_up")
    return [matrix.reshape(-1, width) for matrix in joined]


def join_down(gathered, blocks, me, rows):
    planes, count, part_rows, width = gathered.shape
    groups, part_groups = rows // 16, part_rows // 16
    rest = groups - planes * part_groups
    gathered = gathered.reshape(planes, count, part_groups, 16, width)

    def moves(index, ins):
        found = [
            (ins[0].at[p, t], 0, t * groups + p * part_groups, part_groups)
            for p in range(planes)
            for t in range(count)
        ]
        return found + [
            (
                ref.at[pl.ds(2 * groups, rest)],
                0,
                (index ^ k) * groups + planes * part_groups,
                rest,
            )
            for k, ref in enumerate(ins[1:])
        ]

    shape = (count * groups, 16, width)
    return copy_rows(moves, [shape], [gathered, *blocks], me, "join_down")[0].reshape(-1, width)


def project(mine, other, own_w, other_w, chip, rows_dev, pieces):
    total, width = mine.shape
    chips = total // rows_dev
    model = own_w.shape[1]
    rows = rows_dev // pieces

    def kernel(chip_ref, mine_ref, other_ref, own_ref, other_w_ref, *outs):
        def ordered(ref):
            places = [
                pl.multiple_of((chip_ref[0] ^ j) * rows_dev, rows_dev) for j in range(chips)
            ]
            return jnp.concatenate([ref[pl.ds(place, rows_dev), :] for place in places], axis=0)

        res = jnp.dot(ordered(mine_ref), own_ref[...], preferred_element_type=jnp.float32)
        res = res + jnp.dot(
            ordered(other_ref), other_w_ref[...], preferred_element_type=jnp.float32
        )
        for h in range(pieces):
            outs[h][...] = res[h * rows : (h + 1) * rows]
            for j in range(1, chips):
                first = j * rows_dev + h * rows
                outs[pieces + h * (chips - 1) + j - 1][...] = res[first : first + rows].astype(
                    jnp.bfloat16
                )
        outs[-1][...] = own_ref[...]

    whole = [
        pl.BlockSpec(shape, lambda i, c: (0, 0))
        for shape in (mine.shape, other.shape, own_w.shape, other_w.shape)
    ]
    sent = [(rows, model)] * (pieces * (chips - 1))
    res = pl.pallas_call(
        kernel,
        out_shape=[jax.ShapeDtypeStruct((rows, model), jnp.float32)] * pieces
        + [jax.ShapeDtypeStruct(shape, jnp.bfloat16) for shape in sent + [own_w.shape]],
        grid_spec=pltpu.PrefetchScalarGridSpec(
            num_scalar_prefetch=1,
            grid=(1,),
            in_specs=whole,
            out_specs=[
                pl.BlockSpec(shape, lambda i, c: (0, 0))
                for shape in [(rows, model)] * pieces + sent + [own_w.shape]
            ],
        ),
        compiler_params=pltpu.CompilerParams(vmem_limit_bytes=56 * 1024 * 1024),
        name="project",
    )(chip.reshape(1), mine, other, own_w, other_w)
    sent = [res[pieces + h * (chips - 1) :][: chips - 1] for h in range(pieces)]
    return res[:pieces], sent, res[-1]


def expert(mine, other, gate_w, up_w, down_w):
    rows, model = mine.shape
    units = gate_w.shape[1]
    block = min(512, 2 * rows)

    def kernel(mine_in, other_in, gate_in, up_in, down_in, mine_out, other_out, x_all, w_all, sem):
        copies = [
            pltpu.make_async_copy(source, place, sem.at[i])
            for i, (source, place) in enumerate(
                (
                    (other_in, x_all.at[pl.ds(0, rows), :]),
                    (mine_in, x_all.at[pl.ds(rows, rows), :]),
                    (gate_in, w_all.at[0]),
                    (up_in, w_all.at[1]),
                    (down_in, w_all.at[2]),
                )
            )
        ]
        for copy in copies:
            copy.start()
        copies[0].wait()
        copies[1].wait()
        for place in range(0, 2 * rows, block):
            x = x_all[place : place + block]
            if place == 0:
                copies[2].wait()
            gate = jnp.dot(x, w_all[0], preferred_element_type=jnp.float32)
            if place == 0:
                copies[3].wait()
            up = jnp.dot(x, w_all[1], preferred_element_type=jnp.float32)
            act = (gate / (1.0 + jnp.exp(-gate)) * up).astype(jnp.bfloat16)
            if place == 0:
                copies[4].wait()
            res = dot_nt(act, w_all[2]).astype(jnp.bfloat16)
            if block == 2 * rows:
                other_out[...] = res[:rows]
                mine_out[...] = res[rows:]
            elif place < rows:
                other_out[place : place + block] = res
            else:
                mine_out[place - rows : place - rows + block] = res

    return pl.pallas_call(
        kernel,
        out_shape=[jax.ShapeDtypeStruct((rows, model), jnp.bfloat16)] * 2,
        in_specs=[pl.BlockSpec(memory_space=pl.ANY)] * 5,
        out_specs=[pl.BlockSpec(memory_space=pltpu.VMEM)] * 2,
        scratch_shapes=[
            pltpu.VMEM((2 * rows, model), jnp.bfloat16),
            pltpu.VMEM((3, model, units), jnp.bfloat16),
            pltpu.SemaphoreType.DMA((5,)),
        ],
        compiler_params=pltpu.CompilerParams(vmem_limit_bytes=56 * 1024 * 1024),
        cost_estimate=pl.CostEstimate(
            flops=12 * rows * model * units,
            bytes_accessed=6 * model * units,
            transcendentals=2 * rows * units,
        ),
        name="expert",
    )(mine, other, gate_w, up_w, down_w)


def dot_nt(a, b):
    return lax.dot_general(a, b, (((1,), (1,)), ((), ())), preferred_element_type=jnp.float32)


def attention(tokens, weights, cosine, sine, scalars, rows_dev):
    seq, model = tokens.shape
    width = weights.shape[2]
    heads = width // HEAD_DIM
    block = min(256, seq)
    steps = seq // block
    half = HEAD_DIM // 2

    def kernel(s_ref, x_ref, w_ref, cos_ref, sin_ref, kv_ref, att_ref, k_all, v_all):
        step = pl.program_id(0)
        lane = lax.broadcasted_iota(jnp.int32, (block, width), 1)
        low = lax.rem(lane, HEAD_DIM) < half
        head_of = lax.div(lane, HEAD_DIM)
        x = x_ref[...]

        def rotated(j):
            m = jnp.dot(x, w_ref[j], preferred_element_type=jnp.float32)
            turned = jnp.where(
                low, -pltpu.roll(m, width - half, 1), pltpu.roll(m, half, 1)
            )
            return m * cos_ref[...] + turned * sin_ref[...]

        row = step * block + lax.broadcasted_iota(jnp.int32, (block, width), 0)
        valid = row < s_ref[0]
        start = pl.multiple_of(step * block, block)
        key = rotated(1)
        k_all[pl.ds(start, block), :] = key.astype(jnp.bfloat16)
        kv_ref[0] = jnp.where(valid, key, 0.0).astype(jnp.bfloat16)
        value = jnp.dot(x, w_ref[2], preferred_element_type=jnp.float32)
        v_all[pl.ds(start, block), :] = value.astype(jnp.bfloat16)
        kv_ref[1] = jnp.where(valid, value, 0.0).astype(jnp.bfloat16)
        query = rotated(0).astype(jnp.bfloat16).astype(jnp.float32) * HEAD_DIM ** (-0.5)

        for here in range(steps):

            @pl.when(step == here)
            def _():
                lo = here * block
                causal = lax.broadcasted_iota(
                    jnp.int32, (block, block), 0
                ) >= lax.broadcasted_iota(jnp.int32, (block, block), 1)
                out = jnp.zeros((block, width), jnp.float32)
                for h in range(heads):
                    q = jnp.where(head_of == h, query, 0.0).astype(jnp.bfloat16)
                    diag = jnp.where(causal, dot_nt(q, k_all[lo : lo + block, :]), -1e30)
                    top = jnp.max(diag, axis=-1, keepdims=True)
                    if lo:
                        past = dot_nt(q, k_all[:lo, :])
                        top = jnp.maximum(top, jnp.max(past, axis=-1, keepdims=True))
                        past = jnp.exp(past - top)
                    diag = jnp.exp(diag - top)
                    total = jnp.sum(diag, axis=-1, keepdims=True)
                    if lo:
                        total = total + jnp.sum(past, axis=-1, keepdims=True)
                    inv = 1.0 / total
                    res = jnp.dot(
                        (diag * inv).astype(jnp.bfloat16),
                        v_all[lo : lo + block, :],
                        preferred_element_type=jnp.float32,
                    )
                    if lo:
                        res = res + jnp.dot(
                            (past * inv).astype(jnp.bfloat16),
                            v_all[:lo, :],
                            preferred_element_type=jnp.float32,
                        )
                    out = jnp.where(head_of == h, res, out)
                out = out.astype(jnp.bfloat16)
                for piece in range(block // rows_dev):
                    dev = here * (block // rows_dev) + piece
                    slot = jnp.where(s_ref[1] == dev % 2, 0, 1)
                    att_ref[slot, (dev // 2) * rows_dev : (dev // 2 + 1) * rows_dev, :] = out[
                        piece * rows_dev : (piece + 1) * rows_dev
                    ]

    return pl.pallas_call(
        kernel,
        out_shape=(
            jax.ShapeDtypeStruct((2, seq, width), jnp.bfloat16),
            jax.ShapeDtypeStruct((2, seq // 2, width), jnp.bfloat16),
        ),
        grid_spec=pltpu.PrefetchScalarGridSpec(
            num_scalar_prefetch=1,
            grid=(steps,),
            in_specs=[
                pl.BlockSpec((block, model), lambda i, s: (i, 0)),
                pl.BlockSpec((3, model, width), lambda i, s: (0, 0, 0)),
                pl.BlockSpec((block, width), lambda i, s: (i, 0)),
                pl.BlockSpec((block, width), lambda i, s: (i, 0)),
            ],
            out_specs=(
                pl.BlockSpec((2, block, width), lambda i, s: (0, i, 0)),
                pl.BlockSpec((2, seq // 2, width), lambda i, s: (0, 0, 0)),
            ),
            scratch_shapes=[
                pltpu.VMEM((seq, width), jnp.bfloat16),
                pltpu.VMEM((seq, width), jnp.bfloat16),
            ],
        ),
        compiler_params=pltpu.CompilerParams(vmem_limit_bytes=48 * 1024 * 1024),
        cost_estimate=pl.CostEstimate(
            flops=6 * seq * model * width + 4 * seq * seq * width,
            bytes_accessed=2 * (seq * model + 3 * model * width),
            transcendentals=seq * seq * heads,
        ),
        name="attention",
    )(scalars, tokens, weights, cosine, sine)


def rms_scale(values, gain_row):
    mean_sq = jnp.mean(values * values, axis=-1, keepdims=True)
    return values * lax.rsqrt(mean_sq + 1e-05) * gain_row


def shards(
    hidden_in,
    prompt_len,
    start_pos,
    routes,
    trainer_qkv,
    trainer_out,
    trainer_gate,
    trainer_up,
    trainer_down,
    attn_gain,
    moe_gain,
    router,
):
    size = lax.axis_size("tensor")
    replicas = lax.axis_size("dp")
    chips = size // 2
    me = lax.axis_index("tensor").astype(jnp.int32)
    plane = lax.axis_index("dp").astype(jnp.int32)
    chip, core = me // 2, me % 2
    rows_dev, model = hidden_in.shape[1], hidden_in.shape[2]
    seq_len = rows_dev * size
    length = prompt_len[0]
    offset = start_pos[0]
    my_first = me * rows_dev

    mat_rows = trainer_down.shape[0]
    part_rows = mat_rows // (16 * replicas) * 16
    local_width = trainer_qkv.shape[2] // size
    qkv_parts = split_heads(trainer_qkv.transpose(1, 0, 2), size)
    qkv_cols = lax.all_to_all(qkv_parts, "tensor", 0, 0, tiled=True)
    parts = split_columns(
        trainer_gate, trainer_up, trainer_down[part_rows * replicas :], size, me
    )
    tokens = hidden_in[0].astype(jnp.float32)
    normed = rms_scale(tokens, attn_gain).astype(jnp.bfloat16)
    qkv_cols, normed, *parts = lax.optimization_barrier((qkv_cols, normed, *parts))
    qkv_all = lax.all_gather(qkv_cols, "dp", axis=0)
    down_parts = split_rows(trainer_down, size, plane, part_rows)
    down_cols = lax.all_to_all(down_parts, "tensor", 0, 0, tiled=True)
    same_core = [normed] + [send(normed, size, 2 * j) for j in range(1, chips)]
    other_core = send(jnp.stack(same_core), size, 1)
    blocks = []
    for j in range(chips):
        blocks += [same_core[j], other_core[j]]
    piece = join_blocks(blocks, me)

    first = [1, 2, 4][: size.bit_length() - 1]
    rest = [k for k in range(3, size) if k not in first]
    rest = sorted(rest, key=lambda k: k % 2)
    early = [send(parts[k], size, k) for k in first]
    after = list(lax.optimization_barrier((*[parts[k] for k in rest], *early)))
    early = after[len(rest) :] + [send(after[0], size, rest[0])]
    late = list(lax.optimization_barrier((*after[1 : len(rest)], *early)))
    early = late[len(rest) - 1 :]
    late = [send(block, size, k) for block, k in zip(late, rest[1:])]

    half_dim = HEAD_DIM // 2
    inv_freq = jnp.power(
        10000.0, jnp.arange(half_dim, dtype=jnp.float32) * (-2.0 / HEAD_DIM)
    )
    places = offset + jnp.arange(seq_len, dtype=jnp.int32)
    angles = places.astype(jnp.float32)[:, None] * jnp.tile(inv_freq, local_width // half_dim)
    cosine, sine_part = jnp.cos(angles), jnp.sin(angles)
    server_out = lax.all_gather(trainer_out.astype(jnp.bfloat16), "dp", axis=0, tiled=True)
    qkv_all, server_out, down_cols, piece, cosine, sine_part, *early = lax.optimization_barrier(
        (qkv_all, server_out, down_cols, piece, cosine, sine_part, *early)
    )
    down_all = lax.all_gather(down_cols, "dp", axis=0)
    qkv_server = qkv_all.transpose(2, 1, 0, 3, 4).reshape(3, model, local_width)
    server_qkv = qkv_server.transpose(1, 0, 2)
    scalars = jnp.stack([length, core])
    cache_pair, attended = attention(
        piece, qkv_server, cosine, sine_part, scalars, rows_dev
    )
    half = len(late) // 2
    attended, *late[:half] = lax.optimization_barrier((attended, *late[:half]))
    pieces = 2
    rows = rows_dev // pieces
    out_other = send(server_out, size, 1)
    att_other = send(attended[1], size, 1)
    att_other, *late[half:] = lax.optimization_barrier((att_other, *late[half:]))
    own_part, partial, server_out = project(
        attended[0], att_other, server_out, out_other, chip, rows_dev, pieces
    )
    joined = [parts[0]] * size
    for block, k in zip(early + late, first + rest):
        joined[k] = block

    gate, up = join_gate_up(joined, me, mat_rows)
    down = join_down(down_all, joined, me, mat_rows)
    flipped = [gate, up]
    middles, normed_moes, moe_rows = [], [], []
    got = []
    for h in range(pieces):
        sent = partial[h]
        if h:
            sent = list(lax.optimization_barrier((*sent, *got)))[: chips - 1]
        got = [send(block, size, 2 * j + 2) for j, block in enumerate(sent)]
        if h:
            *got, down, normed_moes[0] = lax.optimization_barrier((*got, down, normed_moes[0]))
        attn_sum = add_up(own_part[h], got)
        if h:
            flipped[1], *normed_moes = lax.optimization_barrier((flipped[1], *normed_moes))
            flipped[1] = with_layout_constraint(flipped[1], Layout((1, 0)))
            *moe_rows[0], flipped[1] = lax.optimization_barrier((*moe_rows[0], flipped[1]))
        else:
            attn_sum, gate, up = lax.optimization_barrier((attn_sum, gate, up))
        middles.append((tokens[h * rows : (h + 1) * rows] + attn_sum).astype(jnp.bfloat16))
        normed = rms_scale(middles[h].astype(jnp.float32), moe_gain).astype(jnp.bfloat16)
        normed_moes.append(normed)
        if h:
            normed, *moe_rows[0] = lax.optimization_barrier((normed, *moe_rows[0]))
        moe_rows.append([normed] + [send(normed, size, 2 * j) for j in range(1, chips)])
    *moe_rows[0], gate, up, down = lax.optimization_barrier((*moe_rows[0], gate, up, down))
    middle = jnp.concatenate(middles, axis=0)
    normed_moe = jnp.concatenate(normed_moes, axis=0)

    local_routes = lax.dynamic_slice_in_dim(routes[0], my_first, rows_dev, 0)
    local_valid = my_first + jnp.arange(rows_dev, dtype=jnp.int32) < length
    logits = jnp.dot(normed_moe, router, preferred_element_type=jnp.float32)
    expert_ids = jnp.arange(router.shape[1], dtype=jnp.int32)
    logit_first = jnp.sum(
        jnp.where(local_routes[:, 0:1] == expert_ids[None, :], logits, 0.0), axis=1
    )
    logit_second = jnp.sum(
        jnp.where(local_routes[:, 1:2] == expert_ids[None, :], logits, 0.0), axis=1
    )
    other_logit = jnp.where(local_routes[:, 0] == 0, logit_second, logit_first)
    local_routed = jnp.any(local_routes == 0, axis=1)
    route_w = jnp.where(local_routed, jax.nn.sigmoid(logits[:, 0] - other_logit), 0.0)

    expert_sums, back = [], []
    for h in range(pieces):
        moe_mine = jnp.stack(moe_rows[h])
        moe_other = send(moe_mine, size, 1)
        sums_mine, sums_other = expert(
            moe_mine.reshape(-1, model), moe_other.reshape(-1, model), gate, up, down
        )
        if h:
            sums_other, *back = lax.optimization_barrier((sums_other, *back))
            expert_sums.append(add_up(total, back))
        else:
            sums_other, *moe_rows[1] = lax.optimization_barrier((sums_other, *moe_rows[1]))
        from_other = send(sums_other, size, 1)
        sums = [
            sums_mine[j * rows : (j + 1) * rows].astype(jnp.float32)
            + from_other[j * rows : (j + 1) * rows].astype(jnp.float32)
            for j in range(chips)
        ]
        total = sums[0]
        sent = [block.astype(jnp.bfloat16) for block in sums[1:]]
        back = [send(block, size, 2 * j + 2) for j, block in enumerate(sent)]
    expert_sums.append(add_up(total, back))
    down_late, gate_late, _ = lax.optimization_barrier((down, gate, sent[0]))
    expert_sum = jnp.concatenate(expert_sums, axis=0)
    expert_sum = jnp.where(local_routed[:, None], expert_sum, 0.0)
    result = middle.astype(jnp.float32) + route_w[:, None] * expert_sum
    hidden_out = jnp.where(local_valid[:, None], result, 0.0).astype(jnp.bfloat16)[None]
    return (
        server_qkv,
        server_out,
        gate_late,
        flipped[1],
        down_late,
        hidden_out,
        cache_pair[None],
    )


def solution(mesh):
    placed = (
        P("dp", "tensor", None),
        P("dp"),
        P("dp"),
        P("dp", None, None),
        P(("tensor", "dp"), None, None),
        P(("tensor", "dp"), None),
        P("tensor", None),
        P("tensor", None),
        P("tensor", None),
        P(),
        P(),
        P(),
    )
    return jax.shard_map(
        shards,
        mesh=mesh,
        in_specs=placed,
        out_specs=(
            P(None, None, "tensor"),
            P("tensor", None),
            P(None, "tensor"),
            P(None, "tensor"),
            P(None, "tensor"),
            P("dp", "tensor", None),
            P("dp", None, None, "tensor"),
        ),
        check_vma=False,
    )
```

```python
import jax
import jax.numpy as jnp
from jax import lax
from jax.experimental import pallas as pl
from jax.experimental.layout import Layout, with_layout_constraint
from jax.experimental.pallas import tpu as pltpu
from jax.sharding import PartitionSpec as P

HEAD_DIM = 64


def swap_pairs(size, step):
    return [(i, i ^ step) for i in range(size)]


def send(block, size, step):
    return lax.ppermute(block, "tensor", swap_pairs(size, step))


def add_up(total, blocks):
    for block in blocks:
        total = total + block.astype(jnp.float32)
    return total


def split_heads(qkv, parts):
    _, rows, width = qkv.shape
    part = width // parts

    def kernel(x_ref, o_ref):
        for t in range(parts):
            for j in range(3):
                o_ref[t, j] = x_ref[j, :, t * part : (t + 1) * part].astype(jnp.bfloat16)

    return pl.pallas_call(
        kernel,
        out_shape=jax.ShapeDtypeStruct((parts, 3, rows, part), jnp.bfloat16),
        name="split_heads",
    )(qkv)


def split_rows(matrix, parts, plane, rows):
    width = matrix.shape[1]
    part = width // parts

    def kernel(p_ref, x_ref, o_ref):
        for t in range(parts):
            o_ref[t] = x_ref[:, t * part : (t + 1) * part].astype(jnp.bfloat16)

    return pl.pallas_call(
        kernel,
        out_shape=jax.ShapeDtypeStruct((parts, rows, part), jnp.bfloat16),
        grid_spec=pltpu.PrefetchScalarGridSpec(
            num_scalar_prefetch=1,
            grid=(1,),
            in_specs=[pl.BlockSpec((rows, width), lambda i, p: (p[0], 0))],
            out_specs=pl.BlockSpec((parts, rows, part), lambda i, p: (0, 0, 0)),
        ),
        compiler_params=pltpu.CompilerParams(vmem_limit_bytes=32 * 1024 * 1024),
        name="split_rows",
    )(plane.reshape(1), matrix)


def split_columns(gate, up, down_tail, parts, me):
    rows, width = gate.shape
    tail = down_tail.shape[0]
    part = width // parts
    window = min(width, (part + 127) // 128 * 128 + 128)
    chunk = 48 if rows % 48 == 0 else 16

    def kernel(me_ref, gate_ref, up_ref, tail_ref, *o_refs):
        step = pl.program_id(0)
        groups = chunk // 16

        def columns(x_ref, k):
            left = (me_ref[0] ^ k) * part
            base = jnp.minimum(lax.div(left, 128) * 128, width - window)
            cols = x_ref[:, pl.ds(pl.multiple_of(base, 128), window)]
            cols = pltpu.roll(cols, window - (left - base), 1)[:, :part]
            return cols.astype(jnp.bfloat16).reshape(-1, 16, part)

        for k in range(parts):
            o_refs[k][pl.ds(step * groups, groups)] = columns(gate_ref, k)
            o_refs[k][pl.ds(step * groups + rows // 16, groups)] = columns(up_ref, k)

        @pl.when(step == 0)
        def _():
            for k in range(parts):
                o_refs[k][rows // 8 : (2 * rows + tail) // 16] = columns(tail_ref, k)

    return pl.pallas_call(
        kernel,
        out_shape=[jax.ShapeDtypeStruct(((2 * rows + tail) // 16, 16, part), jnp.bfloat16)]
        * parts,
        grid_spec=pltpu.PrefetchScalarGridSpec(
            num_scalar_prefetch=1,
            grid=(rows // chunk,),
            in_specs=[pl.BlockSpec((chunk, width), lambda i, m: (i, 0))] * 2
            + [pl.BlockSpec((tail, width), lambda i, m: (0, 0))],
            out_specs=[
                pl.BlockSpec(((2 * rows + tail) // 16, 16, part), lambda i, m: (0, 0, 0))
            ]
            * parts,
        ),
        compiler_params=pltpu.CompilerParams(vmem_limit_bytes=40 * 1024 * 1024),
        name="split_columns",
    )(me.reshape(1), gate, up, down_tail)


def copy_rows(moves, outs_shape, sources, me, name):
    count = len(sources)
    outs = len(outs_shape)

    def kernel(me_ref, *refs):
        ins, o_refs, sem = refs[:count], refs[count : count + outs], refs[count + outs]
        copies = [
            pltpu.make_async_copy(source, o_refs[out].at[pl.ds(first, groups)], sem.at[i])
            for i, (source, out, first, groups) in enumerate(moves(me_ref[0], ins))
        ]
        for copy in copies:
            copy.start()
        for copy in copies:
            copy.wait()

    return pl.pallas_call(
        kernel,
        out_shape=[jax.ShapeDtypeStruct(shape, jnp.bfloat16) for shape in outs_shape],
        grid_spec=pltpu.PrefetchScalarGridSpec(
            num_scalar_prefetch=1,
            grid=(1,),
            in_specs=[pl.BlockSpec(memory_space=pl.ANY)] * count,
            out_specs=[pl.BlockSpec(shape, lambda i, m: (0, 0, 0)) for shape in outs_shape],
            scratch_shapes=[pltpu.SemaphoreType.DMA((160,))],
        ),
        compiler_params=pltpu.CompilerParams(vmem_limit_bytes=40 * 1024 * 1024),
        name=name,
    )(me.reshape(1), *sources)


def join_blocks(blocks, me):
    rows, width = blocks[0].shape
    groups = rows // 16

    def moves(index, ins):
        return [(ref, 0, (index ^ k) * groups, groups) for k, ref in enumerate(ins)]

    blocks = [block.reshape(groups, 16, width) for block in blocks]
    shape = (len(blocks) * groups, 16, width)
    return copy_rows(moves, [shape], blocks, me, "join_blocks")[0].reshape(-1, width)


def join_gate_up(blocks, me, rows):
    width = blocks[0].shape[2]
    groups = rows // 16

    def moves(index, ins):
        return [
            (ref.at[pl.ds(i * groups, groups)], i, (index ^ k) * groups, groups)
            for i in range(2)
            for k, ref in enumerate(ins)
        ]

    shape = (len(blocks) * groups, 16, width)
    joined = copy_rows(moves, [shape, shape], blocks, me, "join_gate_up")
    return [matrix.reshape(-1, width) for matrix in joined]


def join_down(gathered, blocks, me, rows):
    planes, count, part_rows, width = gathered.shape
    groups, part_groups = rows // 16, part_rows // 16
    rest = groups - planes * part_groups
    gathered = gathered.reshape(planes, count, part_groups, 16, width)

    def moves(index, ins):
        found = [
            (ins[0].at[p, t], 0, t * groups + p * part_groups, part_groups)
            for p in range(planes)
            for t in range(count)
        ]
        return found + [
            (
                ref.at[pl.ds(2 * groups, rest)],
                0,
                (index ^ k) * groups + planes * part_groups,
                rest,
            )
            for k, ref in enumerate(ins[1:])
        ]

    shape = (count * groups, 16, width)
    return copy_rows(moves, [shape], [gathered, *blocks], me, "join_down")[0].reshape(-1, width)


def project(mine, other, own_w, other_w, chip, rows_dev, pieces):
    total, width = mine.shape
    chips = total // rows_dev
    model = own_w.shape[1]
    rows = rows_dev // pieces

    def kernel(chip_ref, mine_ref, other_ref, own_ref, other_w_ref, *outs):
        def ordered(ref):
            places = [
                pl.multiple_of((chip_ref[0] ^ j) * rows_dev, rows_dev) for j in range(chips)
            ]
            return jnp.concatenate([ref[pl.ds(place, rows_dev), :] for place in places], axis=0)

        res = jnp.dot(ordered(mine_ref), own_ref[...], preferred_element_type=jnp.float32)
        res = res + jnp.dot(
            ordered(other_ref), other_w_ref[...], preferred_element_type=jnp.float32
        )
        for h in range(pieces):
            outs[h][...] = res[h * rows : (h + 1) * rows]
            for j in range(1, chips):
                first = j * rows_dev + h * rows
                outs[pieces + h * (chips - 1) + j - 1][...] = res[first : first + rows].astype(
                    jnp.bfloat16
                )
        outs[-1][...] = own_ref[...]

    whole = [
        pl.BlockSpec(shape, lambda i, c: (0, 0))
        for shape in (mine.shape, other.shape, own_w.shape, other_w.shape)
    ]
    sent = [(rows, model)] * (pieces * (chips - 1))
    res = pl.pallas_call(
        kernel,
        out_shape=[jax.ShapeDtypeStruct((rows, model), jnp.float32)] * pieces
        + [jax.ShapeDtypeStruct(shape, jnp.bfloat16) for shape in sent + [own_w.shape]],
        grid_spec=pltpu.PrefetchScalarGridSpec(
            num_scalar_prefetch=1,
            grid=(1,),
            in_specs=whole,
            out_specs=[
                pl.BlockSpec(shape, lambda i, c: (0, 0))
                for shape in [(rows, model)] * pieces + sent + [own_w.shape]
            ],
        ),
        compiler_params=pltpu.CompilerParams(vmem_limit_bytes=56 * 1024 * 1024),
        name="project",
    )(chip.reshape(1), mine, other, own_w, other_w)
    sent = [res[pieces + h * (chips - 1) :][: chips - 1] for h in range(pieces)]
    return res[:pieces], sent, res[-1]


def expert(mine, other, gate_w, up_w, down_w):
    rows, model = mine.shape
    units = gate_w.shape[1]
    block = min(512, 2 * rows)

    def kernel(mine_in, other_in, gate_in, up_in, down_in, mine_out, other_out, x_all, w_all, sem):
        copies = [
            pltpu.make_async_copy(source, place, sem.at[i])
            for i, (source, place) in enumerate(
                (
                    (other_in, x_all.at[pl.ds(0, rows), :]),
                    (mine_in, x_all.at[pl.ds(rows, rows), :]),
                    (gate_in, w_all.at[0]),
                    (up_in, w_all.at[1]),
                    (down_in, w_all.at[2]),
                )
            )
        ]
        for copy in copies:
            copy.start()
        copies[0].wait()
        copies[1].wait()
        for place in range(0, 2 * rows, block):
            x = x_all[place : place + block]
            if place == 0:
                copies[2].wait()
            gate = jnp.dot(x, w_all[0], preferred_element_type=jnp.float32)
            if place == 0:
                copies[3].wait()
            up = jnp.dot(x, w_all[1], preferred_element_type=jnp.float32)
            act = (gate / (1.0 + jnp.exp(-gate)) * up).astype(jnp.bfloat16)
            if place == 0:
                copies[4].wait()
            res = dot_nt(act, w_all[2]).astype(jnp.bfloat16)
            if block == 2 * rows:
                other_out[...] = res[:rows]
                mine_out[...] = res[rows:]
            elif place < rows:
                other_out[place : place + block] = res
            else:
                mine_out[place - rows : place - rows + block] = res

    return pl.pallas_call(
        kernel,
        out_shape=[jax.ShapeDtypeStruct((rows, model), jnp.bfloat16)] * 2,
        in_specs=[pl.BlockSpec(memory_space=pl.ANY)] * 5,
        out_specs=[pl.BlockSpec(memory_space=pltpu.VMEM)] * 2,
        scratch_shapes=[
            pltpu.VMEM((2 * rows, model), jnp.bfloat16),
            pltpu.VMEM((3, model, units), jnp.bfloat16),
            pltpu.SemaphoreType.DMA((5,)),
        ],
        compiler_params=pltpu.CompilerParams(vmem_limit_bytes=56 * 1024 * 1024),
        cost_estimate=pl.CostEstimate(
            flops=12 * rows * model * units,
            bytes_accessed=6 * model * units,
            transcendentals=2 * rows * units,
        ),
        name="expert",
    )(mine, other, gate_w, up_w, down_w)


def dot_nt(a, b):
    return lax.dot_general(a, b, (((1,), (1,)), ((), ())), preferred_element_type=jnp.float32)


def attention(tokens, weights, cosine, sine, scalars, rows_dev):
    seq, model = tokens.shape
    width = weights.shape[2]
    heads = width // HEAD_DIM
    block = min(256, seq)
    steps = seq // block
    half = HEAD_DIM // 2

    def kernel(s_ref, x_ref, w_ref, cos_ref, sin_ref, kv_ref, att_ref, k_all, v_all):
        step = pl.program_id(0)
        lane = lax.broadcasted_iota(jnp.int32, (block, width), 1)
        low = lax.rem(lane, HEAD_DIM) < half
        head_of = lax.div(lane, HEAD_DIM)
        x = x_ref[...]

        def rotated(j):
            m = jnp.dot(x, w_ref[j], preferred_element_type=jnp.float32)
            turned = jnp.where(
                low, -pltpu.roll(m, width - half, 1), pltpu.roll(m, half, 1)
            )
            return m * cos_ref[...] + turned * sin_ref[...]

        row = step * block + lax.broadcasted_iota(jnp.int32, (block, width), 0)
        valid = row < s_ref[0]
        start = pl.multiple_of(step * block, block)
        key = rotated(1)
        k_all[pl.ds(start, block), :] = key.astype(jnp.bfloat16)
        kv_ref[0] = jnp.where(valid, key, 0.0).astype(jnp.bfloat16)
        value = jnp.dot(x, w_ref[2], preferred_element_type=jnp.float32)
        v_all[pl.ds(start, block), :] = value.astype(jnp.bfloat16)
        kv_ref[1] = jnp.where(valid, value, 0.0).astype(jnp.bfloat16)
        query = rotated(0).astype(jnp.bfloat16).astype(jnp.float32) * HEAD_DIM ** (-0.5)

        for here in range(steps):

            @pl.when(step == here)
            def _():
                lo = here * block
                causal = lax.broadcasted_iota(
                    jnp.int32, (block, block), 0
                ) >= lax.broadcasted_iota(jnp.int32, (block, block), 1)
                out = jnp.zeros((block, width), jnp.float32)
                for h in range(heads):
                    q = jnp.where(head_of == h, query, 0.0).astype(jnp.bfloat16)
                    diag = jnp.where(causal, dot_nt(q, k_all[lo : lo + block, :]), -1e30)
                    top = jnp.max(diag, axis=-1, keepdims=True)
                    if lo:
                        past = dot_nt(q, k_all[:lo, :])
                        top = jnp.maximum(top, jnp.max(past, axis=-1, keepdims=True))
                        past = jnp.exp(past - top)
                    diag = jnp.exp(diag - top)
                    total = jnp.sum(diag, axis=-1, keepdims=True)
                    if lo:
                        total = total + jnp.sum(past, axis=-1, keepdims=True)
                    inv = 1.0 / total
                    res = jnp.dot(
                        (diag * inv).astype(jnp.bfloat16),
                        v_all[lo : lo + block, :],
                        preferred_element_type=jnp.float32,
                    )
                    if lo:
                        res = res + jnp.dot(
                            (past * inv).astype(jnp.bfloat16),
                            v_all[:lo, :],
                            preferred_element_type=jnp.float32,
                        )
                    out = jnp.where(head_of == h, res, out)
                out = out.astype(jnp.bfloat16)
                for piece in range(block // rows_dev):
                    dev = here * (block // rows_dev) + piece
                    slot = jnp.where(s_ref[1] == dev % 2, 0, 1)
                    att_ref[slot, (dev // 2) * rows_dev : (dev // 2 + 1) * rows_dev, :] = out[
                        piece * rows_dev : (piece + 1) * rows_dev
                    ]

    return pl.pallas_call(
        kernel,
        out_shape=(
            jax.ShapeDtypeStruct((2, seq, width), jnp.bfloat16),
            jax.ShapeDtypeStruct((2, seq // 2, width), jnp.bfloat16),
        ),
        grid_spec=pltpu.PrefetchScalarGridSpec(
            num_scalar_prefetch=1,
            grid=(steps,),
            in_specs=[
                pl.BlockSpec((block, model), lambda i, s: (i, 0)),
                pl.BlockSpec((3, model, width), lambda i, s: (0, 0, 0)),
                pl.BlockSpec((block, width), lambda i, s: (i, 0)),
                pl.BlockSpec((block, width), lambda i, s: (i, 0)),
            ],
            out_specs=(
                pl.BlockSpec((2, block, width), lambda i, s: (0, i, 0)),
                pl.BlockSpec((2, seq // 2, width), lambda i, s: (0, 0, 0)),
            ),
            scratch_shapes=[
                pltpu.VMEM((seq, width), jnp.bfloat16),
                pltpu.VMEM((seq, width), jnp.bfloat16),
            ],
        ),
        compiler_params=pltpu.CompilerParams(vmem_limit_bytes=48 * 1024 * 1024),
        cost_estimate=pl.CostEstimate(
            flops=6 * seq * model * width + 4 * seq * seq * width,
            bytes_accessed=2 * (seq * model + 3 * model * width),
            transcendentals=seq * seq * heads,
        ),
        name="attention",
    )(scalars, tokens, weights, cosine, sine)


def rms_scale(values, gain_row):
    mean_sq = jnp.mean(values * values, axis=-1, keepdims=True)
    return values * lax.rsqrt(mean_sq + 1e-05) * gain_row


def shards(
    hidden_in,
    prompt_len,
    start_pos,
    routes,
    trainer_qkv,
    trainer_out,
    trainer_gate,
    trainer_up,
    trainer_down,
    attn_gain,
    moe_gain,
    router,
):
    size = lax.axis_size("tensor")
    replicas = lax.axis_size("dp")
    chips = size // 2
    me = lax.axis_index("tensor").astype(jnp.int32)
    plane = lax.axis_index("dp").astype(jnp.int32)
    chip, core = me // 2, me % 2
    rows_dev, model = hidden_in.shape[1], hidden_in.shape[2]
    seq_len = rows_dev * size
    length = prompt_len[0]
    offset = start_pos[0]
    my_first = me * rows_dev

    mat_rows = trainer_down.shape[0]
    part_rows = mat_rows // (16 * replicas) * 16
    local_width = trainer_qkv.shape[2] // size
    qkv_parts = split_heads(trainer_qkv.transpose(1, 0, 2), size)
    qkv_cols = lax.all_to_all(qkv_parts, "tensor", 0, 0, tiled=True)
    parts = split_columns(
        trainer_gate, trainer_up, trainer_down[part_rows * replicas :], size, me
    )
    tokens = hidden_in[0].astype(jnp.float32)
    normed = rms_scale(tokens, attn_gain).astype(jnp.bfloat16)
    qkv_cols, normed, *parts = lax.optimization_barrier((qkv_cols, normed, *parts))
    qkv_all = lax.all_gather(qkv_cols, "dp", axis=0)
    same_core = [normed] + [send(normed, size, 2 * j) for j in range(1, chips)]
    other_core = send(jnp.stack(same_core), size, 1)
    blocks = []
    for j in range(chips):
        blocks += [same_core[j], other_core[j]]
    piece = join_blocks(blocks, me)
    plane, piece = lax.optimization_barrier((plane, piece))
    down_parts = split_rows(trainer_down, size, plane, part_rows)
    down_cols = lax.all_to_all(down_parts, "tensor", 0, 0, tiled=True)

    first = [1, 2, 4][: size.bit_length() - 1]
    rest = [k for k in range(3, size) if k not in first]
    rest = sorted(rest, key=lambda k: k % 2)
    early = [send(parts[k], size, k) for k in first]
    after = list(lax.optimization_barrier((*[parts[k] for k in rest], *early)))
    early = after[len(rest) :] + [send(after[0], size, rest[0])]
    late = list(lax.optimization_barrier((*after[1 : len(rest)], *early)))
    early = late[len(rest) - 1 :]
    late = [send(block, size, k) for block, k in zip(late, rest[1:])]

    half_dim = HEAD_DIM // 2
    inv_freq = jnp.power(
        10000.0, jnp.arange(half_dim, dtype=jnp.float32) * (-2.0 / HEAD_DIM)
    )
    places = offset + jnp.arange(seq_len, dtype=jnp.int32)
    angles = places.astype(jnp.float32)[:, None] * jnp.tile(inv_freq, local_width // half_dim)
    cosine, sine_part = jnp.cos(angles), jnp.sin(angles)
    server_out = lax.all_gather(trainer_out.astype(jnp.bfloat16), "dp", axis=0, tiled=True)
    qkv_all, server_out, down_cols, piece, cosine, sine_part, *early = lax.optimization_barrier(
        (qkv_all, server_out, down_cols, piece, cosine, sine_part, *early)
    )
    down_all = lax.all_gather(down_cols, "dp", axis=0)
    qkv_server = qkv_all.transpose(2, 1, 0, 3, 4).reshape(3, model, local_width)
    server_qkv = qkv_server.transpose(1, 0, 2)
    scalars = jnp.stack([length, core])
    cache_pair, attended = attention(
        piece, qkv_server, cosine, sine_part, scalars, rows_dev
    )
    half = len(late) // 2
    attended, *late[:half] = lax.optimization_barrier((attended, *late[:half]))
    pieces = 2
    rows = rows_dev // pieces
    out_other = send(server_out, size, 1)
    att_other = send(attended[1], size, 1)
    att_other, *late[half:] = lax.optimization_barrier((att_other, *late[half:]))
    own_part, partial, server_out = project(
        attended[0], att_other, server_out, out_other, chip, rows_dev, pieces
    )
    joined = [parts[0]] * size
    for block, k in zip(early + late, first + rest):
        joined[k] = block

    gate, up = join_gate_up(joined, me, mat_rows)
    down = join_down(down_all, joined, me, mat_rows)
    flipped = [gate, up]
    middles, normed_moes, moe_rows = [], [], []
    got = []
    for h in range(pieces):
        sent = partial[h]
        if h:
            sent = list(lax.optimization_barrier((*sent, *got)))[: chips - 1]
        got = [send(block, size, 2 * j + 2) for j, block in enumerate(sent)]
        if h:
            *got, down, normed_moes[0] = lax.optimization_barrier((*got, down, normed_moes[0]))
        attn_sum = add_up(own_part[h], got)
        if h:
            flipped[1], *normed_moes = lax.optimization_barrier((flipped[1], *normed_moes))
            flipped[1] = with_layout_constraint(flipped[1], Layout((1, 0)))
            *moe_rows[0], flipped[1] = lax.optimization_barrier((*moe_rows[0], flipped[1]))
        else:
            attn_sum, gate, up = lax.optimization_barrier((attn_sum, gate, up))
        middles.append((tokens[h * rows : (h + 1) * rows] + attn_sum).astype(jnp.bfloat16))
        normed = rms_scale(middles[h].astype(jnp.float32), moe_gain).astype(jnp.bfloat16)
        normed_moes.append(normed)
        if h:
            normed, *moe_rows[0] = lax.optimization_barrier((normed, *moe_rows[0]))
        moe_rows.append([normed] + [send(normed, size, 2 * j) for j in range(1, chips)])
    *moe_rows[0], gate, up, down = lax.optimization_barrier((*moe_rows[0], gate, up, down))
    middle = jnp.concatenate(middles, axis=0)
    normed_moe = jnp.concatenate(normed_moes, axis=0)

    local_routes = lax.dynamic_slice_in_dim(routes[0], my_first, rows_dev, 0)
    local_valid = my_first + jnp.arange(rows_dev, dtype=jnp.int32) < length
    logits = jnp.dot(normed_moe, router, preferred_element_type=jnp.float32)
    expert_ids = jnp.arange(router.shape[1], dtype=jnp.int32)
    logit_first = jnp.sum(
        jnp.where(local_routes[:, 0:1] == expert_ids[None, :], logits, 0.0), axis=1
    )
    logit_second = jnp.sum(
        jnp.where(local_routes[:, 1:2] == expert_ids[None, :], logits, 0.0), axis=1
    )
    other_logit = jnp.where(local_routes[:, 0] == 0, logit_second, logit_first)
    local_routed = jnp.any(local_routes == 0, axis=1)
    route_w = jnp.where(local_routed, jax.nn.sigmoid(logits[:, 0] - other_logit), 0.0)

    expert_sums, back = [], []
    for h in range(pieces):
        moe_mine = jnp.stack(moe_rows[h])
        moe_other = send(moe_mine, size, 1)
        sums_mine, sums_other = expert(
            moe_mine.reshape(-1, model), moe_other.reshape(-1, model), gate, up, down
        )
        if h:
            sums_other, *back = lax.optimization_barrier((sums_other, *back))
            expert_sums.append(add_up(total, back))
        else:
            sums_other, *moe_rows[1] = lax.optimization_barrier((sums_other, *moe_rows[1]))
        from_other = send(sums_other, size, 1)
        sums = [
            sums_mine[j * rows : (j + 1) * rows].astype(jnp.float32)
            + from_other[j * rows : (j + 1) * rows].astype(jnp.float32)
            for j in range(chips)
        ]
        total = sums[0]
        sent = [block.astype(jnp.bfloat16) for block in sums[1:]]
        back = [send(block, size, 2 * j + 2) for j, block in enumerate(sent)]
    expert_sums.append(add_up(total, back))
    down_late, gate_late, _ = lax.optimization_barrier((down, gate, sent[0]))
    expert_sum = jnp.concatenate(expert_sums, axis=0)
    expert_sum = jnp.where(local_routed[:, None], expert_sum, 0.0)
    result = middle.astype(jnp.float32) + route_w[:, None] * expert_sum
    hidden_out = jnp.where(local_valid[:, None], result, 0.0).astype(jnp.bfloat16)[None]
    return (
        server_qkv,
        server_out,
        gate_late,
        flipped[1],
        down_late,
        hidden_out,
        cache_pair[None],
    )


def solution(mesh):
    placed = (
        P("dp", "tensor", None),
        P("dp"),
        P("dp"),
        P("dp", None, None),
        P(("tensor", "dp"), None, None),
        P(("tensor", "dp"), None),
        P("tensor", None),
        P("tensor", None),
        P("tensor", None),
        P(),
        P(),
        P(),
    )
    return jax.shard_map(
        shards,
        mesh=mesh,
        in_specs=placed,
        out_specs=(
            P(None, None, "tensor"),
            P("tensor", None),
            P(None, "tensor"),
            P(None, "tensor"),
            P(None, "tensor"),
            P("dp", "tensor", None),
            P("dp", None, None, "tensor"),
        ),
        check_vma=False,
    )
```
